32 devices in a mesh: tm: 8 (over z, x), rows: 4 (over y, core).
Axes of the slice: x: 2, y: 2, z: 4, core: 2. Of those that a mesh axis runs over, the one named last changes fastest.
Arguments:
- observations: float32 [8, 2048], P('tm'), may hold values from -48 to 48
- site_ids: int32 [8, 2048], P('tm'), may hold values from 0 to 4095
- counts: int32 [8], P('tm'), may hold values from 1 to 2048, 12288 in all
- frequencies: float32 [128], replicated, may hold values from -3.140625 to 3.140625
- decay: float32 [128], replicated, may hold values from 0.02 to 0.2
- proc_var: float32 [128], replicated, may hold values from 0.05 to 0.2
Outputs:
- smooth_mean: float32 [8, 256], P('tm', 'rows')
- smooth_cov: float32 [8, 256, 256], P('tm', 'rows')
The draws below stay inside these ranges and needn't reach their ends.
Inputs may be any that keep to these rules, and one draw needn't show every extreme that they name: Step t observes the sites in its first counts[t] slots; the other slots are ignored.
All inputs are finite; a program needn't handle non-finite values. No bound on the sum of `counts` on one device may be relied on, other than what follows from the above.
Results may differ from the reference program's by a relative error of at most 0.0003.
Values sent between devices are 32-bit elements; how exact they have to be, the bound alone decides.
A program may use at most 128 MiB of HBM per device.

```python
import math
import jax
import jax.numpy as jnp
import numpy as np
from jax import lax

MODES = 128
SITES = 2048
GRID = 4096
OBS_VAR = 64
STEPS = 8


def with_ends(result, stream_key, low, top_value):
    longest = result.shape.index(max(result.shape))
    spots = []
    for shift in (0, 1):
        where = [jax.random.randint(jax.random.fold_in(stream_key, axis), (), 0, length) for axis, length in enumerate(result.shape)]
        where[longest] = (where[longest] + shift) % result.shape[longest]
        spots.append(tuple(where))
    return result.at[spots[0]].set(low).at[spots[1]].set(top_value)


def steps_of(rng, dims, shards, smallest, high):
    def one(axis_at, blocks):
        heights = jax.random.uniform(jax.random.fold_in(jax.random.fold_in(rng, 6), axis_at), (blocks,), jnp.float32, smallest / len(shards), high / len(shards))
        return jnp.repeat(jnp.exp(heights), dims[axis_at] // blocks).reshape((-1,) + (1,) * (len(dims) - axis_at - 1))

    loudness = one(*shards[0])
    for cut in shards[1:]:
        loudness = loudness * one(*cut)
    return loudness


def profile(amount, total, bound, lean):
    loads = [(1 << 20) // math.isqrt(rank ** lean) + 1 for rank in range(2, amount + 1)]
    rest, given = total - bound - (amount - 1), [1] * (amount - 1)
    while rest > 0:
        candidates = [i for i in range(amount - 1) if given[i] < bound]
        pool, remaining = sum([loads[i] for i in candidates]), rest
        for i in candidates:
            addition = min(bound - given[i], max(1, remaining * loads[i] // pool), rest)
            given[i] = given[i] + addition
            rest = rest - addition
    return np.array([bound] + given)


def ragged_sizes(key, amount, total, most, lean):
    if amount == 2:
        one = jax.random.randint(key, (), max(1, total - most), min(most, total - 1) + 1)
        return jnp.stack([one, total - one])
    sizes = jnp.asarray(profile(amount, total, most, lean), jnp.int32)
    twos = (amount - 1) // 2
    donor, sink = sizes[1:1 + 2 * twos:2], sizes[2:2 + 2 * twos:2]
    room = jnp.minimum(donor - 1, most - sink)
    passed = jax.random.randint(jax.random.fold_in(key, 1), (twos,), 0, 1 << 20) % (room + 1)
    sizes = sizes.at[1:1 + 2 * twos:2].set(donor - passed).at[2:2 + 2 * twos:2].set(sink + passed)
    return sizes[jax.random.permutation(jax.random.fold_in(key, 2), amount)]


def gaussian(stream_key, shape, deviation, bound, split=(), held_as=jnp.bfloat16):
    values = deviation * jax.random.normal(stream_key, shape, jnp.float32)
    if split:
        values = values * steps_of(stream_key, shape, split, -0.22, 0.18)
    return jnp.clip(values, -bound, bound).astype(held_as)


def setup_inputs(seed: int = 0) -> dict:
    key_of = jax.random.split(jax.random.key(seed), 7)
    return {
        "observations": gaussian(key_of[0], (STEPS, SITES), 8.0, 48.0, ((0, 8),), jnp.float32),
        "site_ids": with_ends(jax.random.randint(key_of[1], (STEPS, SITES), 0, GRID), jax.random.fold_in(key_of[1], 1), 0, GRID - 1).astype(jnp.int32),
        "counts": ragged_sizes(key_of[2], STEPS, STEPS * SITES * 3 // 4, SITES, 0).astype(jnp.int32),
        "frequencies": jnp.clip(jax.random.uniform(key_of[3], (MODES,), jnp.float32, -3.140625, 3.140625), -3.140625, 3.140625),
        "decay": jnp.clip(jnp.exp(jax.random.uniform(key_of[4], (MODES,), jnp.float32, math.log(0.02), math.log(0.2))), 0.02, 0.2),
        "proc_var": jnp.clip(jnp.exp(jax.random.uniform(key_of[5], (MODES,), jnp.float32, math.log(0.05), math.log(0.2))), 0.05, 0.2),
    }


exact_mode = lax.Precision.HIGHEST

def product(left, right):
    return jnp.dot(left.astype(jnp.float32), right.astype(jnp.float32), precision=exact_mode, preferred_element_type=jnp.float32)

def rotate_rows(matrix, damping, cosines, sines, backward):
    width = matrix.shape[0]
    pairs = matrix.reshape((width // 2, 2) + matrix.shape[1:])
    expand = (width // 2,) + (1,) * (matrix.ndim - 1)
    damp_part = damping.reshape(expand)
    cos_part = cosines.reshape(expand)
    sin_part = sines.reshape(expand)
    upper = pairs[:, 0]
    lower = pairs[:, 1]
    if backward:
        new_upper = damp_part * (cos_part * upper + sin_part * lower)
        new_lower = damp_part * (cos_part * lower - sin_part * upper)
    else:
        new_upper = damp_part * (cos_part * upper - sin_part * lower)
        new_lower = damp_part * (sin_part * upper + cos_part * lower)
    return jnp.stack([new_upper, new_lower], axis=1).reshape(matrix.shape)

def rotate_cols(matrix, damping, cosines, sines, transposed):
    return rotate_rows(matrix.T, damping, cosines, sines, not transposed).T

def site_features(site_row, live, modes):
    slots = jnp.arange(site_row.shape[0], dtype=jnp.int32)
    weights = (slots < live).astype(jnp.float32)
    orders = jnp.arange(1, modes + 1, dtype=jnp.int32)
    phase = site_row[:, None] * orders[None, :] % GRID
    angles = phase.astype(jnp.float32) * (2.0 * math.pi / GRID)
    features = jnp.stack([jnp.cos(angles), jnp.sin(angles)], axis=-1)
    features = features.reshape(site_row.shape[0], 2 * modes) * (1.0 / math.sqrt(modes))
    return (features, weights)

def gram(weighted, features):
    return lax.dot_general(weighted.astype(jnp.float32), features.astype(jnp.float32), (((0,), (0,)), ((), ())), precision=exact_mode, preferred_element_type=jnp.float32)

def build_element(precision_obs, info_obs, first, damping, cosines, sines, proc_var):
    per_mode = jnp.where(first, (1.0 - damping * damping) / proc_var, 1.0 / proc_var)
    diag_prec = jnp.repeat(per_mode, 2)
    keep = jnp.where(first, 0.0, 1.0).astype(jnp.float32)
    width = diag_prec.shape[0]
    factor = jnp.linalg.cholesky(jnp.diag(diag_prec) + precision_obs)
    covariance = jax.scipy.linalg.cho_solve((factor, True), jnp.eye(width, dtype=jnp.float32))
    shift_vec = product(covariance, info_obs)
    trans = rotate_cols(covariance * diag_prec[None, :], damping, cosines, sines, False) * keep
    inner_mat = jnp.diag(diag_prec) - diag_prec[:, None] * covariance * diag_prec[None, :]
    prec_mat = rotate_cols(rotate_rows(inner_mat, damping, cosines, sines, True), damping, cosines, sines, False) * keep
    info_vec = rotate_rows(diag_prec * shift_vec, damping, cosines, sines, True) * keep
    return (trans, shift_vec, covariance, info_vec, prec_mat)

def combine(earlier, later):
    a_trans, a_shift, a_cov, a_info, a_prec = earlier
    b_trans, b_shift, b_cov, b_info, b_prec = later
    width = a_cov.shape[0]
    factor = jnp.linalg.cholesky(a_cov)
    inner_mat = jnp.eye(width, dtype=jnp.float32) + product(product(factor.T, b_prec), factor)
    inner_fac = jnp.linalg.cholesky(inner_mat)
    solved = jax.scipy.linalg.cho_solve((inner_fac, True), product(factor.T, b_trans.T)).T
    gain_cov = product(solved, factor.T)
    gain_dyn = b_trans - product(gain_cov, b_prec)
    new_trans = product(gain_dyn, a_trans)
    new_shift = product(gain_dyn, a_shift) + product(gain_cov, b_info) + b_shift
    new_cov = product(gain_cov, b_trans.T) + b_cov
    back_prec = product(a_trans.T, b_prec)
    weight_solve = jax.scipy.linalg.cho_solve((inner_fac, True), product(factor.T, back_prec.T)).T
    weight_cov = product(weight_solve, factor.T)
    back_map = a_trans.T - weight_cov
    back_full = back_prec - product(weight_cov, b_prec)
    new_info = product(back_map, b_info) - product(back_full, a_shift) + a_info
    new_prec = product(back_full, a_trans) + a_prec
    return (new_trans, new_shift, new_cov, new_info, new_prec)

def smooth_element(mean, covariance, last, damping, cosines, sines, proc_var):
    keep = jnp.where(last, 0.0, 1.0).astype(jnp.float32)
    forward_cov = rotate_rows(covariance, damping, cosines, sines, False)
    predicted = rotate_cols(forward_cov, damping, cosines, sines, True) + jnp.diag(jnp.repeat(proc_var, 2))
    gain = jax.scipy.linalg.cho_solve((jnp.linalg.cholesky(predicted), True), forward_cov).T
    moved_mean = rotate_rows(mean, damping, cosines, sines, False)
    smooth_shift = mean - keep * product(gain, moved_mean)
    smooth_rest = covariance - keep * product(gain, forward_cov)
    return (gain * keep, smooth_shift, smooth_rest)

def smooth_combine(earlier, later):
    a_gain, a_shift, a_rest = earlier
    b_gain, b_shift, b_rest = later
    return (product(a_gain, b_gain), product(a_gain, b_shift) + a_shift, product(product(a_gain, b_rest), a_gain.T) + a_rest)

def reference(observations, site_ids, counts, frequencies, decay, proc_var):
    damping = jnp.exp(-decay)
    cosines = jnp.cos(frequencies)
    sines = jnp.sin(frequencies)
    modes = frequencies.shape[0]
    total = observations.shape[0]
    indices = jnp.arange(total, dtype=jnp.int32)
    noise_scale = 1.0 / OBS_VAR

    def element_at(packed):
        site_row, obs_row, live, index = packed
        features, weights = site_features(site_row, live, modes)
        weighted = features * weights[:, None]
        precision_obs = gram(weighted, features) * noise_scale
        info_obs = jnp.dot((obs_row * weights).astype(jnp.float32), features.astype(jnp.float32), precision=exact_mode, preferred_element_type=jnp.float32) * noise_scale
        return build_element(precision_obs, info_obs, index == 0, damping, cosines, sines, proc_var)
    elements = lax.map(element_at, (site_ids, observations, counts, indices))
    head = jax.tree.map(lambda whole: whole[0], elements)
    others = jax.tree.map(lambda whole: whole[1:], elements)

    def forward(carry, element):
        merged = combine(carry, element)
        return (merged, (merged[1], merged[2]))
    _, (means_rest, covs_rest) = lax.scan(forward, head, others)
    means = jnp.concatenate([head[1][None], means_rest], axis=0)
    covs = jnp.concatenate([head[2][None], covs_rest], axis=0)

    def smooth_at(packed):
        mean, covariance, index = packed
        return smooth_element(mean, covariance, index == total - 1, damping, cosines, sines, proc_var)
    smoothing = lax.map(smooth_at, (means, covs, indices))
    tail = jax.tree.map(lambda whole: whole[-1], smoothing)
    before = jax.tree.map(lambda whole: whole[:-1], smoothing)

    def backward(carry, element):
        merged = smooth_combine(element, carry)
        return (merged, (merged[1], merged[2]))
    _, (shift_rest, rest_rest) = lax.scan(backward, tail, before, reverse=True)
    smooth_mean = jnp.concatenate([shift_rest, tail[1][None]], axis=0)
    smooth_cov = jnp.concatenate([rest_rest, tail[2][None]], axis=0)
    return (smooth_mean, smooth_cov)
```

```python
import functools
import math

import jax
import jax.numpy as jnp
from jax import lax
from jax.experimental import pallas as pl
from jax.experimental.pallas import tpu as pltpu
from jax.sharding import PartitionSpec as P

GRID = 4096
OBS_VAR = 64
FINE = 16
TILE = 8
CHAIN_BOUND = 2.5e-3
LAST_BOUND = 5e-3
TOLERANCE = 1e-6

exact_mode = lax.Precision.HIGHEST


def exact(left, right):
    return jnp.dot(left, right, precision=exact_mode, preferred_element_type=jnp.float32)


dot = functools.partial(jnp.dot, preferred_element_type=jnp.float32)


def halves(value):
    high = value.astype(jnp.bfloat16)
    return high, (value - high.astype(jnp.float32)).astype(jnp.bfloat16)


def spread_by(value, picks):
    high, low = halves(value)
    picks = picks.astype(jnp.bfloat16)
    return dot(high, picks) + dot(low, picks)


def circle(angle):
    square = angle * angle
    cosine = 1.0 / 40320.0 - square * (1.0 / 3628800.0)
    cosine = 1.0 - square * (0.5 - square * (1.0 / 24.0 - square * (1.0 / 720.0 - square * cosine)))
    sine = 1.0 / 5040.0 - square * (1.0 / 362880.0)
    sine = angle * (1.0 - square * (1.0 / 6.0 - square * (1.0 / 120.0 - square * sine)))
    return cosine, sine


def quarter_turn(quadrant, cosine, sine):
    odd = (quadrant & 1) == 1
    new_cosine = jnp.where(odd, sine, cosine)
    new_sine = jnp.where(odd, cosine, sine)
    new_cosine = jnp.where(((quadrant + 1) & 2) == 2, -new_cosine, new_cosine)
    new_sine = jnp.where((quadrant & 2) == 2, -new_sine, new_sine)
    return new_cosine, new_sine


def share_kernel(
    tm_axis, counts_ref, site_ref, obs_ref, freq_ref, decay_ref, var_ref,
    sums_ref, turn_ref, damp_ref, mine, held, send_sem, recv_sem,
):
    count = lax.axis_size(tm_axis)
    own = lax.axis_index(tm_axis)
    sites = site_ref.shape[1]
    modes = freq_ref.shape[1]
    steps = sums_ref.shape[0]
    barrier = pltpu.get_barrier_semaphore()
    for offset in range(1, count):
        pl.semaphore_signal(
            barrier, inc=1, device_id={tm_axis: lax.rem(own + offset, count)},
            device_id_type=pl.DeviceIdType.MESH,
        )

    frequency = freq_ref[...]
    turns = jnp.where(jnp.abs(frequency) > 0.25 * math.pi, 1, 0) + jnp.where(
        jnp.abs(frequency) > 0.75 * math.pi, 1, 0
    )
    turns = jnp.where(frequency < 0.0, -turns, turns)
    share = turns.astype(jnp.float32)
    reduced = (frequency - share * 1.5703125) - share * (0.5 * math.pi - 1.5703125)
    cosine, sine = quarter_turn(turns + 4, *circle(reduced))
    now_cos = jnp.sqrt(var_ref[...])
    now_sin = jnp.zeros_like(now_cos)
    own_cos, own_sin = now_cos, now_sin
    for step in range(steps):
        turn_ref[step, 0:1, :] = now_cos
        turn_ref[step, 1:2, :] = now_sin
        own_cos = jnp.where(own == step, now_cos, own_cos)
        own_sin = jnp.where(own == step, now_sin, own_sin)
        now_cos, now_sin = now_cos * cosine - now_sin * sine, now_cos * sine + now_sin * cosine
    damp_ref[...] = jnp.broadcast_to(jnp.exp(-decay_ref[...]), damp_ref.shape)

    groups = 2 * modes // FINE
    total = 2 * groups + groups // 2 + FINE
    last = total - FINE
    spot = lax.broadcasted_iota(jnp.int32, (total, sites), 0)
    exponent = jnp.where(spot < groups, spot * FINE - modes, (spot - groups) * FINE + 2)
    exponent = jnp.where(spot >= 2 * groups, (spot - 2 * groups) * FINE + 1, exponent)
    exponent = jnp.where(spot >= last, spot - last, exponent)
    phase = (exponent * site_ref[...]) & (GRID - 1)
    quadrant = (phase + GRID // 8) >> int(math.log2(GRID // 4))
    angle = (phase - quadrant * (GRID // 4)).astype(jnp.float32) * (2.0 * math.pi / GRID)
    cosines, sines = quarter_turn(quadrant, *circle(angle))
    slots = lax.broadcasted_iota(jnp.int32, (1, sites), 1)
    weights = jnp.where(slots < counts_ref[0], 1.0, 0.0)
    scale = jnp.where(spot[:last] < 2 * groups, weights, weights * obs_ref[...])
    left = jnp.concatenate([cosines[:last] * scale, sines[:last] * scale], axis=0)
    right = jnp.concatenate([cosines[last:], sines[last:]], axis=0)
    left_high, left_low = halves(left)
    right_high, right_low = halves(right)
    beside = functools.partial(
        lax.dot_general,
        dimension_numbers=(((1,), (1,)), ((), ())),
        preferred_element_type=jnp.float32,
    )
    sums = beside(left_high, right_high) + (beside(left_high, right_low) + beside(left_low, right_high))
    width = 3 * modes
    tall = lax.broadcasted_iota(jnp.int32, (2 * FINE, width), 0)
    wide = lax.broadcasted_iota(jnp.int32, (2 * FINE, width), 1)
    wide = jnp.where(wide < 2 * modes, wide, 2 * (wide - 2 * modes))
    by_cos = spread_by(sums, jnp.where(tall == (wide & (FINE - 1)), 1.0, 0.0))
    by_sin = spread_by(sums, jnp.where(tall - FINE == (wide & (FINE - 1)), 1.0, 0.0))
    one, two = groups, 2 * groups
    real = by_cos[:last] - by_sin[last:]
    imaginary = by_cos[last:] + by_sin[:last]
    lane = lax.broadcasted_iota(jnp.int32, (groups, width), 1)
    lane = jnp.where(lane < 2 * modes, lane, 2 * (lane - 2 * modes))
    keep = jnp.where(lane // FINE == lax.broadcasted_iota(jnp.int32, (groups, width), 0), 1.0, 0.0)

    def flat(value):
        return jnp.sum(value * keep[: value.shape[0]], axis=0, keepdims=True)

    near_cos, near_sin = flat(real[:one])[:, : 2 * modes], flat(imaginary[:one])[:, : 2 * modes]
    far_cos, far_sin = flat(real[one:two]), flat(imaginary[one:two])
    info_cos, info_sin = flat(real[two:])[:, :modes], flat(imaginary[two:])[:, :modes]
    info_scale = 1.0 / (OBS_VAR * math.sqrt(modes))
    turn_cos, turn_sin = own_cos * info_scale, own_sin * info_scale
    info = jnp.concatenate(
        [turn_cos * info_cos + turn_sin * info_sin, turn_cos * info_sin - turn_sin * info_cos], axis=1
    )
    square, cross = own_cos * own_cos, own_sin * own_sin
    level = (square + cross) * near_cos[:, modes : modes + 1]
    swing = (square - cross) * far_cos[:, 2 * modes :] + (2.0 * own_cos * own_sin) * far_sin[:, 2 * modes :]
    weight = jnp.concatenate([level + swing, level - swing], axis=1) * (0.5 / (OBS_VAR * modes))
    empty = jnp.zeros((2, 2 * modes), jnp.float32)
    mine[...] = jnp.concatenate(
        [near_cos, near_sin, far_cos[:, : 2 * modes], far_sin[:, : 2 * modes], info, weight, empty], axis=0
    )

    pl.semaphore_wait(barrier, count - 1)
    copies = []
    for offset in range(1, count):
        copy = pltpu.make_async_remote_copy(
            src_ref=mine,
            dst_ref=held.at[offset],
            send_sem=send_sem.at[offset],
            recv_sem=recv_sem.at[offset],
            device_id={tm_axis: lax.rem(own + offset, count)},
            device_id_type=pl.DeviceIdType.MESH,
        )
        copy.start()
        copies.append(copy)
    sums_ref[own] = mine[...]
    for offset in range(1, count):
        copies[offset - 1].wait()
        sums_ref[lax.rem(own + count - offset, count)] = held[offset]


def solve_kernel(
    tm_axis, rows_axis, sums_ref, turn_ref, damp_ref, mean_ref, cov_ref,
    tab, cols, gain, told, fresh, main, full, kept, narrow, squared, lhs, rhs, answer, spare, result,
):
    steps = sums_ref.shape[0]
    width = sums_ref.shape[2]
    modes = width // 2
    block = cov_ref.shape[1]
    own = lax.axis_index(tm_axis)
    block_row = lax.axis_index(rows_axis)
    links = steps - 1
    sides = (slice(0, modes), slice(modes, width))
    root = math.sqrt(0.5 / (OBS_VAR * modes))
    damp = damp_ref[0:1, :]
    damp_sq = damp * damp
    lane = lax.broadcasted_iota(jnp.int32, (TILE, modes), 1)
    sub = lax.broadcasted_iota(jnp.int32, (TILE, modes), 0)

    def node(i):
        return own if i == links else jnp.where(own > i, i, links - (i - own))

    def inverse_root(value):
        guess = lax.rsqrt(value)
        return guess * (1.5 - 0.5 * value * guess * guess)

    def load(ref, index, row):
        return tuple(ref[index, row : row + 1, side] for side in sides)

    def put(i, scaled, joins):
        cosines, sines = turn_ref[node(i), 0:1, :] * root, turn_ref[node(i), 1:2, :] * root
        rows = (cosines * scaled[0], sines * scaled[0], cosines * scaled[1], sines * scaled[1], *joins)
        for k, row in enumerate(rows):
            tab[TILE * i + k : TILE * i + k + 1, :] = row

    scaled = None
    for i in range(links):
        at = node(i)
        inner = jnp.where(jnp.logical_or(at == 0, at == links), 0.0, 1.0)
        keep = jnp.where(own == i, 0.0, 1.0) if i else 0.0
        level = [1.0 + inner * damp_sq + weight for weight in load(sums_ref, at, 5)]
        if i:
            level = [value - (keep * damp_sq) * (old * old) for value, old in zip(level, scaled)]
        new = [inverse_root(value) for value in level]
        joins = [(keep * damp) * value * old for value, old in zip(new, scaled)] if i else [jnp.zeros_like(damp)] * 2
        put(i, new, joins)
        for side, value, told_info in zip(sides, new, load(sums_ref, at, 4)):
            gain[i, 0:1, side] = value
            told[i, 0:1, side] = value * told_info
        scaled = new
    before = jnp.maximum(own - 1, 0)
    has_left, has_right = jnp.where(own > 0, 1.0, 0.0), jnp.where(own < links, 1.0, 0.0)
    left, right = load(gain, before, 0), scaled
    level = [
        1.0 + (has_left * has_right) * damp_sq + weight
        - (has_left * damp_sq) * (a * a) - (has_right * damp_sq) * (b * b)
        for weight, a, b in zip(load(sums_ref, own, 5), left, right)
    ]
    new = [inverse_root(value) for value in level]
    put(
        links, new,
        [(has_left * damp) * value * old for value, old in zip(new, left)]
        + [(has_right * damp) * value * old for value, old in zip(new, right)],
    )
    for side, value, told_info in zip(sides, new, load(sums_ref, own, 4)):
        gain[links, 0:1, side] = value
        told[links, 0:1, side] = value * told_info
    for chunk in range(tab.shape[0] // modes):
        cols[chunk] = tab[chunk * modes : (chunk + 1) * modes, :].T

    def row_of(i, k):
        return tab[TILE * i + k : TILE * i + k + 1, :]

    def col_of(i, k, rows):
        at = TILE * i + k
        return jnp.broadcast_to(cols[at // modes, rows, at % modes : at % modes + 1], (rows.stop - rows.start, modes))

    def build(i):
        at = node(i)
        bases = []
        for row in range(4):
            base = jnp.broadcast_to(sums_ref[at, row : row + 1, :], (TILE, width))
            if row < 2:
                base = pltpu.roll(base, 0, 1, stride=1, stride_axis=0)
                bases.append((base[:, :modes], base[:, modes:]))
            else:
                base = pltpu.roll(base, width - TILE + 1, 1, stride=1, stride_axis=0)
                bases.append([jnp.take_along_axis(base[:, side], TILE - 1 - sub, axis=0) for side in sides])
        cos_l, sin_l, cos_r, sin_r = [jnp.broadcast_to(row_of(i, k), (TILE, modes)) for k in range(4)]
        for q in range(modes // TILE):
            shift = TILE * q
            rows = slice(shift, shift + TILE)

            def moved(low, high, edge, amount):
                value = jnp.where(lane >= edge, low, high) if edge else low
                return pltpu.roll(value, amount, 1) if amount % modes else value

            near_cos, near_sin = [
                moved(low, high, modes - shift, shift) if shift else high for low, high in bases[:2]
            ]
            far_cos, far_sin = [moved(low, high, shift, modes - shift) for low, high in bases[2:]]
            up_a, up_b = near_cos + far_cos, far_sin + near_sin
            low_a, low_b = far_sin - near_sin, near_cos - far_cos
            up_left, up_right = up_a * cos_l + up_b * sin_l, up_b * cos_r - up_a * sin_r
            low_left, low_right = low_a * cos_l + low_b * sin_l, low_b * cos_r - low_a * sin_r
            cos_t, sin_t, cos_b, sin_b = [col_of(i, k, rows) for k in range(4)]
            off = lane != sub + shift
            under = slice(modes + shift, modes + shift + TILE)
            fresh[i, rows, sides[0]] = jnp.where(off, cos_t * up_left + sin_t * low_left, 0.0)
            fresh[i, rows, sides[1]] = cos_t * up_right + sin_t * low_right
            fresh[i, under, sides[0]] = cos_b * low_left - sin_b * up_left
            fresh[i, under, sides[1]] = jnp.where(off, cos_b * low_right - sin_b * up_right, 0.0)

    pair = 2 * TILE
    strips = [
        (half, slice(start, start + pair), slice(half * modes + start, half * modes + start + pair))
        for half in range(2) for start in range(0, modes, pair)
    ]
    pair_lane = lax.broadcasted_iota(jnp.int32, (pair, modes), 1)
    pair_sub = lax.broadcasted_iota(jnp.int32, (pair, modes), 0)

    def flow(i, state, third):
        sums = [jnp.zeros((pair, modes), jnp.float32) for _ in sides]
        for half, part, rows in strips:
            parts = []
            for k, side in enumerate(sides):
                value = main[i, rows, side] + third[rows, side]
                full[i, rows, side] = value
                parts.append(value * state[k])
            column = jnp.sum(parts[0] + parts[1], axis=1, keepdims=True)
            sums[half] += jnp.where(pair_lane == pair_sub + part.start, column, 0.0)
        moved = [value - jnp.sum(total, axis=0, keepdims=True) for value, total in zip(state, sums)]
        for side, value in zip(sides, moved):
            gain[i, 1:2, side] = value
        return moved

    build(0)
    third, state, most = None, None, jnp.zeros((TILE, width), jnp.float32)
    for i in range(links):
        slot = i % 2
        for half, part, rows in strips:
            join = col_of(i, 4 + half, part) if i else None
            for k, side in enumerate(sides):
                value = fresh[i, rows, side]
                if i:
                    value = value + join * (main[i - 1, rows, side] * row_of(i, 4 + k))
                    kept[slot, rows, side] = value
                narrow[slot, rows, side] = value.astype(jnp.bfloat16)
        square = dot(narrow[slot], narrow[slot])
        build(i + 1)
        if i:
            moved = flow(i - 1, state, third)
        state = [told[i, 0:1, side] + (row_of(i, 4 + k) * moved[k] if i else 0.0) for k, side in enumerate(sides)]
        for half, part, rows in strips:
            join = col_of(i, 4 + half, part) if i else None
            for k, side in enumerate(sides):
                value = square[rows, side]
                squared[slot, rows, side] = value.astype(jnp.bfloat16)
                if i:
                    main[i, rows, side] = (kept[slot, rows, side] - value) + join * (third[rows, side] * row_of(i, 4 + k))
                else:
                    main[i, rows, side] = fresh[i, rows, side] - value
        weight = jnp.abs(square)
        total = weight[:TILE]
        for start in range(TILE, width, TILE):
            total = total + weight[start : start + TILE]
        most = jnp.maximum(most, jnp.broadcast_to(jnp.sum(total, axis=0, keepdims=True), most.shape))
        third = dot(squared[slot], narrow[slot])
    moved = flow(links - 1, state, third)

    odd = lhs.shape[0] - width
    height = block + pair
    tall = lax.broadcasted_iota(jnp.int32, (block, modes), 0)
    wide = lax.broadcasted_iota(jnp.int32, (block, modes), 1)
    hit = wide == (tall + block_row * block) // 2
    even = tall % 2 == 0
    cos_l, sin_l, cos_r, sin_r = [row_of(links, k) * (1.0 / root) for k in range(4)]

    def last_state():
        joins = [row_of(links, k) for k in range(4, 8)]
        return [
            told[links, 0:1, side] + joins[k] * gain[before, 1:2, side] + joins[2 + k] * gain[links - 1, 1:2, side]
            for k, side in enumerate(sides)
        ]

    def pose(state):
        spare[:block, sides[0]] = jnp.where(hit, jnp.where(even, cos_l, sin_l), 0.0)
        spare[:block, sides[1]] = jnp.where(hit, jnp.where(even, -sin_r, cos_r), 0.0)
        for side, value in zip(sides, state):
            spare[block:, side] = jnp.where(pair_sub == 0, value, 0.0)

    def split(value, rows, side):
        high, low = halves(value)
        at, deep = side.start, width
        lhs[rows, at : at + modes] = high
        lhs[rows, deep + at : deep + at + modes] = high
        lhs[rows, 2 * deep + at : 2 * deep + at + modes] = low
        return high, low

    for half, part, rows in strips:
        first, second = col_of(links, 4 + half, part), col_of(links, 6 + half, part)
        for k, side in enumerate(sides):
            value = fresh[links, rows, side] + first * (full[before, rows, side] * row_of(links, 4 + k))
            value = value + second * (full[links - 1, rows, side] * row_of(links, 6 + k))
            high, low = split(value, rows, side)
            for number, piece in enumerate((high, low, high)):
                rhs[0, number * width + rows.start : number * width + rows.stop, side] = piece
    pose(last_state())
    asked = slice(width, width + height)
    for side in sides:
        split(spare[:, side], asked, side)
    both = dot(lhs[...], rhs[0])
    square = both[:width]
    first = spare[...] - both[width:]
    for side in sides:
        split(first[:, side], asked, side)
    for half, part, rows in strips:
        for side in sides:
            high, low = halves(square[rows, side])
            for number, piece in enumerate((high, low, high)):
                rhs[1, number * width + rows.start : number * width + rows.stop, side] = piece
    second = first + dot(lhs[asked, :], rhs[1])
    fourth = dot(rhs[1, :width, :], rhs[1, :width, :])
    weight = jnp.abs(fourth)
    total = weight[:TILE]
    for start in range(TILE, width, TILE):
        total = total + weight[start : start + TILE]
    total = jnp.sum(total, axis=0, keepdims=True)
    answer[...] = second + dot(second.astype(jnp.bfloat16), fourth.astype(jnp.bfloat16))
    good = jnp.logical_and(jnp.max(most) <= CHAIN_BOUND, jnp.max(total) <= LAST_BOUND)

    @pl.when(jnp.logical_not(good))
    def _():
        rows = lax.broadcasted_iota(jnp.int32, (width, width), 0)
        unit = rows == lax.broadcasted_iota(jnp.int32, (width, width), 1)
        source, target = result.at[0], result.at[1]

        def both_ways(value, i, k):
            row = jnp.concatenate([tab[pl.ds(TILE * i + k, 1), :], tab[pl.ds(TILE * i + k + 1, 1), :]], axis=1)
            column = jnp.sum(jnp.where(unit, row, 0.0), axis=1, keepdims=True)
            return column * value * row

        def invert(low):
            high = 1.001 * jnp.max(jnp.sum(jnp.abs(source[...]), axis=0, keepdims=True))
            low = jnp.minimum(low, 0.5 * high)
            center = (high + low) / (high - low)
            slope = 2.0 / (high - low)
            top = 2.0 * center * center - 1.0
            target[...] = jnp.where(unit, 4.0 * center * slope / top, 0.0) - (2.0 * slope * slope / top) * source[...]

            def improve(radius):
                factor = 2.0 / (2.0 - radius * radius)
                residue = jnp.where(unit, 1.0, 0.0) - exact(source[...], target[...])
                target[...] = factor * (target[...] + exact(target[...], residue))
                return radius * radius / (2.0 - radius * radius)

            lax.while_loop(lambda radius: radius > TOLERANCE, improve, 1.0 / top)

        full[0] = jnp.zeros((width, width), jnp.float32)
        gain[0, 1:2, :] = jnp.zeros((1, width), jnp.float32)

        def advance(i, carry):
            old = jnp.maximum(i - 1, 0)
            source[...] = jnp.where(unit, 1.0, 0.0) + fresh[i] + both_ways(full[old], i, 4)
            scaling = gain[i, 0:1, :]
            invert(0.999 * jnp.min(scaling * scaling))
            join = jnp.concatenate([tab[pl.ds(TILE * i + 4, 1), :], tab[pl.ds(TILE * i + 5, 1), :]], axis=1)
            state = told[i, 0:1, :] + join * gain[old, 1:2, :]
            gain[i, 1:2, :] = exact(jnp.broadcast_to(state, (TILE, width)), target[...])[0:1]
            full[i] = jnp.where(unit, 1.0, 0.0) - target[...]
            return carry

        lax.fori_loop(0, links, advance, 0)
        source[...] = (
            jnp.where(unit, 1.0, 0.0) + fresh[links]
            + both_ways(full[before], links, 4) + both_ways(full[links - 1], links, 6)
        )
        scaling = gain[links, 0:1, :]
        invert(0.999 * jnp.min(1.0 - damp_sq) * jnp.min(scaling * scaling))
        pose(last_state())
        answer[...] = exact(spare[...], target[...])

    left, right = answer[:, sides[0]], answer[:, sides[1]]
    left, right = left * cos_l - right * sin_r, left * sin_l + right * cos_r
    wide = lax.broadcasted_iota(jnp.int32, (height, modes), 1)
    out = []
    for number in range(2):
        pick = wide // 2 + number * (modes // 2)
        out.append(
            jnp.where(wide % 2 == 0, jnp.take_along_axis(left, pick, axis=1), jnp.take_along_axis(right, pick, axis=1))
        )
    for side, value in zip(sides, out):
        cov_ref[0, :, side] = value[:block]
    means = jnp.concatenate([value[block : block + TILE] for value in out], axis=1)
    mean_ref[...] = pltpu.roll(means, width - block_row * block, 1)[0:1, :block]


def local(observations, site_ids, counts, frequencies, decay, proc_var):
    modes = frequencies.shape[0]
    width = 2 * modes
    count = lax.axis_size("tm")
    steps = count * observations.shape[0]
    block = width // lax.axis_size("rows")
    height = block + 2 * TILE
    table = -(-TILE * steps // modes) * modes
    vmem = pl.BlockSpec(memory_space=pltpu.VMEM)
    smem = pl.BlockSpec(memory_space=pltpu.SMEM)
    shared = pl.pallas_call(
        functools.partial(share_kernel, "tm"),
        out_shape=(
            jax.ShapeDtypeStruct((steps, 8, width), jnp.float32),
            jax.ShapeDtypeStruct((steps, 8, modes), jnp.float32),
            jax.ShapeDtypeStruct((8, modes), jnp.float32),
        ),
        in_specs=[smem] + [vmem] * 5,
        out_specs=(vmem,) * 3,
        scratch_shapes=[
            pltpu.VMEM((8, width), jnp.float32),
            pltpu.VMEM((count, 8, width), jnp.float32),
            pltpu.SemaphoreType.DMA((count,)),
            pltpu.SemaphoreType.DMA((count,)),
        ],
        compiler_params=pltpu.CompilerParams(collective_id=0, has_side_effects=True, vmem_limit_bytes=16 << 20),
        name="share",
    )(counts, site_ids, observations, frequencies[None], decay[None], proc_var[None])
    return pl.pallas_call(
        functools.partial(solve_kernel, "tm", "rows"),
        out_shape=(
            jax.ShapeDtypeStruct((1, block), jnp.float32),
            jax.ShapeDtypeStruct((1, block, width), jnp.float32),
        ),
        in_specs=[vmem] * 3,
        out_specs=(vmem, vmem),
        scratch_shapes=[
            pltpu.VMEM((table, modes), jnp.float32),
            pltpu.VMEM((table // modes, modes, modes), jnp.float32),
            pltpu.VMEM((steps, 8, width), jnp.float32),
            pltpu.VMEM((steps, 8, width), jnp.float32),
            pltpu.VMEM((steps, width, width), jnp.float32),
            pltpu.VMEM((steps - 1, width, width), jnp.float32),
            pltpu.VMEM((steps - 1, width, width), jnp.float32),
            pltpu.VMEM((2, width, width), jnp.float32),
            pltpu.VMEM((2, width, width), jnp.bfloat16),
            pltpu.VMEM((2, width, width), jnp.bfloat16),
            pltpu.VMEM((width + height, 3 * width), jnp.bfloat16),
            pltpu.VMEM((2, 3 * width, width), jnp.bfloat16),
            pltpu.VMEM((height, width), jnp.float32),
            pltpu.VMEM((height, width), jnp.float32),
            pltpu.VMEM((2, width, width), jnp.float32),
        ],
        compiler_params=pltpu.CompilerParams(vmem_limit_bytes=40 << 20),
        name="solve",
    )(*shared)


def solution(mesh):
    return jax.shard_map(
        local,
        mesh=mesh,
        in_specs=(P("tm", None), P("tm", None), P("tm"), P(), P(), P()),
        out_specs=(P("tm", "rows"), P("tm", "rows", None)),
        check_vma=False,
    )
```

```python
import functools
import math

import jax
import jax.numpy as jnp
from jax import lax
from jax.experimental import pallas as pl
from jax.experimental.pallas import tpu as pltpu
from jax.sharding import PartitionSpec as P

GRID = 4096
OBS_VAR = 64
FINE = 16
TILE = 8
CHAIN_BOUND = 2.5e-3
LAST_BOUND = 5e-3
TOLERANCE = 1e-6

exact_mode = lax.Precision.HIGHEST


def exact(left, right):
    return jnp.dot(left, right, precision=exact_mode, preferred_element_type=jnp.float32)


dot = functools.partial(jnp.dot, preferred_element_type=jnp.float32)


def halves(value):
    high = value.astype(jnp.bfloat16)
    return high, (value - high.astype(jnp.float32)).astype(jnp.bfloat16)


def spread_by(value, picks):
    high, low = halves(value)
    picks = picks.astype(jnp.bfloat16)
    return dot(high, picks) + dot(low, picks)


def circle(angle):
    square = angle * angle
    cosine = 1.0 / 40320.0 - square * (1.0 / 3628800.0)
    cosine = 1.0 - square * (0.5 - square * (1.0 / 24.0 - square * (1.0 / 720.0 - square * cosine)))
    sine = 1.0 / 5040.0 - square * (1.0 / 362880.0)
    sine = angle * (1.0 - square * (1.0 / 6.0 - square * (1.0 / 120.0 - square * sine)))
    return cosine, sine


def quarter_turn(quadrant, cosine, sine):
    odd = (quadrant & 1) == 1
    new_cosine = jnp.where(odd, sine, cosine)
    new_sine = jnp.where(odd, cosine, sine)
    new_cosine = jnp.where(((quadrant + 1) & 2) == 2, -new_cosine, new_cosine)
    new_sine = jnp.where((quadrant & 2) == 2, -new_sine, new_sine)
    return new_cosine, new_sine


def share_kernel(
    tm_axis, counts_ref, site_hbm, obs_hbm, freq_hbm, decay_hbm, var_hbm,
    sums_ref, turn_ref, tile_ref, damp_ref, site_ref, obs_ref, freq_ref, decay_ref, var_ref,
    mine, held, load_sem, send_sem, recv_sem,
):
    count = lax.axis_size(tm_axis)
    own = lax.axis_index(tm_axis)
    sites = site_ref.shape[1]
    modes = freq_ref.shape[1]
    steps = sums_ref.shape[0]
    barrier = pltpu.get_barrier_semaphore()
    for offset in range(1, count):
        pl.semaphore_signal(
            barrier, inc=1, device_id={tm_axis: lax.rem(own + offset, count)},
            device_id_type=pl.DeviceIdType.MESH,
        )
    loads = [
        pltpu.make_async_copy(source, target, load_sem.at[number])
        for number, (source, target) in enumerate((
            (site_hbm, site_ref), (freq_hbm, freq_ref), (obs_hbm, obs_ref),
            (decay_hbm, decay_ref), (var_hbm, var_ref),
        ))
    ]
    for load in loads:
        load.start()
    for load in loads:
        load.wait()

    frequency = freq_ref[...]
    turns = jnp.where(jnp.abs(frequency) > 0.25 * math.pi, 1, 0) + jnp.where(
        jnp.abs(frequency) > 0.75 * math.pi, 1, 0
    )
    turns = jnp.where(frequency < 0.0, -turns, turns)
    share = turns.astype(jnp.float32)
    reduced = (frequency - share * 1.5703125) - share * (0.5 * math.pi - 1.5703125)
    cosine, sine = quarter_turn(turns + 4, *circle(reduced))
    now_cos = jnp.sqrt(var_ref[...])
    now_sin = jnp.zeros_like(now_cos)
    own_cos, own_sin = now_cos, now_sin
    root = math.sqrt(0.5 / (OBS_VAR * modes))
    for step in range(steps):
        for number, value in enumerate((now_cos * root, now_sin * root, now_cos, now_sin)):
            turn_ref[step, number : number + 1, :] = value
        own_cos = jnp.where(own == step, now_cos, own_cos)
        own_sin = jnp.where(own == step, now_sin, own_sin)
        now_cos, now_sin = now_cos * cosine - now_sin * sine, now_cos * sine + now_sin * cosine
    damp_ref[...] = jnp.broadcast_to(jnp.exp(-decay_ref[...]), damp_ref.shape)

    groups = 2 * modes // FINE
    total = 2 * groups + groups // 2 + FINE
    last = total - FINE
    spot = lax.broadcasted_iota(jnp.int32, (total, sites), 0)
    exponent = jnp.where(spot < groups, spot * FINE - modes, (spot - groups) * FINE + 2)
    exponent = jnp.where(spot >= 2 * groups, (spot - 2 * groups) * FINE + 1, exponent)
    exponent = jnp.where(spot >= last, spot - last, exponent)
    phase = (exponent * site_ref[...]) & (GRID - 1)
    quadrant = (phase + GRID // 8) >> int(math.log2(GRID // 4))
    angle = (phase - quadrant * (GRID // 4)).astype(jnp.float32) * (2.0 * math.pi / GRID)
    cosines, sines = quarter_turn(quadrant, *circle(angle))
    slots = lax.broadcasted_iota(jnp.int32, (1, sites), 1)
    weights = jnp.where(slots < counts_ref[0], 1.0, 0.0)
    scale = jnp.where(spot[:last] < 2 * groups, weights, weights * obs_ref[...])
    left = jnp.concatenate([cosines[:last] * scale, sines[:last] * scale], axis=0)
    right = jnp.concatenate([cosines[last:], sines[last:]], axis=0)
    left_high, left_low = halves(left)
    right_high, right_low = halves(right)
    beside = functools.partial(
        lax.dot_general,
        dimension_numbers=(((1,), (1,)), ((), ())),
        preferred_element_type=jnp.float32,
    )
    sums = beside(left_high, right_high) + (beside(left_high, right_low) + beside(left_low, right_high))
    width = 3 * modes
    tall = lax.broadcasted_iota(jnp.int32, (2 * FINE, width), 0)
    wide = lax.broadcasted_iota(jnp.int32, (2 * FINE, width), 1)
    wide = jnp.where(wide < 2 * modes, wide, 2 * (wide - 2 * modes))
    by_cos = spread_by(sums, jnp.where(tall == (wide & (FINE - 1)), 1.0, 0.0))
    by_sin = spread_by(sums, jnp.where(tall - FINE == (wide & (FINE - 1)), 1.0, 0.0))
    one, two = groups, 2 * groups
    real = by_cos[:last] - by_sin[last:]
    imaginary = by_cos[last:] + by_sin[:last]
    lane = lax.broadcasted_iota(jnp.int32, (groups, width), 1)
    lane = jnp.where(lane < 2 * modes, lane, 2 * (lane - 2 * modes))
    keep = jnp.where(lane // FINE == lax.broadcasted_iota(jnp.int32, (groups, width), 0), 1.0, 0.0)

    def flat(value):
        return jnp.sum(value * keep[: value.shape[0]], axis=0, keepdims=True)

    near_cos, near_sin = flat(real[:one])[:, : 2 * modes], flat(imaginary[:one])[:, : 2 * modes]
    far_cos, far_sin = flat(real[one:two]), flat(imaginary[one:two])
    info_cos, info_sin = flat(real[two:])[:, :modes], flat(imaginary[two:])[:, :modes]
    info_scale = 1.0 / (OBS_VAR * math.sqrt(modes))
    turn_cos, turn_sin = own_cos * info_scale, own_sin * info_scale
    info = jnp.concatenate(
        [turn_cos * info_cos + turn_sin * info_sin, turn_cos * info_sin - turn_sin * info_cos], axis=1
    )
    square, cross = own_cos * own_cos, own_sin * own_sin
    level = (square + cross) * near_cos[:, modes : modes + 1]
    swing = (square - cross) * far_cos[:, 2 * modes :] + (2.0 * own_cos * own_sin) * far_sin[:, 2 * modes :]
    weight = jnp.concatenate([level + swing, level - swing], axis=1) * (0.5 / (OBS_VAR * modes))
    empty = jnp.zeros((2, 2 * modes), jnp.float32)
    mine[...] = jnp.concatenate(
        [near_cos, near_sin, far_cos[:, : 2 * modes], far_sin[:, : 2 * modes], info, weight, empty], axis=0
    )

    pl.semaphore_wait(barrier, count - 1)
    copies = []
    for offset in range(1, count):
        copy = pltpu.make_async_remote_copy(
            src_ref=mine,
            dst_ref=held.at[offset],
            send_sem=send_sem.at[offset],
            recv_sem=recv_sem.at[offset],
            device_id={tm_axis: lax.rem(own + offset, count)},
            device_id_type=pl.DeviceIdType.MESH,
        )
        copy.start()
        copies.append(copy)
    sums_ref[own] = mine[...]
    for step in range(steps):
        for number in range(2):
            tile_ref[step, number] = jnp.broadcast_to(turn_ref[step, number : number + 1, :], (modes, modes)).T
    for offset in range(1, count):
        copies[offset - 1].wait()
        sums_ref[lax.rem(own + count - offset, count)] = held[offset]


def solve_kernel(
    tm_axis, rows_axis, sums_ref, turn_ref, tile_ref, damp_ref, mean_ref, cov_ref,
    tab, cols, line, fresh, main, full, answer, spare, result,
):
    steps = sums_ref.shape[0]
    width = sums_ref.shape[2]
    modes = width // 2
    block = cov_ref.shape[1]
    own = lax.axis_index(tm_axis)
    block_row = lax.axis_index(rows_axis)
    links = steps - 1
    sides = (slice(0, modes), slice(modes, width))
    damp = damp_ref[0:1, :]
    damp_sq = damp * damp
    lane = lax.broadcasted_iota(jnp.int32, (TILE, modes), 1)
    sub = lax.broadcasted_iota(jnp.int32, (TILE, modes), 0)
    before = jnp.maximum(own - 1, 0)
    inverse_row, flow_row, right_row, info_row, left_row, other_row = range(6)

    def node(i):
        return own if i == links else jnp.where(own > i, i, links - (i - own))

    def load(ref, index, row):
        return tuple(ref[index, row : row + 1, side] for side in sides)

    def note(i, row, values):
        for side, value in zip(sides, values):
            line[i, row : row + 1, side] = value

    past = None
    for i in range(links):
        at = node(i)
        inner = jnp.where(jnp.logical_or(at == 0, at == links), 0.0, 1.0)
        keep = jnp.where(own == i, 0.0, 1.0) if i else 0.0
        level = [1.0 + inner * damp_sq + weight for weight in load(sums_ref, at, 5)]
        if i:
            level = [value - (keep * damp_sq) * old for value, old in zip(level, past)]
        inverse = [1.0 / value for value in level]
        note(i, inverse_row, inverse)
        note(i, right_row, [(keep * damp) * value for value in inverse])
        note(i, info_row, load(sums_ref, at, 4))
        note(i, other_row, [(keep * damp) * old for old in past] if i else [jnp.zeros_like(damp)] * 2)
        for half, value in enumerate(inverse):
            tab[2 * i + half : 2 * i + half + 1, :] = damp * value
        past = inverse
    has_left, has_right = jnp.where(own > 0, 1.0, 0.0), jnp.where(own < links, 1.0, 0.0)
    left, right = load(line, before, inverse_row), past
    level = [
        1.0 + (has_left * has_right) * damp_sq + weight - (has_left * damp_sq) * a - (has_right * damp_sq) * b
        for weight, a, b in zip(load(sums_ref, own, 5), left, right)
    ]
    inverse = [1.0 / value for value in level]
    note(links, inverse_row, inverse)
    note(links, right_row, [damp * value for value in inverse])
    note(links, info_row, load(sums_ref, own, 4))
    left, right = [(has_left * damp) * value for value in left], [(has_right * damp) * value for value in right]
    note(links, left_row, left)
    note(links, other_row, right)
    for half in range(2):
        tab[2 * links + half : 2 * links + half + 1, :] = left[half]
        tab[2 * steps + half : 2 * steps + half + 1, :] = right[half]
    for chunk in range(tab.shape[0] // modes):
        cols[chunk] = tab[chunk * modes : (chunk + 1) * modes, :].T

    def col_of(at, rows):
        value = cols[at // modes, rows, at % modes : at % modes + 1]
        return jnp.broadcast_to(value, (rows.stop - rows.start, modes))

    def build(i):
        at = node(i)
        bases = []
        for row in range(4):
            base = jnp.broadcast_to(sums_ref[at, row : row + 1, :], (TILE, width))
            if row < 2:
                base = pltpu.roll(base, 0, 1, stride=1, stride_axis=0)
                bases.append((base[:, :modes], base[:, modes:]))
            else:
                base = pltpu.roll(base, width - TILE + 1, 1, stride=1, stride_axis=0)
                bases.append([jnp.take_along_axis(base[:, side], TILE - 1 - sub, axis=0) for side in sides])
        turn = [turn_ref[at, k : k + 1, :] for k in range(2)]
        cos_l, sin_l, cos_r, sin_r = [
            jnp.broadcast_to(value * scale, (TILE, modes)) for scale in load(line, i, inverse_row) for value in turn
        ]
        for q in range(modes // TILE):
            shift = TILE * q
            rows = slice(shift, shift + TILE)

            def moved(low, high, edge, amount):
                value = jnp.where(lane >= edge, low, high) if edge else low
                return pltpu.roll(value, amount, 1) if amount % modes else value

            near_cos, near_sin = [
                moved(low, high, modes - shift, shift) if shift else high for low, high in bases[:2]
            ]
            far_cos, far_sin = [moved(low, high, shift, modes - shift) for low, high in bases[2:]]
            up_a, up_b = near_cos + far_cos, far_sin + near_sin
            low_a, low_b = far_sin - near_sin, near_cos - far_cos
            up_left, up_right = up_a * cos_l + up_b * sin_l, up_b * cos_r - up_a * sin_r
            low_left, low_right = low_a * cos_l + low_b * sin_l, low_b * cos_r - low_a * sin_r
            cos_t, sin_t = tile_ref[at, 0, rows, :], tile_ref[at, 1, rows, :]
            off = lane != sub + shift
            under = slice(modes + shift, modes + shift + TILE)
            fresh[i, rows, sides[0]] = jnp.where(off, cos_t * up_left + sin_t * low_left, 0.0)
            fresh[i, rows, sides[1]] = cos_t * up_right + sin_t * low_right
            fresh[i, under, sides[0]] = cos_t * low_left - sin_t * up_left
            fresh[i, under, sides[1]] = jnp.where(off, cos_t * low_right - sin_t * up_right, 0.0)

    pair = 2 * TILE
    strips = [
        (half, slice(start, start + pair), slice(half * modes + start, half * modes + start + pair))
        for half in range(2) for start in range(0, modes, pair)
    ]
    pair_lane = lax.broadcasted_iota(jnp.int32, (pair, modes), 1)
    pair_sub = lax.broadcasted_iota(jnp.int32, (pair, modes), 0)
    ones = jnp.ones((TILE, width), jnp.bfloat16)

    def flow(i, state, third):
        sums = [jnp.zeros((pair, modes), jnp.float32) for _ in sides]
        for half, part, rows in strips:
            parts = []
            for k, side in enumerate(sides):
                value = main[i, rows, side] + third[rows, side]
                full[i, rows, side] = value
                parts.append(value * state[k])
            column = jnp.sum(parts[0] + parts[1], axis=1, keepdims=True)
            sums[half] += jnp.where(pair_lane == pair_sub + part.start, column, 0.0)
        moved = [value - jnp.sum(total, axis=0, keepdims=True) for value, total in zip(state, sums)]
        note(i, flow_row, moved)
        return moved

    def joined(i, old):
        rights = load(line, i, right_row)
        whole = []
        for half, part, rows in strips:
            values = [fresh[i, rows, side] for side in sides]
            if i:
                down = col_of(2 * (i - 1) + half, part)
                values = [value + down * (old[i - 1, rows, side] * right) for value, side, right in zip(values, sides, rights)]
            whole.append(values)
        return whole

    def packed(whole):
        return jnp.concatenate([jnp.concatenate(values, axis=1) for values in whole], axis=0).astype(jnp.bfloat16)

    build(0)
    third, state, most = None, None, jnp.zeros((TILE, width), jnp.float32)
    for i in range(links):
        narrow = packed(joined(i, main))
        square = dot(narrow, narrow)
        if i:
            moved = flow(i - 1, state, third)
            state = [a + b * c for a, b, c in zip(load(line, i, info_row), load(line, i, other_row), moved)]
        else:
            state = load(line, i, info_row)
        build(i + 1)
        for (half, part, rows), values in zip(strips, joined(i, full)):
            for side, value in zip(sides, values):
                main[i, rows, side] = value - square[rows, side]
        squared = square.astype(jnp.bfloat16)
        third = dot(squared, narrow)
        most = jnp.maximum(most, dot(ones, jnp.abs(squared)))
    flow(links - 1, state, third)

    height = block + pair
    tall = lax.broadcasted_iota(jnp.int32, (block, modes), 0)
    wide = lax.broadcasted_iota(jnp.int32, (block, modes), 1)
    hit = wide == (tall + block_row * block) // 2
    even = tall % 2 == 0
    cosines, sines = turn_ref[own, 2:3, :], turn_ref[own, 3:4, :]

    def pose():
        state = [
            a + b * c + d * e
            for a, b, c, d, e in zip(
                load(line, links, info_row), load(line, links, left_row), load(line, before, flow_row),
                load(line, links, other_row), load(line, links - 1, flow_row),
            )
        ]
        scales = load(line, links, inverse_row)
        spare[:block, sides[0]] = jnp.where(hit, jnp.where(even, cosines, sines) * scales[0], 0.0)
        spare[:block, sides[1]] = jnp.where(hit, jnp.where(even, -sines, cosines) * scales[1], 0.0)
        for side, value, scale in zip(sides, state, scales):
            spare[block:, side] = jnp.where(pair_sub == 0, value * scale, 0.0)

    def product(left, right):
        return dot(left[0], right[0]) + (dot(left[0], right[1]) + dot(left[1], right[0]))

    whole = []
    rights = load(line, links, right_row)
    for half, part, rows in strips:
        first, second = col_of(2 * links + half, part), col_of(2 * steps + half, part)
        whole.append([
            fresh[links, rows, side] + (first * full[before, rows, side] + second * full[links - 1, rows, side]) * right
            for side, right in zip(sides, rights)
        ])
    whole = halves(jnp.concatenate([jnp.concatenate(values, axis=1) for values in whole], axis=0))
    square = halves(product(whole, whole))
    pose()
    asked = spare[...]
    first = asked - product(halves(asked), whole)
    fourth = dot(square[0], square[0]).astype(jnp.bfloat16)
    second = first + product(halves(first), square)
    last = dot(ones, jnp.abs(fourth))
    answer[...] = second + dot(second.astype(jnp.bfloat16), fourth)
    good = jnp.logical_and(jnp.max(most) <= CHAIN_BOUND, jnp.max(last) <= LAST_BOUND)

    @pl.when(jnp.logical_not(good))
    def _():
        rows = lax.broadcasted_iota(jnp.int32, (width, width), 0)
        unit = rows == lax.broadcasted_iota(jnp.int32, (width, width), 1)
        source, target = result.at[0], result.at[1]

        def column(row):
            return jnp.sum(jnp.where(unit, row, 0.0), axis=1, keepdims=True)

        def invert(low):
            high = 1.001 * jnp.max(jnp.sum(jnp.abs(source[...]), axis=0, keepdims=True))
            low = jnp.minimum(low, 0.5 * high)
            center = (high + low) / (high - low)
            slope = 2.0 / (high - low)
            top = 2.0 * center * center - 1.0
            target[...] = jnp.where(unit, 4.0 * center * slope / top, 0.0) - (2.0 * slope * slope / top) * source[...]

            def improve(radius):
                factor = 2.0 / (2.0 - radius * radius)
                residue = jnp.where(unit, 1.0, 0.0) - exact(source[...], target[...])
                target[...] = factor * (target[...] + exact(target[...], residue))
                return radius * radius / (2.0 - radius * radius)

            lax.while_loop(lambda radius: radius > TOLERANCE, improve, 1.0 / top)

        def even_out(i, whole):
            root = jnp.sqrt(line[i, inverse_row : inverse_row + 1, :])
            source[...] = jnp.where(unit, 1.0, 0.0) + column(root) * whole * (1.0 / root)
            return root, column(root)

        full[0] = jnp.zeros((width, width), jnp.float32)
        note(0, flow_row, [jnp.zeros_like(damp)] * 2)

        def advance(i, carry):
            old = jnp.maximum(i - 1, 0)
            down = column(line[old, inverse_row : inverse_row + 1, :] * jnp.concatenate([damp, damp], axis=1))
            root, root_col = even_out(i, fresh[i] + down * full[old] * line[i, right_row : right_row + 1, :])
            invert(0.999 * jnp.min(root * root))
            state = line[i, info_row : info_row + 1, :]
            state = state + line[i, other_row : other_row + 1, :] * line[old, flow_row : flow_row + 1, :]
            scaled = jnp.broadcast_to(state * root, (TILE, width))
            line[i, flow_row : flow_row + 1, :] = exact(scaled, target[...])[0:1] * (1.0 / root)
            full[i] = (1.0 / root_col) * (jnp.where(unit, 1.0, 0.0) - target[...]) * root
            return carry

        lax.fori_loop(0, links, advance, 0)
        root, root_col = even_out(
            links,
            fresh[links] + (
                column(line[links, left_row : left_row + 1, :]) * full[before]
                + column(line[links, other_row : other_row + 1, :]) * full[links - 1]
            ) * line[links, right_row : right_row + 1, :],
        )
        invert(0.999 * jnp.min(1.0 - damp_sq) * jnp.min(root * root))
        pose()
        answer[...] = exact(spare[...] * (1.0 / root), target[...]) * root

    left, right = answer[:, sides[0]], answer[:, sides[1]]
    left, right = left * cosines - right * sines, left * sines + right * cosines
    wide = lax.broadcasted_iota(jnp.int32, (height, modes), 1)
    out = []
    for number in range(2):
        pick = wide // 2 + number * (modes // 2)
        out.append(
            jnp.where(wide % 2 == 0, jnp.take_along_axis(left, pick, axis=1), jnp.take_along_axis(right, pick, axis=1))
        )
    for side, value in zip(sides, out):
        cov_ref[0, :, side] = value[:block]
    means = jnp.concatenate([value[block : block + TILE] for value in out], axis=1)
    mean_ref[...] = pltpu.roll(means, width - block_row * block, 1)[0:1, :block]


def local(observations, site_ids, counts, frequencies, decay, proc_var):
    modes = frequencies.shape[0]
    width = 2 * modes
    count = lax.axis_size("tm")
    steps = count * observations.shape[0]
    block = width // lax.axis_size("rows")
    height = block + 2 * TILE
    table = -(-(2 * steps + 2) // modes) * modes
    vmem = pl.BlockSpec(memory_space=pltpu.VMEM)
    smem = pl.BlockSpec(memory_space=pltpu.SMEM)
    hbm = pl.BlockSpec(memory_space=pltpu.HBM)
    shared = pl.pallas_call(
        functools.partial(share_kernel, "tm"),
        out_shape=(
            jax.ShapeDtypeStruct((steps, 8, width), jnp.float32),
            jax.ShapeDtypeStruct((steps, 8, modes), jnp.float32),
            jax.ShapeDtypeStruct((steps, 2, modes, modes), jnp.float32),
            jax.ShapeDtypeStruct((8, modes), jnp.float32),
        ),
        in_specs=[smem] + [hbm] * 5,
        out_specs=(vmem,) * 4,
        scratch_shapes=[
            pltpu.VMEM(site_ids.shape, jnp.int32),
            pltpu.VMEM(observations.shape, jnp.float32),
            pltpu.VMEM((1, modes), jnp.float32),
            pltpu.VMEM((1, modes), jnp.float32),
            pltpu.VMEM((1, modes), jnp.float32),
            pltpu.VMEM((8, width), jnp.float32),
            pltpu.VMEM((count, 8, width), jnp.float32),
            pltpu.SemaphoreType.DMA((5,)),
            pltpu.SemaphoreType.DMA((count,)),
            pltpu.SemaphoreType.DMA((count,)),
        ],
        compiler_params=pltpu.CompilerParams(collective_id=0, has_side_effects=True, vmem_limit_bytes=16 << 20),
        name="share",
    )(
        counts,
        *(
            pltpu.with_memory_space_constraint(value, pltpu.HBM)
            for value in (site_ids, observations, frequencies[None], decay[None], proc_var[None])
        ),
    )
    return pl.pallas_call(
        functools.partial(solve_kernel, "tm", "rows"),
        out_shape=(
            jax.ShapeDtypeStruct((1, block), jnp.float32),
            jax.ShapeDtypeStruct((1, block, width), jnp.float32),
        ),
        in_specs=[vmem] * 4,
        out_specs=(vmem, vmem),
        scratch_shapes=[
            pltpu.VMEM((table, modes), jnp.float32),
            pltpu.VMEM((table // modes, modes, modes), jnp.float32),
            pltpu.VMEM((steps, 8, width), jnp.float32),
            pltpu.VMEM((steps, width, width), jnp.float32),
            pltpu.VMEM((steps - 1, width, width), jnp.float32),
            pltpu.VMEM((steps - 1, width, width), jnp.float32),
            pltpu.VMEM((height, width), jnp.float32),
            pltpu.VMEM((height, width), jnp.float32),
            pltpu.VMEM((2, width, width), jnp.float32),
        ],
        compiler_params=pltpu.CompilerParams(vmem_limit_bytes=40 << 20),
        name="solve",
    )(*shared)


def solution(mesh):
    return jax.shard_map(
        local,
        mesh=mesh,
        in_specs=(P("tm", None), P("tm", None), P("tm"), P(), P(), P()),
        out_specs=(P("tm", "rows"), P("tm", "rows", None)),
        check_vma=False,
    )
```

```python
import functools
import math

import jax
import jax.numpy as jnp
from jax import lax
from jax.experimental import pallas as pl
from jax.experimental.pallas import tpu as pltpu
from jax.sharding import PartitionSpec as P

GRID = 4096
OBS_VAR = 64
FINE = 16
TILE = 8
CHAIN_BOUND = 2.5e-3
LAST_BOUND = 5e-3
TOLERANCE = 1e-6

exact_mode = lax.Precision.HIGHEST


def exact(left, right):
    return jnp.dot(left, right, precision=exact_mode, preferred_element_type=jnp.float32)


dot = functools.partial(jnp.dot, preferred_element_type=jnp.float32)


def halves(value):
    high = value.astype(jnp.bfloat16)
    return high, (value - high.astype(jnp.float32)).astype(jnp.bfloat16)


def spread_by(value, picks):
    high, low = halves(value)
    picks = picks.astype(jnp.bfloat16)
    return dot(high, picks) + dot(low, picks)


def circle(angle):
    square = angle * angle
    cosine = 1.0 / 40320.0 - square * (1.0 / 3628800.0)
    cosine = 1.0 - square * (0.5 - square * (1.0 / 24.0 - square * (1.0 / 720.0 - square * cosine)))
    sine = 1.0 / 5040.0 - square * (1.0 / 362880.0)
    sine = angle * (1.0 - square * (1.0 / 6.0 - square * (1.0 / 120.0 - square * sine)))
    return cosine, sine


def quarter_turn(quadrant, cosine, sine):
    odd = (quadrant & 1) == 1
    new_cosine = jnp.where(odd, sine, cosine)
    new_sine = jnp.where(odd, cosine, sine)
    new_cosine = jnp.where(((quadrant + 1) & 2) == 2, -new_cosine, new_cosine)
    new_sine = jnp.where((quadrant & 2) == 2, -new_sine, new_sine)
    return new_cosine, new_sine


def share_kernel(
    tm_axis, counts_ref, site_hbm, obs_hbm, freq_hbm, decay_hbm, var_hbm,
    sums_ref, turn_ref, tile_ref, mode_ref, site_ref, obs_ref, freq_ref, decay_ref, var_ref,
    mine, held, load_sem, send_sem, recv_sem,
):
    count = lax.axis_size(tm_axis)
    own = lax.axis_index(tm_axis)
    sites = site_ref.shape[1]
    modes = freq_ref.shape[1]
    steps = sums_ref.shape[0]
    loads = [
        pltpu.make_async_copy(source, target, load_sem.at[number])
        for number, (source, target) in enumerate((
            (site_hbm, site_ref), (obs_hbm, obs_ref), (freq_hbm, freq_ref), (var_hbm, var_ref), (decay_hbm, decay_ref),
        ))
    ]
    for load in loads:
        load.start()
    barrier = pltpu.get_barrier_semaphore()
    for offset in range(1, count):
        pl.semaphore_signal(
            barrier, inc=1, device_id={tm_axis: lax.rem(own + offset, count)},
            device_id_type=pl.DeviceIdType.MESH,
        )
    for load in loads:
        load.wait()

    frequency = freq_ref[...]
    turns = jnp.where(jnp.abs(frequency) > 0.25 * math.pi, 1, 0) + jnp.where(
        jnp.abs(frequency) > 0.75 * math.pi, 1, 0
    )
    turns = jnp.where(frequency < 0.0, -turns, turns)
    share = turns.astype(jnp.float32)
    reduced = (frequency - share * 1.5703125) - share * (0.5 * math.pi - 1.5703125)
    turn_cosine, turn_sine = quarter_turn(turns + 4, *circle(reduced))
    level = 0.5 / (OBS_VAR * modes)
    root = math.sqrt(level)
    variance = var_ref[...]
    mode_ref[0:1, :] = jnp.exp(-decay_ref[...])
    now_cos = jnp.sqrt(variance)
    now_sin = jnp.zeros_like(now_cos)
    own_cos, own_sin = now_cos, now_sin
    for step in range(steps):
        for number, value in enumerate((now_cos * root, now_sin * root, now_cos, now_sin)):
            turn_ref[step, number : number + 1, :] = value
        own_cos = jnp.where(own == step, now_cos, own_cos)
        own_sin = jnp.where(own == step, now_sin, own_sin)
        now_cos, now_sin = (
            now_cos * turn_cosine - now_sin * turn_sine, now_cos * turn_sine + now_sin * turn_cosine
        )

    def wave(stride):
        exponent = lax.broadcasted_iota(jnp.int32, (TILE, sites), 0) * stride
        phase = (exponent * site_ref[...]) & (GRID - 1)
        quadrant = (phase + GRID // 8) >> int(math.log2(GRID // 4))
        angle = (phase - quadrant * (GRID // 4)).astype(jnp.float32) * (2.0 * math.pi / GRID)
        return quarter_turn(quadrant, *circle(angle))

    def turned(wave, by):
        return wave[0] * by[0] - wave[1] * by[1], wave[0] * by[1] + wave[1] * by[0]

    def one(wave, row):
        return wave[0][row : row + 1], wave[1][row : row + 1]

    fine, coarse = wave(1), wave(FINE)
    eight = turned(one(fine, 4), one(fine, 4))
    far = turned(one(coarse, 4), one(coarse, 4))
    far = turned(far, one(fine, 2))
    slots = lax.broadcasted_iota(jnp.int32, (1, sites), 1)
    weights = jnp.where(slots < counts_ref[0], 1.0, 0.0)
    near = coarse[0] * weights, coarse[1] * weights
    seen = turned(near, one(fine, 1))
    tiles = (near, turned(near, one(fine, 2)), turned(near, far), (seen[0] * obs_ref[...], seen[1] * obs_ref[...]))
    left = jnp.concatenate([tile[0] for tile in tiles] + [tile[1] for tile in tiles], axis=0)
    upper = turned(fine, eight)
    right = jnp.concatenate([fine[0], upper[0], fine[1], upper[1]], axis=0)
    left_high, left_low = halves(left)
    right_high, right_low = halves(right)
    beside = functools.partial(
        lax.dot_general,
        dimension_numbers=(((1,), (1,)), ((), ())),
        preferred_element_type=jnp.float32,
    )
    sums = beside(left_high, right_high) + (beside(left_high, right_low) + beside(left_low, right_high))
    tall = lax.broadcasted_iota(jnp.int32, (2 * FINE, 6 * modes), 0)
    wide = lax.broadcasted_iota(jnp.int32, (2 * FINE, 6 * modes), 1)
    picks = jnp.where(wide < 2 * modes, wide, jnp.where(wide < 4 * modes, 2 * wide, 6 * modes - wide)) & (FINE - 1)
    spread = spread_by(sums, jnp.where(tall == picks + (FINE * (wide // modes)) % (2 * FINE), 1.0, 0.0))
    half = left.shape[0] // 2
    pieces = [spread[:, number * modes : (number + 1) * modes] for number in range(6)]
    real, even_real, back_real = [pieces[number][:half] - pieces[number + 1][half:] for number in (0, 2, 4)]
    imaginary, even_imaginary, back_imaginary = [
        pieces[number][half:] + pieces[number + 1][:half] for number in (0, 2, 4)
    ]
    lane = lax.broadcasted_iota(jnp.int32, (TILE, modes), 1)
    group = lax.broadcasted_iota(jnp.int32, (TILE, modes), 0)
    keep = jnp.where(lane // FINE == group, 1.0, 0.0)
    keep_low = jnp.where(2 * lane // FINE == group, 1.0, 0.0)
    keep_back = jnp.where((modes - lane) // FINE == group, 1.0, 0.0)
    keep_high = jnp.where(2 * lane // FINE == group + TILE, 1.0, 0.0)

    def tile(value, number):
        return value[number * TILE : (number + 1) * TILE]

    def flat(value, number, keep=keep):
        return jnp.sum(tile(value, number) * keep, axis=0, keepdims=True)

    def even(value):
        return jnp.sum(tile(value, 1) * keep_low + tile(value, 2) * keep_high, axis=0, keepdims=True)

    info_scale = 1.0 / (OBS_VAR * math.sqrt(modes))
    turn_cos, turn_sin = own_cos * info_scale, own_sin * info_scale
    info_cos, info_sin = flat(real, 3), flat(imaginary, 3)
    near_cos = flat(real, 0)
    mass = (variance * level) * near_cos[:, 0:1]
    swing = (own_cos * own_cos - own_sin * own_sin) * level * even(even_real)
    swing = swing + (own_cos * own_sin) * (2.0 * level) * even(even_imaginary)
    rows = (
        near_cos, flat(imaginary, 0), flat(real, 1), flat(real, 2), flat(imaginary, 1), flat(imaginary, 2),
        turn_cos * info_cos + turn_sin * info_sin, turn_cos * info_sin - turn_sin * info_cos,
        mass + swing, mass - swing, flat(back_real, 0, keep_back), -flat(back_imaginary, 0, keep_back),
        jnp.zeros((4, modes), jnp.float32),
    )
    mine[...] = jnp.concatenate(rows, axis=0)

    pl.semaphore_wait(barrier, count - 1)
    copies = []
    for offset in range(1, count):
        copy = pltpu.make_async_remote_copy(
            src_ref=mine,
            dst_ref=held.at[offset],
            send_sem=send_sem.at[offset],
            recv_sem=recv_sem.at[offset],
            device_id={tm_axis: lax.rem(own + offset, count)},
            device_id_type=pl.DeviceIdType.MESH,
        )
        copy.start()
        copies.append(copy)
    sums_ref[own] = mine[...]
    for step in range(steps):
        for number in range(2):
            tile_ref[step, number] = jnp.broadcast_to(turn_ref[step, number : number + 1, :], (modes, modes)).T
    for offset in range(1, count):
        copies[offset - 1].wait()
        sums_ref[lax.rem(own + count - offset, count)] = held[offset]


def solve_kernel(
    tm_axis, rows_axis, sums_ref, turn_ref, tile_ref, mode_ref, mean_ref, cov_ref,
    tab, cols, line, fresh, main, full, answer, spare, result,
):
    steps = sums_ref.shape[0]
    modes = sums_ref.shape[2]
    width = 2 * modes
    block = cov_ref.shape[1]
    own = lax.axis_index(tm_axis)
    block_row = lax.axis_index(rows_axis)
    links = steps - 1
    sides = (slice(0, modes), slice(modes, width))
    damp = mode_ref[0:1, :]
    damp_sq = damp * damp
    lane = lax.broadcasted_iota(jnp.int32, (TILE, modes), 1)
    sub = lax.broadcasted_iota(jnp.int32, (TILE, modes), 0)
    before = jnp.maximum(own - 1, 0)
    inverse_row, flow_row, right_row, info_row, left_row, other_row = range(6)

    def node(i):
        return own if i == links else jnp.where(own > i, i, links - (i - own))

    def load(ref, index, row):
        return tuple(ref[index, row : row + 1, side] for side in sides)

    def weights_of(at):
        return tuple(sums_ref[at, row : row + 1, :] for row in (8, 9))

    def info_of(at):
        return tuple(sums_ref[at, row : row + 1, :] for row in (6, 7))

    def note(i, row, values):
        for side, value in zip(sides, values):
            line[i, row : row + 1, side] = value

    past = None
    for i in range(links):
        at = node(i)
        inner = jnp.where(jnp.logical_or(at == 0, at == links), 0.0, 1.0)
        keep = jnp.where(own == i, 0.0, 1.0) if i else 0.0
        level = [1.0 + inner * damp_sq + mass for mass in weights_of(at)]
        if i:
            level = [value - (keep * damp_sq) * old for value, old in zip(level, past)]
        inverse = [1.0 / value for value in level]
        note(i, inverse_row, inverse)
        note(i, right_row, [(keep * damp) * value for value in inverse])
        note(i, info_row, info_of(at))
        note(i, other_row, [(keep * damp) * old for old in past] if i else [jnp.zeros_like(damp)] * 2)
        for half, value in enumerate(inverse):
            tab[2 * i + half : 2 * i + half + 1, :] = damp * value
        past = inverse
    has_left, has_right = jnp.where(own > 0, 1.0, 0.0), jnp.where(own < links, 1.0, 0.0)
    left, right = load(line, before, inverse_row), past
    level = [
        1.0 + (has_left * has_right) * damp_sq + mass - (has_left * damp_sq) * a - (has_right * damp_sq) * b
        for mass, a, b in zip(weights_of(own), left, right)
    ]
    inverse = [1.0 / value for value in level]
    note(links, inverse_row, inverse)
    note(links, right_row, [damp * value for value in inverse])
    note(links, info_row, info_of(own))
    left, right = [(has_left * damp) * value for value in left], [(has_right * damp) * value for value in right]
    note(links, left_row, left)
    note(links, other_row, right)
    for half in range(2):
        tab[2 * links + half : 2 * links + half + 1, :] = left[half]
        tab[2 * steps + half : 2 * steps + half + 1, :] = right[half]
    for chunk in range(tab.shape[0] // modes):
        cols[chunk] = tab[chunk * modes : (chunk + 1) * modes, :].T

    def col_of(at, rows):
        value = cols[at // modes, rows, at % modes : at % modes + 1]
        return jnp.broadcast_to(value, (rows.stop - rows.start, modes))

    def build(i):
        at = node(i)
        bases = []
        for rows in ((10, 0), (11, 1)):
            base = jnp.concatenate(
                [jnp.broadcast_to(sums_ref[at, row : row + 1, :], (TILE, modes)) for row in rows], axis=1
            )
            base = pltpu.roll(base, 0, 1, stride=1, stride_axis=0)
            bases.append((base[:, :modes], base[:, modes:]))
        for row in (2, 4):
            base = jnp.concatenate(
                [jnp.broadcast_to(sums_ref[at, row + k : row + k + 1, :], (TILE, modes)) for k in range(2)], axis=1
            )
            base = pltpu.roll(base, width - TILE + 1, 1, stride=1, stride_axis=0)
            bases.append([jnp.take_along_axis(base[:, side], TILE - 1 - sub, axis=0) for side in sides])
        turn = [turn_ref[at, k : k + 1, :] for k in range(2)]
        cos_l, sin_l, cos_r, sin_r = [
            jnp.broadcast_to(value * scale, (TILE, modes)) for scale in load(line, i, inverse_row) for value in turn
        ]
        for q in range(modes // TILE):
            shift = TILE * q
            rows = slice(shift, shift + TILE)

            def moved(low, high, edge, amount):
                value = jnp.where(lane >= edge, low, high) if edge else low
                return pltpu.roll(value, amount, 1) if amount % modes else value

            near_cos, near_sin = [
                moved(low, high, modes - shift, shift) if shift else high for low, high in bases[:2]
            ]
            far_cos, far_sin = [moved(low, high, shift, modes - shift) for low, high in bases[2:]]
            up_a, up_b = near_cos + far_cos, far_sin + near_sin
            low_a, low_b = far_sin - near_sin, near_cos - far_cos
            up_left, up_right = up_a * cos_l + up_b * sin_l, up_b * cos_r - up_a * sin_r
            low_left, low_right = low_a * cos_l + low_b * sin_l, low_b * cos_r - low_a * sin_r
            cos_t, sin_t = tile_ref[at, 0, rows, :], tile_ref[at, 1, rows, :]
            off = lane != sub + shift
            under = slice(modes + shift, modes + shift + TILE)
            fresh[i, rows, sides[0]] = jnp.where(off, cos_t * up_left + sin_t * low_left, 0.0)
            fresh[i, rows, sides[1]] = cos_t * up_right + sin_t * low_right
            fresh[i, under, sides[0]] = cos_t * low_left - sin_t * up_left
            fresh[i, under, sides[1]] = jnp.where(off, cos_t * low_right - sin_t * up_right, 0.0)

    pair = 2 * TILE
    strips = [
        (half, slice(start, start + pair), slice(half * modes + start, half * modes + start + pair))
        for half in range(2) for start in range(0, modes, pair)
    ]
    pair_lane = lax.broadcasted_iota(jnp.int32, (pair, modes), 1)
    pair_sub = lax.broadcasted_iota(jnp.int32, (pair, modes), 0)
    ones = jnp.ones((TILE, width), jnp.bfloat16)

    def flow(i, state, third):
        sums = [jnp.zeros((pair, modes), jnp.float32) for _ in sides]
        for half, part, rows in strips:
            parts = []
            for k, side in enumerate(sides):
                value = main[i, rows, side] + third[rows, side]
                full[i, rows, side] = value
                parts.append(value * state[k])
            column = jnp.sum(parts[0] + parts[1], axis=1, keepdims=True)
            sums[half] += jnp.where(pair_lane == pair_sub + part.start, column, 0.0)
        moved = [value - jnp.sum(total, axis=0, keepdims=True) for value, total in zip(state, sums)]
        note(i, flow_row, moved)
        return moved

    def joined(i, old):
        rights = load(line, i, right_row)
        whole = []
        for half, part, rows in strips:
            values = [fresh[i, rows, side] for side in sides]
            if i:
                down = col_of(2 * (i - 1) + half, part)
                values = [value + down * (old[i - 1, rows, side] * right) for value, side, right in zip(values, sides, rights)]
            whole.append(values)
        return whole

    def packed(whole):
        return jnp.concatenate([jnp.concatenate(values, axis=1) for values in whole], axis=0).astype(jnp.bfloat16)

    build(0)
    third, state, most = None, None, jnp.zeros((TILE, width), jnp.float32)
    for i in range(links):
        narrow = packed(joined(i, main))
        square = dot(narrow, narrow)
        if i:
            moved = flow(i - 1, state, third)
            state = [a + b * c for a, b, c in zip(load(line, i, info_row), load(line, i, other_row), moved)]
        else:
            state = load(line, i, info_row)
        build(i + 1)
        for (half, part, rows), values in zip(strips, joined(i, full)):
            for side, value in zip(sides, values):
                main[i, rows, side] = value - square[rows, side]
        squared = square.astype(jnp.bfloat16)
        third = dot(squared, narrow)
        most = jnp.maximum(most, dot(ones, jnp.abs(squared)))
    flow(links - 1, state, third)

    height = block + pair
    tall = lax.broadcasted_iota(jnp.int32, (block, modes), 0)
    wide = lax.broadcasted_iota(jnp.int32, (block, modes), 1)
    hit = wide == (tall + block_row * block) // 2
    even = tall % 2 == 0
    cosines, sines = turn_ref[own, 2:3, :], turn_ref[own, 3:4, :]

    def pose():
        state = [
            a + b * c + d * e
            for a, b, c, d, e in zip(
                load(line, links, info_row), load(line, links, left_row), load(line, before, flow_row),
                load(line, links, other_row), load(line, links - 1, flow_row),
            )
        ]
        scales = load(line, links, inverse_row)
        spare[:block, sides[0]] = jnp.where(hit, jnp.where(even, cosines, sines) * scales[0], 0.0)
        spare[:block, sides[1]] = jnp.where(hit, jnp.where(even, -sines, cosines) * scales[1], 0.0)
        for side, value, scale in zip(sides, state, scales):
            spare[block:, side] = jnp.where(pair_sub == 0, value * scale, 0.0)

    def product(left, right):
        return dot(left[0], right[0]) + (dot(left[0], right[1]) + dot(left[1], right[0]))

    whole = []
    rights = load(line, links, right_row)
    for half, part, rows in strips:
        first, second = col_of(2 * links + half, part), col_of(2 * steps + half, part)
        whole.append([
            fresh[links, rows, side] + (first * full[before, rows, side] + second * full[links - 1, rows, side]) * right
            for side, right in zip(sides, rights)
        ])
    whole = halves(jnp.concatenate([jnp.concatenate(values, axis=1) for values in whole], axis=0))
    square = halves(product(whole, whole))
    pose()
    asked = spare[...]
    first = asked - product(halves(asked), whole)
    fourth = dot(square[0], square[0]).astype(jnp.bfloat16)
    second = first + product(halves(first), square)
    last = dot(ones, jnp.abs(fourth))
    answer[...] = second + dot(second.astype(jnp.bfloat16), fourth)
    good = jnp.logical_and(jnp.max(most) <= CHAIN_BOUND, jnp.max(last) <= LAST_BOUND)

    @pl.when(jnp.logical_not(good))
    def _():
        rows = lax.broadcasted_iota(jnp.int32, (width, width), 0)
        unit = rows == lax.broadcasted_iota(jnp.int32, (width, width), 1)
        source, target = result.at[0], result.at[1]

        def column(row):
            return jnp.sum(jnp.where(unit, row, 0.0), axis=1, keepdims=True)

        def invert(low):
            high = 1.001 * jnp.max(jnp.sum(jnp.abs(source[...]), axis=0, keepdims=True))
            low = jnp.minimum(low, 0.5 * high)
            center = (high + low) / (high - low)
            slope = 2.0 / (high - low)
            top = 2.0 * center * center - 1.0
            target[...] = jnp.where(unit, 4.0 * center * slope / top, 0.0) - (2.0 * slope * slope / top) * source[...]

            def improve(radius):
                factor = 2.0 / (2.0 - radius * radius)
                residue = jnp.where(unit, 1.0, 0.0) - exact(source[...], target[...])
                target[...] = factor * (target[...] + exact(target[...], residue))
                return radius * radius / (2.0 - radius * radius)

            lax.while_loop(lambda radius: radius > TOLERANCE, improve, 1.0 / top)

        def even_out(i, whole):
            root = jnp.sqrt(line[i, inverse_row : inverse_row + 1, :])
            source[...] = jnp.where(unit, 1.0, 0.0) + column(root) * whole * (1.0 / root)
            return root, column(root)

        full[0] = jnp.zeros((width, width), jnp.float32)
        note(0, flow_row, [jnp.zeros_like(damp)] * 2)

        def advance(i, carry):
            old = jnp.maximum(i - 1, 0)
            down = column(line[old, inverse_row : inverse_row + 1, :] * jnp.concatenate([damp, damp], axis=1))
            root, root_col = even_out(i, fresh[i] + down * full[old] * line[i, right_row : right_row + 1, :])
            invert(0.999 * jnp.min(root * root))
            state = line[i, info_row : info_row + 1, :]
            state = state + line[i, other_row : other_row + 1, :] * line[old, flow_row : flow_row + 1, :]
            scaled = jnp.broadcast_to(state * root, (TILE, width))
            line[i, flow_row : flow_row + 1, :] = exact(scaled, target[...])[0:1] * (1.0 / root)
            full[i] = (1.0 / root_col) * (jnp.where(unit, 1.0, 0.0) - target[...]) * root
            return carry

        lax.fori_loop(0, links, advance, 0)
        root, root_col = even_out(
            links,
            fresh[links] + (
                column(line[links, left_row : left_row + 1, :]) * full[before]
                + column(line[links, other_row : other_row + 1, :]) * full[links - 1]
            ) * line[links, right_row : right_row + 1, :],
        )
        invert(0.999 * jnp.min(1.0 - damp_sq) * jnp.min(root * root))
        pose()
        answer[...] = exact(spare[...] * (1.0 / root), target[...]) * root

    left, right = answer[:, sides[0]], answer[:, sides[1]]
    left, right = left * cosines - right * sines, left * sines + right * cosines
    wide = lax.broadcasted_iota(jnp.int32, (height, modes), 1)
    out = []
    for number in range(2):
        pick = wide // 2 + number * (modes // 2)
        out.append(
            jnp.where(wide % 2 == 0, jnp.take_along_axis(left, pick, axis=1), jnp.take_along_axis(right, pick, axis=1))
        )
    for side, value in zip(sides, out):
        cov_ref[0, :, side] = value[:block]
    means = jnp.concatenate([value[block : block + TILE] for value in out], axis=1)
    mean_ref[...] = pltpu.roll(means, width - block_row * block, 1)[0:1, :block]


def local(observations, site_ids, counts, frequencies, decay, proc_var):
    modes = frequencies.shape[0]
    width = 2 * modes
    count = lax.axis_size("tm")
    steps = count * observations.shape[0]
    block = width // lax.axis_size("rows")
    height = block + 2 * TILE
    table = -(-(2 * steps + 2) // modes) * modes
    vmem = pl.BlockSpec(memory_space=pltpu.VMEM)
    smem = pl.BlockSpec(memory_space=pltpu.SMEM)
    hbm = pl.BlockSpec(memory_space=pltpu.HBM)
    shared = pl.pallas_call(
        functools.partial(share_kernel, "tm"),
        out_shape=(
            jax.ShapeDtypeStruct((steps, 2 * TILE, modes), jnp.float32),
            jax.ShapeDtypeStruct((steps, 8, modes), jnp.float32),
            jax.ShapeDtypeStruct((steps, 2, modes, modes), jnp.float32),
            jax.ShapeDtypeStruct((8, modes), jnp.float32),
        ),
        in_specs=[smem] + [hbm] * 5,
        out_specs=(vmem,) * 4,
        scratch_shapes=[
            pltpu.VMEM(site_ids.shape, jnp.int32),
            pltpu.VMEM(observations.shape, jnp.float32),
            pltpu.VMEM((1, modes), jnp.float32),
            pltpu.VMEM((1, modes), jnp.float32),
            pltpu.VMEM((1, modes), jnp.float32),
            pltpu.VMEM((2 * TILE, modes), jnp.float32),
            pltpu.VMEM((count, 2 * TILE, modes), jnp.float32),
            pltpu.SemaphoreType.DMA((5,)),
            pltpu.SemaphoreType.DMA((count,)),
            pltpu.SemaphoreType.DMA((count,)),
        ],
        compiler_params=pltpu.CompilerParams(collective_id=0, has_side_effects=True, vmem_limit_bytes=16 << 20),
        name="share",
    )(
        counts,
        *(
            pltpu.with_memory_space_constraint(value, pltpu.HBM)
            for value in (site_ids, observations, frequencies[None], decay[None], proc_var[None])
        ),
    )
    return pl.pallas_call(
        functools.partial(solve_kernel, "tm", "rows"),
        out_shape=(
            jax.ShapeDtypeStruct((1, block), jnp.float32),
            jax.ShapeDtypeStruct((1, block, width), jnp.float32),
        ),
        in_specs=[vmem] * 4,
        out_specs=(vmem, vmem),
        scratch_shapes=[
            pltpu.VMEM((table, modes), jnp.float32),
            pltpu.VMEM((table // modes, modes, modes), jnp.float32),
            pltpu.VMEM((steps, 8, width), jnp.float32),
            pltpu.VMEM((steps, width, width), jnp.float32),
            pltpu.VMEM((steps - 1, width, width), jnp.float32),
            pltpu.VMEM((steps - 1, width, width), jnp.float32),
            pltpu.VMEM((height, width), jnp.float32),
            pltpu.VMEM((height, width), jnp.float32),
            pltpu.VMEM((2, width, width), jnp.float32),
        ],
        compiler_params=pltpu.CompilerParams(vmem_limit_bytes=40 << 20),
        name="solve",
    )(*shared)


def solution(mesh):
    return jax.shard_map(
        local,
        mesh=mesh,
        in_specs=(P("tm", None), P("tm", None), P("tm"), P(), P(), P()),
        out_specs=(P("tm", "rows"), P("tm", "rows", None)),
        check_vma=False,
    )
```

```python
import functools
import math

import jax
import jax.numpy as jnp
from jax import lax
from jax.experimental import pallas as pl
from jax.experimental.pallas import tpu as pltpu
from jax.sharding import PartitionSpec as P

GRID = 4096
OBS_VAR = 64
FINE = 16
TILE = 8
LANES = 128
CHAIN_BOUND = 2.5e-3
LAST_BOUND = 5e-3
TOLERANCE = 1e-6
HALF_UNIT = math.pi / GRID
HALF_SINE = tuple(-2.0 * c * HALF_UNIT ** (2 * k + 1) for k, c in enumerate((
    0.9999999766, -0.1666664763, 0.008332899823, -0.0001980089775, 2.590488469e-06
)))
HALF_COSINE = tuple(c * HALF_UNIT ** (2 * k) for k, c in enumerate((
    0.9999999535, -0.4999990535, 0.04166358469, -0.001385370429, 2.315393125e-05
)))

exact_mode = lax.Precision.HIGHEST


def exact(left, right):
    return jnp.dot(left, right, precision=exact_mode, preferred_element_type=jnp.float32)


dot = functools.partial(jnp.dot, preferred_element_type=jnp.float32)


def halves(value):
    high = value.astype(jnp.bfloat16)
    return high, (value - high.astype(jnp.float32)).astype(jnp.bfloat16)


def spread_by(value, picks):
    high, low = halves(value)
    picks = picks.astype(jnp.bfloat16)
    return dot(high, picks) + dot(low, picks)


def circle(angle):
    square = angle * angle
    cosine = 1.0 / 40320.0 - square * (1.0 / 3628800.0)
    cosine = 1.0 - square * (0.5 - square * (1.0 / 24.0 - square * (1.0 / 720.0 - square * cosine)))
    sine = 1.0 / 5040.0 - square * (1.0 / 362880.0)
    sine = angle * (1.0 - square * (1.0 / 6.0 - square * (1.0 / 120.0 - square * sine)))
    return cosine, sine


def quarter_turn(quadrant, cosine, sine):
    odd = (quadrant & 1) == 1
    new_cosine = jnp.where(odd, sine, cosine)
    new_sine = jnp.where(odd, cosine, sine)
    new_cosine = jnp.where(((quadrant + 1) & 2) == 2, -new_cosine, new_cosine)
    new_sine = jnp.where((quadrant & 2) == 2, -new_sine, new_sine)
    return new_cosine, new_sine


def share_kernel(
    tm_axis, counts_ref, site_hbm, obs_hbm, freq_hbm, decay_hbm, var_hbm,
    sums_ref, turn_ref, fresh_ref, mode_ref, site_ref, obs_ref, freq_ref, decay_ref, var_ref,
    tile_ref, factor_ref, mine, held, load_sem, send_sem, recv_sem,
):
    count = lax.axis_size(tm_axis)
    own = lax.axis_index(tm_axis)
    modes = freq_ref.shape[1]
    steps = sums_ref.shape[0]
    loads = [
        pltpu.make_async_copy(source, target, load_sem.at[number])
        for number, (source, target) in enumerate((
            (site_hbm, site_ref), (obs_hbm, obs_ref), (freq_hbm, freq_ref), (var_hbm, var_ref), (decay_hbm, decay_ref),
        ))
    ]
    for load in loads:
        load.start()
    barrier = pltpu.get_barrier_semaphore()
    for offset in range(1, count):
        pl.semaphore_signal(
            barrier, inc=1, device_id={tm_axis: lax.rem(own + offset, count)},
            device_id_type=pl.DeviceIdType.MESH,
        )
    for load in loads:
        load.wait()

    frequency = freq_ref[...]
    turns = jnp.where(jnp.abs(frequency) > 0.25 * math.pi, 1, 0) + jnp.where(
        jnp.abs(frequency) > 0.75 * math.pi, 1, 0
    )
    turns = jnp.where(frequency < 0.0, -turns, turns)
    share = turns.astype(jnp.float32)
    reduced = (frequency - share * 1.5703125) - share * (0.5 * math.pi - 1.5703125)
    turn_cosine, turn_sine = quarter_turn(turns + 4, *circle(reduced))
    level = 0.5 / (OBS_VAR * modes)
    root = math.sqrt(level)
    variance = var_ref[...]
    mode_ref[0:1, :] = jnp.exp(-decay_ref[...])
    now_cos = jnp.sqrt(variance)
    now_sin = jnp.zeros_like(now_cos)
    own_cos, own_sin = now_cos, now_sin
    for step in range(steps):
        for number, value in enumerate((now_cos * root, now_sin * root, now_cos, now_sin)):
            turn_ref[step, number : number + 1, :] = value
        own_cos = jnp.where(own == step, now_cos, own_cos)
        own_sin = jnp.where(own == step, now_sin, own_sin)
        now_cos, now_sin = (
            now_cos * turn_cosine - now_sin * turn_sine, now_cos * turn_sine + now_sin * turn_cosine
        )

    rows, lanes = site_ref.shape
    half_turn = GRID // 2
    place = lax.broadcasted_iota(jnp.int32, (TILE, lanes), 0)

    def wave(sites, exponent):
        at = ((exponent * sites) & (GRID - 1)).astype(jnp.float32) - half_turn
        square = at * at
        sine, cosine = HALF_SINE[-1], HALF_COSINE[-1]
        for a in HALF_SINE[-2::-1]:
            sine = sine * square + a
        for a in HALF_COSINE[-2::-1]:
            cosine = cosine * square + a
        sine = sine * at
        return (sine * sine) * 0.5 - 1.0, sine * cosine

    def turned(wave, by):
        return wave[0] * by[0] - wave[1] * by[1], wave[0] * by[1] + wave[1] * by[0]

    sites = site_ref[...]
    one = wave(sites, 1)
    two = turned(one, one)
    far = turned(wave(sites, FINE * TILE), two)
    slots = lax.broadcasted_iota(jnp.int32, (rows, lanes), 0) * lanes + lax.broadcasted_iota(jnp.int32, (rows, lanes), 1)
    live = jnp.where(slots < counts_ref[0], 1.0, 0.0)
    seen = live * obs_ref[...]
    factors = (live, *[v * live for v in two], *[v * live for v in far], *[v * seen for v in one], *wave(sites, TILE))
    for number, value in enumerate(factors):
        factor_ref[number] = value
    left, right = [], []
    for row in range(rows):
        spot = jnp.broadcast_to(site_ref[row : row + 1, :], (TILE, lanes))
        fine, coarse = wave(spot, place), wave(spot, place * FINE)
        live, *by = [jnp.broadcast_to(factor_ref[k, row : row + 1, :], (TILE, lanes)) for k in range(len(factors))]
        tiles = [(coarse[0] * live, coarse[1] * live)] + [turned(coarse, by[k : k + 2]) for k in (0, 2, 4)]
        upper = turned(fine, by[6:8])
        left.append(jnp.concatenate([tile[0] for tile in tiles] + [tile[1] for tile in tiles], axis=0))
        right.append(jnp.concatenate([fine[0], upper[0], fine[1], upper[1]], axis=0))
    left, right = jnp.concatenate(left, axis=1), jnp.concatenate(right, axis=1)
    left_high, left_low = halves(left)
    right_high, right_low = halves(right)
    beside = functools.partial(
        lax.dot_general,
        dimension_numbers=(((1,), (1,)), ((), ())),
        preferred_element_type=jnp.float32,
    )
    sums = beside(left_high, right_high) + (beside(left_high, right_low) + beside(left_low, right_high))
    tall = lax.broadcasted_iota(jnp.int32, (2 * FINE, 6 * modes), 0)
    wide = lax.broadcasted_iota(jnp.int32, (2 * FINE, 6 * modes), 1)
    picks = jnp.where(wide < 2 * modes, wide, jnp.where(wide < 4 * modes, 2 * wide, 6 * modes - wide)) & (FINE - 1)
    spread = spread_by(sums, jnp.where(tall == picks + (FINE * (wide // modes)) % (2 * FINE), 1.0, 0.0))
    half = left.shape[0] // 2
    pieces = [spread[:, number * modes : (number + 1) * modes] for number in range(6)]
    real, even_real, back_real = [pieces[number][:half] - pieces[number + 1][half:] for number in (0, 2, 4)]
    imaginary, even_imaginary, back_imaginary = [
        pieces[number][half:] + pieces[number + 1][:half] for number in (0, 2, 4)
    ]
    lane = lax.broadcasted_iota(jnp.int32, (TILE, modes), 1)
    group = lax.broadcasted_iota(jnp.int32, (TILE, modes), 0)
    keep = jnp.where(lane // FINE == group, 1.0, 0.0)
    keep_low = jnp.where(2 * lane // FINE == group, 1.0, 0.0)
    keep_back = jnp.where((modes - lane) // FINE == group, 1.0, 0.0)
    keep_high = jnp.where(2 * lane // FINE == group + TILE, 1.0, 0.0)

    def tile(value, number):
        return value[number * TILE : (number + 1) * TILE]

    def flat(value, number, keep=keep):
        return jnp.sum(tile(value, number) * keep, axis=0, keepdims=True)

    def even(value):
        return jnp.sum(tile(value, 1) * keep_low + tile(value, 2) * keep_high, axis=0, keepdims=True)

    info_scale = 1.0 / (OBS_VAR * math.sqrt(modes))
    turn_cos, turn_sin = own_cos * info_scale, own_sin * info_scale
    info_cos, info_sin = flat(real, 3), flat(imaginary, 3)
    near_cos = flat(real, 0)
    mass = (variance * level) * near_cos[:, 0:1]
    swing = (own_cos * own_cos - own_sin * own_sin) * level * even(even_real)
    swing = swing + (own_cos * own_sin) * (2.0 * level) * even(even_imaginary)
    rows = (
        near_cos, flat(imaginary, 0), flat(real, 1), flat(real, 2), flat(imaginary, 1), flat(imaginary, 2),
        turn_cos * info_cos + turn_sin * info_sin, turn_cos * info_sin - turn_sin * info_cos,
        mass + swing, mass - swing, flat(back_real, 0, keep_back), -flat(back_imaginary, 0, keep_back),
        jnp.zeros((4, modes), jnp.float32),
    )
    mine[...] = jnp.concatenate(rows, axis=0)

    pl.semaphore_wait(barrier, count - 1)
    copies = []
    for offset in range(1, count):
        copy = pltpu.make_async_remote_copy(
            src_ref=mine,
            dst_ref=held.at[offset],
            send_sem=send_sem.at[offset],
            recv_sem=recv_sem.at[offset],
            device_id={tm_axis: lax.rem(own + offset, count)},
            device_id_type=pl.DeviceIdType.MESH,
        )
        copy.start()
        copies.append(copy)
    for step in range(steps):
        for number in range(2):
            tile_ref[step, number] = jnp.broadcast_to(turn_ref[step, number : number + 1, :], (modes, modes)).T

    sub = group

    def build(at, message):
        bases = []
        for numbers in ((10, 0), (11, 1), (2, 3), (4, 5)):
            base = jnp.concatenate(
                [jnp.broadcast_to(message[number : number + 1, :], (TILE, modes)) for number in numbers], axis=1
            )
            if numbers[0] >= FINE // 2 + 2:
                base = pltpu.roll(base, 0, 1, stride=1, stride_axis=0)
                bases.append((base[:, :modes], base[:, modes:]))
            else:
                base = pltpu.roll(base, 2 * modes - TILE + 1, 1, stride=1, stride_axis=0)
                bases.append([
                    jnp.take_along_axis(base[:, k * modes : (k + 1) * modes], TILE - 1 - sub, axis=0) for k in range(2)
                ])
        cos_c, sin_c = [jnp.broadcast_to(turn_ref[at, k : k + 1, :], (TILE, modes)) for k in range(2)]
        for q in range(modes // TILE):
            shift = TILE * q
            spots = slice(shift, shift + TILE)

            def moved(low, high, edge, amount):
                value = jnp.where(lane >= edge, low, high) if edge else low
                return pltpu.roll(value, amount, 1) if amount % modes else value

            near_cos, near_sin = [
                moved(low, high, modes - shift, shift) if shift else high for low, high in bases[:2]
            ]
            far_cos, far_sin = [moved(low, high, shift, modes - shift) for low, high in bases[2:]]
            up_a, up_b = near_cos + far_cos, far_sin + near_sin
            low_a, low_b = far_sin - near_sin, near_cos - far_cos
            up_left, up_right = up_a * cos_c + up_b * sin_c, up_b * cos_c - up_a * sin_c
            low_left, low_right = low_a * cos_c + low_b * sin_c, low_b * cos_c - low_a * sin_c
            cos_t, sin_t = tile_ref[at, 0, spots, :], tile_ref[at, 1, spots, :]
            off = lane != sub + shift
            under = slice(modes + shift, modes + shift + TILE)
            fresh_ref[at, spots, :modes] = jnp.where(off, cos_t * up_left + sin_t * low_left, 0.0)
            fresh_ref[at, spots, modes:] = cos_t * up_right + sin_t * low_right
            fresh_ref[at, under, :modes] = cos_t * low_left - sin_t * up_left
            fresh_ref[at, under, modes:] = jnp.where(off, cos_t * low_right - sin_t * up_right, 0.0)

    def take(number, carry):
        offset = count - 1 - number
        arrived = pltpu.make_async_remote_copy(
            src_ref=mine,
            dst_ref=held.at[offset],
            send_sem=send_sem.at[offset],
            recv_sem=recv_sem.at[offset],
            device_id={tm_axis: lax.rem(own + offset, count)},
            device_id_type=pl.DeviceIdType.MESH,
        )
        arrived.wait_recv()
        peer = lax.rem(own + count - offset, count)
        message = held[offset]
        sums_ref[peer] = message
        build(peer, message)
        return carry

    message = mine[...]
    sums_ref[own] = message
    build(own, message)
    lax.fori_loop(0, count - 1, take, 0)
    for copy in copies:
        copy.wait_send()


def solve_kernel(
    tm_axis, rows_axis, sums_ref, turn_ref, fresh, mode_ref, mean_ref, cov_ref,
    tab, cols, line, kept, main, full, answer, spare, result,
):
    steps = sums_ref.shape[0]
    modes = sums_ref.shape[2]
    width = 2 * modes
    block = cov_ref.shape[1]
    own = lax.axis_index(tm_axis)
    block_row = lax.axis_index(rows_axis)
    links = steps - 1
    sides = (slice(0, modes), slice(modes, width))
    damp = mode_ref[0:1, :]
    damp_sq = damp * damp
    lane = lax.broadcasted_iota(jnp.int32, (TILE, modes), 1)
    sub = lax.broadcasted_iota(jnp.int32, (TILE, modes), 0)
    before = jnp.maximum(own - 1, 0)
    inverse_row, flow_row, right_row, info_row, left_row, other_row = range(6)

    def node(i):
        return own if i == links else jnp.where(own > i, i, links - (i - own))

    def load(ref, index, row):
        return tuple(ref[index, row : row + 1, side] for side in sides)

    def weights_of(at):
        return tuple(sums_ref[at, row : row + 1, :] for row in (8, 9))

    def info_of(at):
        return tuple(sums_ref[at, row : row + 1, :] for row in (6, 7))

    def note(i, row, values):
        for side, value in zip(sides, values):
            line[i, row : row + 1, side] = value

    past = None
    for i in range(links):
        at = node(i)
        inner = jnp.where(jnp.logical_or(at == 0, at == links), 0.0, 1.0)
        keep = jnp.where(own == i, 0.0, 1.0) if i else 0.0
        level = [1.0 + inner * damp_sq + mass for mass in weights_of(at)]
        if i:
            level = [value - (keep * damp_sq) * old for value, old in zip(level, past)]
        inverse = [1.0 / value for value in level]
        note(i, inverse_row, inverse)
        note(i, right_row, [(keep * damp) * value for value in inverse])
        note(i, info_row, info_of(at))
        note(i, other_row, [(keep * damp) * old for old in past] if i else [jnp.zeros_like(damp)] * 2)
        for half, value in enumerate(inverse):
            tab[2 * i + half : 2 * i + half + 1, :] = damp * value
        past = inverse
    has_left, has_right = jnp.where(own > 0, 1.0, 0.0), jnp.where(own < links, 1.0, 0.0)
    left, right = load(line, before, inverse_row), past
    level = [
        1.0 + (has_left * has_right) * damp_sq + mass - (has_left * damp_sq) * a - (has_right * damp_sq) * b
        for mass, a, b in zip(weights_of(own), left, right)
    ]
    inverse = [1.0 / value for value in level]
    note(links, inverse_row, inverse)
    note(links, right_row, [damp * value for value in inverse])
    note(links, info_row, info_of(own))
    left, right = [(has_left * damp) * value for value in left], [(has_right * damp) * value for value in right]
    note(links, left_row, left)
    note(links, other_row, right)
    for half in range(2):
        tab[2 * links + half : 2 * links + half + 1, :] = left[half]
        tab[2 * steps + half : 2 * steps + half + 1, :] = right[half]
    for chunk in range(tab.shape[0] // modes):
        cols[chunk] = tab[chunk * modes : (chunk + 1) * modes, :].T

    def col_of(at, rows):
        value = cols[at // modes, rows, at % modes : at % modes + 1]
        return jnp.broadcast_to(value, (rows.stop - rows.start, modes))

    pair = 2 * TILE
    strips = [
        (half, slice(start, start + pair), slice(half * modes + start, half * modes + start + pair))
        for half in range(2) for start in range(0, modes, pair)
    ]
    pair_lane = lax.broadcasted_iota(jnp.int32, (pair, modes), 1)
    pair_sub = lax.broadcasted_iota(jnp.int32, (pair, modes), 0)
    ones = jnp.ones((TILE, width), jnp.bfloat16)

    def flow(i, state, third):
        sums = [jnp.zeros((pair, modes), jnp.float32) for _ in sides]
        for half, part, rows in strips:
            parts = []
            for k, side in enumerate(sides):
                value = main[i, rows, side] + third[rows, side]
                full[i, rows, side] = value
                parts.append(value * state[k])
            column = jnp.sum(parts[0] + parts[1], axis=1, keepdims=True)
            sums[half] += jnp.where(pair_lane == pair_sub + part.start, column, 0.0)
        moved = [value - jnp.sum(total, axis=0, keepdims=True) for value, total in zip(state, sums)]
        note(i, flow_row, moved)
        return moved

    def packed(whole):
        return jnp.concatenate([jnp.concatenate(values, axis=1) for values in whole], axis=0).astype(jnp.bfloat16)

    third, state, most = None, None, jnp.zeros((TILE, width), jnp.float32)
    for i in range(links):
        scales, rights = load(line, i, inverse_row), load(line, i, right_row)
        downs = [col_of(2 * (i - 1) + half, part) for half, part, rows in strips] if i else [None] * len(strips)
        whole = []
        for (half, part, rows), down in zip(strips, downs):
            values = []
            for side, scale, right in zip(sides, scales, rights):
                value = fresh[node(i), rows, side] * scale
                if i:
                    value = value + down * (main[i - 1, rows, side] * right)
                kept[i % 2, rows, side] = value
                values.append(value)
            whole.append(values)
        narrow = packed(whole)
        square = dot(narrow, narrow)
        if i:
            moved = flow(i - 1, state, third)
            state = [a + b * c for a, b, c in zip(load(line, i, info_row), load(line, i, other_row), moved)]
        else:
            state = load(line, i, info_row)
        for (half, part, rows), down in zip(strips, downs):
            for side, right in zip(sides, rights):
                value = kept[i % 2, rows, side] - square[rows, side]
                if i:
                    value = value + down * (third[rows, side] * right)
                main[i, rows, side] = value
        squared = square.astype(jnp.bfloat16)
        third = dot(squared, narrow)
        most = jnp.maximum(most, dot(ones, jnp.abs(squared)))
    flow(links - 1, state, third)

    height = block + pair
    tall = lax.broadcasted_iota(jnp.int32, (block, modes), 0)
    wide = lax.broadcasted_iota(jnp.int32, (block, modes), 1)
    hit = wide == (tall + block_row * block) // 2
    even = tall % 2 == 0
    cosines, sines = turn_ref[own, 2:3, :], turn_ref[own, 3:4, :]

    def pose():
        state = [
            a + b * c + d * e
            for a, b, c, d, e in zip(
                load(line, links, info_row), load(line, links, left_row), load(line, before, flow_row),
                load(line, links, other_row), load(line, links - 1, flow_row),
            )
        ]
        scales = load(line, links, inverse_row)
        spare[:block, sides[0]] = jnp.where(hit, jnp.where(even, cosines, sines) * scales[0], 0.0)
        spare[:block, sides[1]] = jnp.where(hit, jnp.where(even, -sines, cosines) * scales[1], 0.0)
        for side, value, scale in zip(sides, state, scales):
            spare[block:, side] = jnp.where(pair_sub == 0, value * scale, 0.0)

    def product(left, right):
        return dot(left[0], right[0]) + (dot(left[0], right[1]) + dot(left[1], right[0]))

    whole = []
    scales, rights = load(line, links, inverse_row), load(line, links, right_row)
    for half, part, rows in strips:
        first, second = col_of(2 * links + half, part), col_of(2 * steps + half, part)
        whole.append([
            fresh[own, rows, side] * scale + (first * full[before, rows, side] + second * full[links - 1, rows, side]) * right
            for side, scale, right in zip(sides, scales, rights)
        ])
    whole = halves(jnp.concatenate([jnp.concatenate(values, axis=1) for values in whole], axis=0))
    square = halves(product(whole, whole))
    pose()
    asked = spare[...]
    first = asked - product(halves(asked), whole)
    fourth = dot(square[0], square[0]).astype(jnp.bfloat16)
    second = first + product(halves(first), square)
    last = dot(ones, jnp.abs(fourth))
    answer[...] = second + dot(second.astype(jnp.bfloat16), fourth)
    good = jnp.logical_and(jnp.max(most) <= CHAIN_BOUND, jnp.max(last) <= LAST_BOUND)

    @pl.when(jnp.logical_not(good))
    def _():
        rows = lax.broadcasted_iota(jnp.int32, (width, width), 0)
        unit = rows == lax.broadcasted_iota(jnp.int32, (width, width), 1)
        source, target = result.at[0], result.at[1]

        def column(row):
            return jnp.sum(jnp.where(unit, row, 0.0), axis=1, keepdims=True)

        def invert(low):
            high = 1.001 * jnp.max(jnp.sum(jnp.abs(source[...]), axis=0, keepdims=True))
            low = jnp.minimum(low, 0.5 * high)
            center = (high + low) / (high - low)
            slope = 2.0 / (high - low)
            top = 2.0 * center * center - 1.0
            target[...] = jnp.where(unit, 4.0 * center * slope / top, 0.0) - (2.0 * slope * slope / top) * source[...]

            def improve(radius):
                factor = 2.0 / (2.0 - radius * radius)
                residue = jnp.where(unit, 1.0, 0.0) - exact(source[...], target[...])
                target[...] = factor * (target[...] + exact(target[...], residue))
                return radius * radius / (2.0 - radius * radius)

            lax.while_loop(lambda radius: radius > TOLERANCE, improve, 1.0 / top)

        def even_out(i, whole):
            root = jnp.sqrt(line[i, inverse_row : inverse_row + 1, :])
            source[...] = jnp.where(unit, 1.0, 0.0) + column(root) * whole * (1.0 / root)
            return root, column(root)

        full[0] = jnp.zeros((width, width), jnp.float32)
        note(0, flow_row, [jnp.zeros_like(damp)] * 2)

        def advance(i, carry):
            old = jnp.maximum(i - 1, 0)
            down = column(line[old, inverse_row : inverse_row + 1, :] * jnp.concatenate([damp, damp], axis=1))
            at = jnp.where(own > i, i, links - (i - own))
            plain = fresh[at] * line[i, inverse_row : inverse_row + 1, :]
            root, root_col = even_out(i, plain + down * full[old] * line[i, right_row : right_row + 1, :])
            invert(0.999 * jnp.min(root * root))
            state = line[i, info_row : info_row + 1, :]
            state = state + line[i, other_row : other_row + 1, :] * line[old, flow_row : flow_row + 1, :]
            scaled = jnp.broadcast_to(state * root, (TILE, width))
            line[i, flow_row : flow_row + 1, :] = exact(scaled, target[...])[0:1] * (1.0 / root)
            full[i] = (1.0 / root_col) * (jnp.where(unit, 1.0, 0.0) - target[...]) * root
            return carry

        lax.fori_loop(0, links, advance, 0)
        root, root_col = even_out(
            links,
            fresh[own] * line[links, inverse_row : inverse_row + 1, :] + (
                column(line[links, left_row : left_row + 1, :]) * full[before]
                + column(line[links, other_row : other_row + 1, :]) * full[links - 1]
            ) * line[links, right_row : right_row + 1, :],
        )
        invert(0.999 * jnp.min(1.0 - damp_sq) * jnp.min(root * root))
        pose()
        answer[...] = exact(spare[...] * (1.0 / root), target[...]) * root

    left, right = answer[:, sides[0]], answer[:, sides[1]]
    left, right = left * cosines - right * sines, left * sines + right * cosines
    wide = lax.broadcasted_iota(jnp.int32, (height, modes), 1)
    out = []
    for number in range(2):
        pick = wide // 2 + number * (modes // 2)
        out.append(
            jnp.where(wide % 2 == 0, jnp.take_along_axis(left, pick, axis=1), jnp.take_along_axis(right, pick, axis=1))
        )
    for side, value in zip(sides, out):
        cov_ref[0, :, side] = value[:block]
    means = jnp.concatenate([value[block : block + TILE] for value in out], axis=1)
    mean_ref[...] = pltpu.roll(means, width - block_row * block, 1)[0:1, :block]


def local(observations, site_ids, counts, frequencies, decay, proc_var):
    modes = frequencies.shape[0]
    width = 2 * modes
    count = lax.axis_size("tm")
    steps = count * observations.shape[0]
    block = width // lax.axis_size("rows")
    height = block + 2 * TILE
    dense = (site_ids.shape[1] // LANES, LANES)
    table = -(-(2 * steps + 2) // modes) * modes
    vmem = pl.BlockSpec(memory_space=pltpu.VMEM)
    smem = pl.BlockSpec(memory_space=pltpu.SMEM)
    hbm = pl.BlockSpec(memory_space=pltpu.HBM)
    shared = pl.pallas_call(
        functools.partial(share_kernel, "tm"),
        out_shape=(
            jax.ShapeDtypeStruct((steps, 2 * TILE, modes), jnp.float32),
            jax.ShapeDtypeStruct((steps, 8, modes), jnp.float32),
            jax.ShapeDtypeStruct((steps, width, width), jnp.float32),
            jax.ShapeDtypeStruct((8, modes), jnp.float32),
        ),
        in_specs=[smem] + [hbm] * 5,
        out_specs=(vmem,) * 4,
        scratch_shapes=[
            pltpu.VMEM(dense, jnp.int32),
            pltpu.VMEM(dense, jnp.float32),
            pltpu.VMEM((1, modes), jnp.float32),
            pltpu.VMEM((1, modes), jnp.float32),
            pltpu.VMEM((1, modes), jnp.float32),
            pltpu.VMEM((steps, 2, modes, modes), jnp.float32),
            pltpu.VMEM((9, *dense), jnp.float32),
            pltpu.VMEM((2 * TILE, modes), jnp.float32),
            pltpu.VMEM((count, 2 * TILE, modes), jnp.float32),
            pltpu.SemaphoreType.DMA((5,)),
            pltpu.SemaphoreType.DMA((count,)),
            pltpu.SemaphoreType.DMA((count,)),
        ],
        compiler_params=pltpu.CompilerParams(collective_id=0, has_side_effects=True, vmem_limit_bytes=16 << 20),
        name="share",
    )(
        counts,
        *(
            pltpu.with_memory_space_constraint(value, pltpu.HBM)
            for value in (site_ids.reshape(dense), observations.reshape(dense), frequencies[None], decay[None], proc_var[None])
        ),
    )
    return pl.pallas_call(
        functools.partial(solve_kernel, "tm", "rows"),
        out_shape=(
            jax.ShapeDtypeStruct((1, block), jnp.float32),
            jax.ShapeDtypeStruct((1, block, width), jnp.float32),
        ),
        in_specs=[vmem] * 4,
        out_specs=(vmem, vmem),
        scratch_shapes=[
            pltpu.VMEM((table, modes), jnp.float32),
            pltpu.VMEM((table // modes, modes, modes), jnp.float32),
            pltpu.VMEM((steps, 8, width), jnp.float32),
            pltpu.VMEM((2, width, width), jnp.float32),
            pltpu.VMEM((steps - 1, width, width), jnp.float32),
            pltpu.VMEM((steps - 1, width, width), jnp.float32),
            pltpu.VMEM((height, width), jnp.float32),
            pltpu.VMEM((height, width), jnp.float32),
            pltpu.VMEM((2, width, width), jnp.float32),
        ],
        compiler_params=pltpu.CompilerParams(vmem_limit_bytes=40 << 20),
        name="solve",
    )(*shared)


def solution(mesh):
    return jax.shard_map(
        local,
        mesh=mesh,
        in_specs=(P("tm", None), P("tm", None), P("tm"), P(), P(), P()),
        out_specs=(P("tm", "rows"), P("tm", "rows", None)),
        check_vma=False,
    )
```

```python
import functools
import math

import jax
import jax.numpy as jnp
from jax import lax
from jax.experimental import pallas as pl
from jax.experimental.pallas import tpu as pltpu
from jax.sharding import PartitionSpec as P

GRID = 4096
OBS_VAR = 64
FINE = 16
TILE = 8
LANES = 128
CHAIN_BOUND = 2.5e-3
LAST_BOUND = 5e-3
TOLERANCE = 1e-6
HALF_UNIT = math.pi / GRID
HALF_SINE = tuple(-2.0 * c * HALF_UNIT ** (2 * k + 1) for k, c in enumerate((
    0.9999999766, -0.1666664763, 0.008332899823, -0.0001980089775, 2.590488469e-06
)))
HALF_COSINE = tuple(c * HALF_UNIT ** (2 * k) for k, c in enumerate((
    0.9999999535, -0.4999990535, 0.04166358469, -0.001385370429, 2.315393125e-05
)))

exact_mode = lax.Precision.HIGHEST


def exact(left, right):
    return jnp.dot(left, right, precision=exact_mode, preferred_element_type=jnp.float32)


dot = functools.partial(jnp.dot, preferred_element_type=jnp.float32)


def halves(value):
    high = value.astype(jnp.bfloat16)
    return high, (value - high.astype(jnp.float32)).astype(jnp.bfloat16)


def spread_by(value, picks):
    high, low = halves(value)
    picks = picks.astype(jnp.bfloat16)
    return dot(high, picks) + dot(low, picks)


def circle(angle):
    square = angle * angle
    cosine = 1.0 / 40320.0 - square * (1.0 / 3628800.0)
    cosine = 1.0 - square * (0.5 - square * (1.0 / 24.0 - square * (1.0 / 720.0 - square * cosine)))
    sine = 1.0 / 5040.0 - square * (1.0 / 362880.0)
    sine = angle * (1.0 - square * (1.0 / 6.0 - square * (1.0 / 120.0 - square * sine)))
    return cosine, sine


def quarter_turn(quadrant, cosine, sine):
    odd = (quadrant & 1) == 1
    new_cosine = jnp.where(odd, sine, cosine)
    new_sine = jnp.where(odd, cosine, sine)
    new_cosine = jnp.where(((quadrant + 1) & 2) == 2, -new_cosine, new_cosine)
    new_sine = jnp.where((quadrant & 2) == 2, -new_sine, new_sine)
    return new_cosine, new_sine


def share_kernel(
    tm_axis, counts_ref, site_hbm, obs_hbm, freq_hbm, decay_hbm, var_hbm,
    sums_ref, turn_ref, fresh_ref, mode_ref, site_ref, obs_ref, freq_ref, decay_ref, var_ref,
    tile_ref, factor_ref, mine, held, load_sem, send_sem, recv_sem,
):
    count = lax.axis_size(tm_axis)
    own = lax.axis_index(tm_axis)
    modes = freq_ref.shape[1]
    steps = sums_ref.shape[0]
    loads = [
        pltpu.make_async_copy(source, target, load_sem.at[number])
        for number, (source, target) in enumerate((
            (site_hbm, site_ref), (obs_hbm, obs_ref), (freq_hbm, freq_ref), (var_hbm, var_ref), (decay_hbm, decay_ref),
        ))
    ]
    for load in loads:
        load.start()
    barrier = pltpu.get_barrier_semaphore()
    for offset in range(1, count):
        pl.semaphore_signal(
            barrier, inc=1, device_id={tm_axis: lax.rem(own + offset, count)},
            device_id_type=pl.DeviceIdType.MESH,
        )
    for load in loads:
        load.wait()

    frequency = freq_ref[...]
    turns = jnp.where(jnp.abs(frequency) > 0.25 * math.pi, 1, 0) + jnp.where(
        jnp.abs(frequency) > 0.75 * math.pi, 1, 0
    )
    turns = jnp.where(frequency < 0.0, -turns, turns)
    share = turns.astype(jnp.float32)
    reduced = (frequency - share * 1.5703125) - share * (0.5 * math.pi - 1.5703125)
    turn_cosine, turn_sine = quarter_turn(turns + 4, *circle(reduced))
    level = 0.5 / (OBS_VAR * modes)
    root = math.sqrt(level)
    variance = var_ref[...]
    mode_ref[0:1, :] = jnp.exp(-decay_ref[...])
    now_cos = jnp.sqrt(variance)
    now_sin = jnp.zeros_like(now_cos)
    own_cos, own_sin = now_cos, now_sin
    for step in range(steps):
        for number, value in enumerate((now_cos * root, now_sin * root, now_cos, now_sin)):
            turn_ref[step, number : number + 1, :] = value
        own_cos = jnp.where(own == step, now_cos, own_cos)
        own_sin = jnp.where(own == step, now_sin, own_sin)
        now_cos, now_sin = (
            now_cos * turn_cosine - now_sin * turn_sine, now_cos * turn_sine + now_sin * turn_cosine
        )

    rows, lanes = site_ref.shape
    half_turn = GRID // 2
    place = lax.broadcasted_iota(jnp.int32, (TILE, lanes), 0)

    def wave(sites, exponent):
        at = ((exponent * sites) & (GRID - 1)).astype(jnp.float32) - half_turn
        square = at * at
        sine, cosine = HALF_SINE[-1], HALF_COSINE[-1]
        for a in HALF_SINE[-2::-1]:
            sine = sine * square + a
        for a in HALF_COSINE[-2::-1]:
            cosine = cosine * square + a
        sine = sine * at
        return (sine * sine) * 0.5 - 1.0, sine * cosine

    def turned(wave, by):
        return wave[0] * by[0] - wave[1] * by[1], wave[0] * by[1] + wave[1] * by[0]

    sites = site_ref[...]
    one = wave(sites, 1)
    two = turned(one, one)
    far = turned(wave(sites, FINE * TILE), two)
    slots = lax.broadcasted_iota(jnp.int32, (rows, lanes), 0) * lanes + lax.broadcasted_iota(jnp.int32, (rows, lanes), 1)
    live = jnp.where(slots < counts_ref[0], 1.0, 0.0)
    seen = live * obs_ref[...]
    factors = (live, *[v * live for v in two], *[v * live for v in far], *[v * seen for v in one], *wave(sites, TILE))
    for number, value in enumerate(factors):
        factor_ref[number] = value
    left, right = [], []
    for row in range(rows):
        spot = jnp.broadcast_to(site_ref[row : row + 1, :], (TILE, lanes))
        fine, coarse = wave(spot, place), wave(spot, place * FINE)
        live, *by = [jnp.broadcast_to(factor_ref[k, row : row + 1, :], (TILE, lanes)) for k in range(len(factors))]
        tiles = [(coarse[0] * live, coarse[1] * live)] + [turned(coarse, by[k : k + 2]) for k in (0, 2, 4)]
        upper = turned(fine, by[6:8])
        left.append(jnp.concatenate([tile[0] for tile in tiles] + [tile[1] for tile in tiles], axis=0))
        right.append(jnp.concatenate([fine[0], upper[0], fine[1], upper[1]], axis=0))
    left, right = jnp.concatenate(left, axis=1), jnp.concatenate(right, axis=1)
    left_high, left_low = halves(left)
    right_high, right_low = halves(right)
    beside = functools.partial(
        lax.dot_general,
        dimension_numbers=(((1,), (1,)), ((), ())),
        preferred_element_type=jnp.float32,
    )
    sums = beside(left_high, right_high) + (beside(left_high, right_low) + beside(left_low, right_high))
    tall = lax.broadcasted_iota(jnp.int32, (2 * FINE, 6 * modes), 0)
    wide = lax.broadcasted_iota(jnp.int32, (2 * FINE, 6 * modes), 1)
    picks = jnp.where(wide < 2 * modes, wide, jnp.where(wide < 4 * modes, 2 * wide, 6 * modes - wide)) & (FINE - 1)
    spread = spread_by(sums, jnp.where(tall == picks + (FINE * (wide // modes)) % (2 * FINE), 1.0, 0.0))
    half = left.shape[0] // 2
    pieces = [spread[:, number * modes : (number + 1) * modes] for number in range(6)]
    real, even_real, back_real = [pieces[number][:half] - pieces[number + 1][half:] for number in (0, 2, 4)]
    imaginary, even_imaginary, back_imaginary = [
        pieces[number][half:] + pieces[number + 1][:half] for number in (0, 2, 4)
    ]
    lane = lax.broadcasted_iota(jnp.int32, (TILE, modes), 1)
    group = lax.broadcasted_iota(jnp.int32, (TILE, modes), 0)
    keep = jnp.where(lane // FINE == group, 1.0, 0.0)
    keep_low = jnp.where(2 * lane // FINE == group, 1.0, 0.0)
    keep_back = jnp.where((modes - lane) // FINE == group, 1.0, 0.0)
    keep_high = jnp.where(2 * lane // FINE == group + TILE, 1.0, 0.0)

    def tile(value, number):
        return value[number * TILE : (number + 1) * TILE]

    def flat(value, number, keep=keep):
        return jnp.sum(tile(value, number) * keep, axis=0, keepdims=True)

    def even(value):
        return jnp.sum(tile(value, 1) * keep_low + tile(value, 2) * keep_high, axis=0, keepdims=True)

    info_scale = 1.0 / (OBS_VAR * math.sqrt(modes))
    turn_cos, turn_sin = own_cos * info_scale, own_sin * info_scale
    info_cos, info_sin = flat(real, 3), flat(imaginary, 3)
    near_cos = flat(real, 0)
    mass = (variance * level) * near_cos[:, 0:1]
    swing = (own_cos * own_cos - own_sin * own_sin) * level * even(even_real)
    swing = swing + (own_cos * own_sin) * (2.0 * level) * even(even_imaginary)
    rows = (
        near_cos, flat(imaginary, 0), flat(real, 1), flat(real, 2), flat(imaginary, 1), flat(imaginary, 2),
        turn_cos * info_cos + turn_sin * info_sin, turn_cos * info_sin - turn_sin * info_cos,
        mass + swing, mass - swing, flat(back_real, 0, keep_back), -flat(back_imaginary, 0, keep_back),
        jnp.zeros((4, modes), jnp.float32),
    )
    mine[...] = jnp.concatenate(rows, axis=0)

    pl.semaphore_wait(barrier, count - 1)
    copies = []
    for offset in range(1, count):
        copy = pltpu.make_async_remote_copy(
            src_ref=mine,
            dst_ref=held.at[offset],
            send_sem=send_sem.at[offset],
            recv_sem=recv_sem.at[offset],
            device_id={tm_axis: lax.rem(own + offset, count)},
            device_id_type=pl.DeviceIdType.MESH,
        )
        copy.start()
        copies.append(copy)
    for step in range(steps):
        for number in range(2):
            tile_ref[step, number] = jnp.broadcast_to(turn_ref[step, number : number + 1, :], (modes, modes)).T

    sub = group

    def build(at, message):
        bases = []
        for numbers in ((10, 0), (11, 1), (2, 3), (4, 5)):
            base = jnp.concatenate(
                [jnp.broadcast_to(message[number : number + 1, :], (TILE, modes)) for number in numbers], axis=1
            )
            if numbers[0] >= FINE // 2 + 2:
                base = pltpu.roll(base, 0, 1, stride=1, stride_axis=0)
                bases.append((base[:, :modes], base[:, modes:]))
            else:
                base = pltpu.roll(base, 2 * modes - TILE + 1, 1, stride=1, stride_axis=0)
                bases.append([
                    jnp.take_along_axis(base[:, k * modes : (k + 1) * modes], TILE - 1 - sub, axis=0) for k in range(2)
                ])
        cos_c, sin_c = [jnp.broadcast_to(turn_ref[at, k : k + 1, :], (TILE, modes)) for k in range(2)]
        for q in range(modes // TILE):
            shift = TILE * q
            spots = slice(shift, shift + TILE)

            def moved(low, high, edge, amount):
                value = jnp.where(lane >= edge, low, high) if edge else low
                return pltpu.roll(value, amount, 1) if amount % modes else value

            near_cos, near_sin = [
                moved(low, high, modes - shift, shift) if shift else high for low, high in bases[:2]
            ]
            far_cos, far_sin = [moved(low, high, shift, modes - shift) for low, high in bases[2:]]
            up_a, up_b = near_cos + far_cos, far_sin + near_sin
            low_a, low_b = far_sin - near_sin, near_cos - far_cos
            up_left, up_right = up_a * cos_c + up_b * sin_c, up_b * cos_c - up_a * sin_c
            low_left, low_right = low_a * cos_c + low_b * sin_c, low_b * cos_c - low_a * sin_c
            cos_t, sin_t = tile_ref[at, 0, spots, :], tile_ref[at, 1, spots, :]
            off = lane != sub + shift
            under = slice(modes + shift, modes + shift + TILE)
            fresh_ref[at, spots, :modes] = jnp.where(off, cos_t * up_left + sin_t * low_left, 0.0)
            fresh_ref[at, spots, modes:] = cos_t * up_right + sin_t * low_right
            fresh_ref[at, under, :modes] = cos_t * low_left - sin_t * up_left
            fresh_ref[at, under, modes:] = jnp.where(off, cos_t * low_right - sin_t * up_right, 0.0)

    def arrive(offset):
        pltpu.make_async_remote_copy(
            src_ref=mine,
            dst_ref=held.at[offset],
            send_sem=send_sem.at[offset],
            recv_sem=recv_sem.at[offset],
            device_id={tm_axis: lax.rem(own + offset, count)},
            device_id_type=pl.DeviceIdType.MESH,
        ).wait_recv()

    def take(offsets):
        for offset in offsets:
            arrive(offset)
        for offset in offsets:
            peer = lax.rem(own + count - offset, count)
            message = held[offset]
            sums_ref[peer] = message
            build(peer, message)

    def take_two(number, carry):
        take((count - 1 - 2 * number, count - 2 - 2 * number))
        return carry

    message = mine[...]
    sums_ref[own] = message
    build(own, message)
    lax.fori_loop(0, (count - 1) // 2, take_two, 0)
    if (count - 1) % 2:
        take((1,))
    for copy in copies:
        copy.wait_send()


def solve_kernel(
    tm_axis, rows_axis, sums_ref, turn_ref, fresh, mode_ref, mean_ref, cov_ref,
    tab, cols, line, kept, main, full, answer, spare, result,
):
    steps = sums_ref.shape[0]
    modes = sums_ref.shape[2]
    width = 2 * modes
    block = cov_ref.shape[1]
    own = lax.axis_index(tm_axis)
    block_row = lax.axis_index(rows_axis)
    links = steps - 1
    sides = (slice(0, modes), slice(modes, width))
    damp = mode_ref[0:1, :]
    damp_sq = damp * damp
    lane = lax.broadcasted_iota(jnp.int32, (TILE, modes), 1)
    sub = lax.broadcasted_iota(jnp.int32, (TILE, modes), 0)
    before = jnp.maximum(own - 1, 0)
    inverse_row, flow_row, right_row, info_row, left_row, other_row = range(6)

    def node(i):
        return own if i == links else jnp.where(own > i, i, links - (i - own))

    def load(ref, index, row):
        return tuple(ref[index, row : row + 1, side] for side in sides)

    def weights_of(at):
        return tuple(sums_ref[at, row : row + 1, :] for row in (8, 9))

    def info_of(at):
        return tuple(sums_ref[at, row : row + 1, :] for row in (6, 7))

    def note(i, row, values):
        for side, value in zip(sides, values):
            line[i, row : row + 1, side] = value

    past = None
    for i in range(links):
        at = node(i)
        inner = jnp.where(jnp.logical_or(at == 0, at == links), 0.0, 1.0)
        keep = jnp.where(own == i, 0.0, 1.0) if i else 0.0
        level = [1.0 + inner * damp_sq + mass for mass in weights_of(at)]
        if i:
            level = [value - (keep * damp_sq) * old for value, old in zip(level, past)]
        inverse = [1.0 / value for value in level]
        note(i, inverse_row, inverse)
        note(i, right_row, [(keep * damp) * value for value in inverse])
        note(i, info_row, info_of(at))
        note(i, other_row, [(keep * damp) * old for old in past] if i else [jnp.zeros_like(damp)] * 2)
        for half, value in enumerate(inverse):
            tab[2 * i + half : 2 * i + half + 1, :] = damp * value
        past = inverse
    has_left, has_right = jnp.where(own > 0, 1.0, 0.0), jnp.where(own < links, 1.0, 0.0)
    left, right = load(line, before, inverse_row), past
    level = [
        1.0 + (has_left * has_right) * damp_sq + mass - (has_left * damp_sq) * a - (has_right * damp_sq) * b
        for mass, a, b in zip(weights_of(own), left, right)
    ]
    inverse = [1.0 / value for value in level]
    note(links, inverse_row, inverse)
    note(links, right_row, [damp * value for value in inverse])
    note(links, info_row, info_of(own))
    left, right = [(has_left * damp) * value for value in left], [(has_right * damp) * value for value in right]
    note(links, left_row, left)
    note(links, other_row, right)
    for half in range(2):
        tab[2 * links + half : 2 * links + half + 1, :] = left[half]
        tab[2 * steps + half : 2 * steps + half + 1, :] = right[half]
    for chunk in range(tab.shape[0] // modes):
        cols[chunk] = tab[chunk * modes : (chunk + 1) * modes, :].T

    def col_of(at, rows):
        value = cols[at // modes, rows, at % modes : at % modes + 1]
        return jnp.broadcast_to(value, (rows.stop - rows.start, modes))

    pair = 2 * TILE
    strips = [
        (half, slice(start, start + pair), slice(half * modes + start, half * modes + start + pair))
        for half in range(2) for start in range(0, modes, pair)
    ]
    pair_lane = lax.broadcasted_iota(jnp.int32, (pair, modes), 1)
    pair_sub = lax.broadcasted_iota(jnp.int32, (pair, modes), 0)
    ones = jnp.ones((TILE, width), jnp.bfloat16)

    def flow(i, state, third):
        sums = [jnp.zeros((pair, modes), jnp.float32) for _ in sides]
        for half, part, rows in strips:
            parts = []
            for k, side in enumerate(sides):
                value = main[i, rows, side] + third[rows, side]
                full[i, rows, side] = value
                parts.append(value * state[k])
            column = jnp.sum(parts[0] + parts[1], axis=1, keepdims=True)
            sums[half] += jnp.where(pair_lane == pair_sub + part.start, column, 0.0)
        moved = [value - jnp.sum(total, axis=0, keepdims=True) for value, total in zip(state, sums)]
        note(i, flow_row, moved)
        return moved

    def packed(whole):
        return jnp.concatenate([jnp.concatenate(values, axis=1) for values in whole], axis=0).astype(jnp.bfloat16)

    third, state, most = None, None, jnp.zeros((TILE, width), jnp.float32)
    for i in range(links):
        scales, rights = load(line, i, inverse_row), load(line, i, right_row)
        downs = [col_of(2 * (i - 1) + half, part) for half, part, rows in strips] if i else [None] * len(strips)
        whole = []
        for (half, part, rows), down in zip(strips, downs):
            values = []
            for side, scale, right in zip(sides, scales, rights):
                value = fresh[node(i), rows, side] * scale
                if i:
                    value = value + down * (main[i - 1, rows, side] * right)
                kept[i % 2, rows, side] = value
                values.append(value)
            whole.append(values)
        narrow = packed(whole)
        square = dot(narrow, narrow)
        if i:
            moved = flow(i - 1, state, third)
            state = [a + b * c for a, b, c in zip(load(line, i, info_row), load(line, i, other_row), moved)]
        else:
            state = load(line, i, info_row)
        for (half, part, rows), down in zip(strips, downs):
            for side, right in zip(sides, rights):
                value = kept[i % 2, rows, side] - square[rows, side]
                if i:
                    value = value + down * (third[rows, side] * right)
                main[i, rows, side] = value
        squared = square.astype(jnp.bfloat16)
        third = dot(squared, narrow)
        most = jnp.maximum(most, dot(ones, jnp.abs(squared)))
    flow(links - 1, state, third)

    height = block + pair
    tall = lax.broadcasted_iota(jnp.int32, (block, modes), 0)
    wide = lax.broadcasted_iota(jnp.int32, (block, modes), 1)
    hit = wide == (tall + block_row * block) // 2
    even = tall % 2 == 0
    cosines, sines = turn_ref[own, 2:3, :], turn_ref[own, 3:4, :]

    def pose():
        state = [
            a + b * c + d * e
            for a, b, c, d, e in zip(
                load(line, links, info_row), load(line, links, left_row), load(line, before, flow_row),
                load(line, links, other_row), load(line, links - 1, flow_row),
            )
        ]
        scales = load(line, links, inverse_row)
        spare[:block, sides[0]] = jnp.where(hit, jnp.where(even, cosines, sines) * scales[0], 0.0)
        spare[:block, sides[1]] = jnp.where(hit, jnp.where(even, -sines, cosines) * scales[1], 0.0)
        for side, value, scale in zip(sides, state, scales):
            spare[block:, side] = jnp.where(pair_sub == 0, value * scale, 0.0)

    def product(left, right):
        return dot(left[0], right[0]) + (dot(left[0], right[1]) + dot(left[1], right[0]))

    whole = []
    scales, rights = load(line, links, inverse_row), load(line, links, right_row)
    for half, part, rows in strips:
        first, second = col_of(2 * links + half, part), col_of(2 * steps + half, part)
        whole.append([
            fresh[own, rows, side] * scale + (first * full[before, rows, side] + second * full[links - 1, rows, side]) * right
            for side, scale, right in zip(sides, scales, rights)
        ])
    whole = halves(jnp.concatenate([jnp.concatenate(values, axis=1) for values in whole], axis=0))
    pose()
    asked = spare[...]
    first = product(halves(asked), whole)
    square = dot(whole[0], whole[0]).astype(jnp.bfloat16)
    second = product(halves(first), whole)
    fourth = dot(square, square).astype(jnp.bfloat16)
    third = dot(second.astype(jnp.bfloat16), whole[0])
    last = dot(ones, jnp.abs(fourth))
    reached = (asked - first) + (second - third)
    answer[...] = reached + dot(reached.astype(jnp.bfloat16), fourth)
    good = jnp.logical_and(jnp.max(most) <= CHAIN_BOUND, jnp.max(last) <= LAST_BOUND)

    @pl.when(jnp.logical_not(good))
    def _():
        rows = lax.broadcasted_iota(jnp.int32, (width, width), 0)
        unit = rows == lax.broadcasted_iota(jnp.int32, (width, width), 1)
        source, target = result.at[0], result.at[1]

        def column(row):
            return jnp.sum(jnp.where(unit, row, 0.0), axis=1, keepdims=True)

        def invert(low):
            high = 1.001 * jnp.max(jnp.sum(jnp.abs(source[...]), axis=0, keepdims=True))
            low = jnp.minimum(low, 0.5 * high)
            center = (high + low) / (high - low)
            slope = 2.0 / (high - low)
            top = 2.0 * center * center - 1.0
            target[...] = jnp.where(unit, 4.0 * center * slope / top, 0.0) - (2.0 * slope * slope / top) * source[...]

            def improve(radius):
                factor = 2.0 / (2.0 - radius * radius)
                residue = jnp.where(unit, 1.0, 0.0) - exact(source[...], target[...])
                target[...] = factor * (target[...] + exact(target[...], residue))
                return radius * radius / (2.0 - radius * radius)

            lax.while_loop(lambda radius: radius > TOLERANCE, improve, 1.0 / top)

        def even_out(i, whole):
            root = jnp.sqrt(line[i, inverse_row : inverse_row + 1, :])
            source[...] = jnp.where(unit, 1.0, 0.0) + column(root) * whole * (1.0 / root)
            return root, column(root)

        full[0] = jnp.zeros((width, width), jnp.float32)
        note(0, flow_row, [jnp.zeros_like(damp)] * 2)

        def advance(i, carry):
            old = jnp.maximum(i - 1, 0)
            down = column(line[old, inverse_row : inverse_row + 1, :] * jnp.concatenate([damp, damp], axis=1))
            at = jnp.where(own > i, i, links - (i - own))
            plain = fresh[at] * line[i, inverse_row : inverse_row + 1, :]
            root, root_col = even_out(i, plain + down * full[old] * line[i, right_row : right_row + 1, :])
            invert(0.999 * jnp.min(root * root))
            state = line[i, info_row : info_row + 1, :]
            state = state + line[i, other_row : other_row + 1, :] * line[old, flow_row : flow_row + 1, :]
            scaled = jnp.broadcast_to(state * root, (TILE, width))
            line[i, flow_row : flow_row + 1, :] = exact(scaled, target[...])[0:1] * (1.0 / root)
            full[i] = (1.0 / root_col) * (jnp.where(unit, 1.0, 0.0) - target[...]) * root
            return carry

        lax.fori_loop(0, links, advance, 0)
        root, root_col = even_out(
            links,
            fresh[own] * line[links, inverse_row : inverse_row + 1, :] + (
                column(line[links, left_row : left_row + 1, :]) * full[before]
                + column(line[links, other_row : other_row + 1, :]) * full[links - 1]
            ) * line[links, right_row : right_row + 1, :],
        )
        invert(0.999 * jnp.min(1.0 - damp_sq) * jnp.min(root * root))
        pose()
        answer[...] = exact(spare[...] * (1.0 / root), target[...]) * root

    left, right = answer[:, sides[0]], answer[:, sides[1]]
    left, right = left * cosines - right * sines, left * sines + right * cosines
    wide = lax.broadcasted_iota(jnp.int32, (height, modes), 1)
    out = []
    for number in range(2):
        pick = wide // 2 + number * (modes // 2)
        out.append(
            jnp.where(wide % 2 == 0, jnp.take_along_axis(left, pick, axis=1), jnp.take_along_axis(right, pick, axis=1))
        )
    for side, value in zip(sides, out):
        cov_ref[0, :, side] = value[:block]
    means = jnp.concatenate([value[block : block + TILE] for value in out], axis=1)
    mean_ref[...] = pltpu.roll(means, width - block_row * block, 1)[0:1, :block]


def local(observations, site_ids, counts, frequencies, decay, proc_var):
    modes = frequencies.shape[0]
    width = 2 * modes
    count = lax.axis_size("tm")
    steps = count * observations.shape[0]
    block = width // lax.axis_size("rows")
    height = block + 2 * TILE
    dense = (site_ids.shape[1] // LANES, LANES)
    table = -(-(2 * steps + 2) // modes) * modes
    vmem = pl.BlockSpec(memory_space=pltpu.VMEM)
    smem = pl.BlockSpec(memory_space=pltpu.SMEM)
    hbm = pl.BlockSpec(memory_space=pltpu.HBM)
    shared = pl.pallas_call(
        functools.partial(share_kernel, "tm"),
        out_shape=(
            jax.ShapeDtypeStruct((steps, 2 * TILE, modes), jnp.float32),
            jax.ShapeDtypeStruct((steps, 8, modes), jnp.float32),
            jax.ShapeDtypeStruct((steps, width, width), jnp.float32),
            jax.ShapeDtypeStruct((8, modes), jnp.float32),
        ),
        in_specs=[smem] + [hbm] * 5,
        out_specs=(vmem,) * 4,
        scratch_shapes=[
            pltpu.VMEM(dense, jnp.int32),
            pltpu.VMEM(dense, jnp.float32),
            pltpu.VMEM((1, modes), jnp.float32),
            pltpu.VMEM((1, modes), jnp.float32),
            pltpu.VMEM((1, modes), jnp.float32),
            pltpu.VMEM((steps, 2, modes, modes), jnp.float32),
            pltpu.VMEM((9, *dense), jnp.float32),
            pltpu.VMEM((2 * TILE, modes), jnp.float32),
            pltpu.VMEM((count, 2 * TILE, modes), jnp.float32),
            pltpu.SemaphoreType.DMA((5,)),
            pltpu.SemaphoreType.DMA((count,)),
            pltpu.SemaphoreType.DMA((count,)),
        ],
        compiler_params=pltpu.CompilerParams(collective_id=0, has_side_effects=True, vmem_limit_bytes=16 << 20),
        name="share",
    )(
        counts,
        *(
            pltpu.with_memory_space_constraint(value, pltpu.HBM)
            for value in (site_ids.reshape(dense), observations.reshape(dense), frequencies[None], decay[None], proc_var[None])
        ),
    )
    return pl.pallas_call(
        functools.partial(solve_kernel, "tm", "rows"),
        out_shape=(
            jax.ShapeDtypeStruct((1, block), jnp.float32),
            jax.ShapeDtypeStruct((1, block, width), jnp.float32),
        ),
        in_specs=[vmem] * 4,
        out_specs=(vmem, vmem),
        scratch_shapes=[
            pltpu.VMEM((table, modes), jnp.float32),
            pltpu.VMEM((table // modes, modes, modes), jnp.float32),
            pltpu.VMEM((steps, 8, width), jnp.float32),
            pltpu.VMEM((2, width, width), jnp.float32),
            pltpu.VMEM((steps - 1, width, width), jnp.float32),
            pltpu.VMEM((steps - 1, width, width), jnp.float32),
            pltpu.VMEM((height, width), jnp.float32),
            pltpu.VMEM((height, width), jnp.float32),
            pltpu.VMEM((2, width, width), jnp.float32),
        ],
        compiler_params=pltpu.CompilerParams(vmem_limit_bytes=40 << 20),
        name="solve",
    )(*shared)


def solution(mesh):
    return jax.shard_map(
        local,
        mesh=mesh,
        in_specs=(P("tm", None), P("tm", None), P("tm"), P(), P(), P()),
        out_specs=(P("tm", "rows"), P("tm", "rows", None)),
        check_vma=False,
    )
```

```python
import functools
import math

import jax
import jax.numpy as jnp
from jax import lax
from jax.experimental import pallas as pl
from jax.experimental.pallas import tpu as pltpu
from jax.sharding import PartitionSpec as P

GRID = 4096
OBS_VAR = 64
FINE = 16
TILE = 8
LANES = 128
CHAIN_BOUND = 2.5e-3
LAST_BOUND = 5e-3
TOLERANCE = 1e-6
HALF_UNIT = math.pi / GRID
HALF_SINE = tuple(-2.0 * c * HALF_UNIT ** (2 * k + 1) for k, c in enumerate((
    0.9999999766, -0.1666664763, 0.008332899823, -0.0001980089775, 2.590488469e-06
)))
HALF_COSINE = tuple(c * HALF_UNIT ** (2 * k) for k, c in enumerate((
    0.9999999535, -0.4999990535, 0.04166358469, -0.001385370429, 2.315393125e-05
)))

exact_mode = lax.Precision.HIGHEST


def exact(left, right):
    return jnp.dot(left, right, precision=exact_mode, preferred_element_type=jnp.float32)


dot = functools.partial(jnp.dot, preferred_element_type=jnp.float32)


def halves(value):
    high = value.astype(jnp.bfloat16)
    return high, (value - high.astype(jnp.float32)).astype(jnp.bfloat16)


def spread_by(value, picks):
    high, low = halves(value)
    picks = picks.astype(jnp.bfloat16)
    return dot(high, picks) + dot(low, picks)


def circle(angle):
    square = angle * angle
    cosine = 1.0 / 40320.0 - square * (1.0 / 3628800.0)
    cosine = 1.0 - square * (0.5 - square * (1.0 / 24.0 - square * (1.0 / 720.0 - square * cosine)))
    sine = 1.0 / 5040.0 - square * (1.0 / 362880.0)
    sine = angle * (1.0 - square * (1.0 / 6.0 - square * (1.0 / 120.0 - square * sine)))
    return cosine, sine


def quarter_turn(quadrant, cosine, sine):
    odd = (quadrant & 1) == 1
    new_cosine = jnp.where(odd, sine, cosine)
    new_sine = jnp.where(odd, cosine, sine)
    new_cosine = jnp.where(((quadrant + 1) & 2) == 2, -new_cosine, new_cosine)
    new_sine = jnp.where((quadrant & 2) == 2, -new_sine, new_sine)
    return new_cosine, new_sine


def share_kernel(
    tm_axis, counts_ref, site_hbm, obs_hbm, freq_hbm, decay_hbm, var_hbm,
    sums_ref, turn_ref, fresh_ref, mode_ref, site_ref, obs_ref, freq_ref, decay_ref, var_ref,
    tile_ref, factor_ref, mine, held, load_sem, send_sem, recv_sem,
):
    count = lax.axis_size(tm_axis)
    own = lax.axis_index(tm_axis)
    modes = freq_ref.shape[1]
    steps = sums_ref.shape[0]
    loads = [
        pltpu.make_async_copy(source, target, load_sem.at[number])
        for number, (source, target) in enumerate((
            (site_hbm, site_ref), (obs_hbm, obs_ref), (freq_hbm, freq_ref), (var_hbm, var_ref), (decay_hbm, decay_ref),
        ))
    ]
    for load in loads:
        load.start()
    barrier = pltpu.get_barrier_semaphore()
    for offset in range(1, count):
        pl.semaphore_signal(
            barrier, inc=1, device_id={tm_axis: lax.rem(own + offset, count)},
            device_id_type=pl.DeviceIdType.MESH,
        )
    for load in loads:
        load.wait()

    frequency = freq_ref[...]
    turns = jnp.where(jnp.abs(frequency) > 0.25 * math.pi, 1, 0) + jnp.where(
        jnp.abs(frequency) > 0.75 * math.pi, 1, 0
    )
    turns = jnp.where(frequency < 0.0, -turns, turns)
    share = turns.astype(jnp.float32)
    reduced = (frequency - share * 1.5703125) - share * (0.5 * math.pi - 1.5703125)
    turn_cosine, turn_sine = quarter_turn(turns + 4, *circle(reduced))
    level = 0.5 / (OBS_VAR * modes)
    root = math.sqrt(level)
    variance = var_ref[...]
    mode_ref[0:1, :] = jnp.exp(-decay_ref[...])
    now_cos = jnp.sqrt(variance)
    now_sin = jnp.zeros_like(now_cos)
    own_cos, own_sin = now_cos, now_sin
    for step in range(steps):
        for number, value in enumerate((now_cos * root, now_sin * root, now_cos, now_sin)):
            turn_ref[step, number : number + 1, :] = value
        own_cos = jnp.where(own == step, now_cos, own_cos)
        own_sin = jnp.where(own == step, now_sin, own_sin)
        now_cos, now_sin = (
            now_cos * turn_cosine - now_sin * turn_sine, now_cos * turn_sine + now_sin * turn_cosine
        )

    rows, lanes = site_ref.shape
    half_turn = GRID // 2
    place = lax.broadcasted_iota(jnp.int32, (TILE, lanes), 0)

    def wave(sites, exponent):
        at = ((exponent * sites) & (GRID - 1)).astype(jnp.float32) - half_turn
        square = at * at
        sine, cosine = HALF_SINE[-1], HALF_COSINE[-1]
        for a in HALF_SINE[-2::-1]:
            sine = sine * square + a
        for a in HALF_COSINE[-2::-1]:
            cosine = cosine * square + a
        sine = sine * at
        return (sine * sine) * 0.5 - 1.0, sine * cosine

    def turned(wave, by):
        return wave[0] * by[0] - wave[1] * by[1], wave[0] * by[1] + wave[1] * by[0]

    sites = site_ref[...]
    one = wave(sites, 1)
    two = turned(one, one)
    far = turned(wave(sites, FINE * TILE), two)
    slots = lax.broadcasted_iota(jnp.int32, (rows, lanes), 0) * lanes + lax.broadcasted_iota(jnp.int32, (rows, lanes), 1)
    live = jnp.where(slots < counts_ref[0], 1.0, 0.0)
    seen = live * obs_ref[...]
    factors = (live, *[v * live for v in two], *[v * live for v in far], *[v * seen for v in one], *wave(sites, TILE))
    for number, value in enumerate(factors):
        factor_ref[number] = value
    left, right = [], []
    for row in range(rows):
        spot = jnp.broadcast_to(site_ref[row : row + 1, :], (TILE, lanes))
        fine, coarse = wave(spot, place), wave(spot, place * FINE)
        live, *by = [jnp.broadcast_to(factor_ref[k, row : row + 1, :], (TILE, lanes)) for k in range(len(factors))]
        tiles = [(coarse[0] * live, coarse[1] * live)] + [turned(coarse, by[k : k + 2]) for k in (0, 2, 4)]
        upper = turned(fine, by[6:8])
        left.append(jnp.concatenate([tile[0] for tile in tiles] + [tile[1] for tile in tiles], axis=0))
        right.append(jnp.concatenate([fine[0], upper[0], fine[1], upper[1]], axis=0))
    left, right = jnp.concatenate(left, axis=1), jnp.concatenate(right, axis=1)
    left_high, left_low = halves(left)
    right_high, right_low = halves(right)
    beside = functools.partial(
        lax.dot_general,
        dimension_numbers=(((1,), (1,)), ((), ())),
        preferred_element_type=jnp.float32,
    )
    sums = beside(left_high, right_high) + (beside(left_high, right_low) + beside(left_low, right_high))
    tall = lax.broadcasted_iota(jnp.int32, (2 * FINE, 6 * modes), 0)
    wide = lax.broadcasted_iota(jnp.int32, (2 * FINE, 6 * modes), 1)
    picks = jnp.where(wide < 2 * modes, wide, jnp.where(wide < 4 * modes, 2 * wide, 6 * modes - wide)) & (FINE - 1)
    spread = spread_by(sums, jnp.where(tall == picks + (FINE * (wide // modes)) % (2 * FINE), 1.0, 0.0))
    half = left.shape[0] // 2
    pieces = [spread[:, number * modes : (number + 1) * modes] for number in range(6)]
    real, even_real, back_real = [pieces[number][:half] - pieces[number + 1][half:] for number in (0, 2, 4)]
    imaginary, even_imaginary, back_imaginary = [
        pieces[number][half:] + pieces[number + 1][:half] for number in (0, 2, 4)
    ]
    lane = lax.broadcasted_iota(jnp.int32, (TILE, modes), 1)
    group = lax.broadcasted_iota(jnp.int32, (TILE, modes), 0)
    keep = jnp.where(lane // FINE == group, 1.0, 0.0)
    keep_low = jnp.where(2 * lane // FINE == group, 1.0, 0.0)
    keep_back = jnp.where((modes - lane) // FINE == group, 1.0, 0.0)
    keep_high = jnp.where(2 * lane // FINE == group + TILE, 1.0, 0.0)

    def tile(value, number):
        return value[number * TILE : (number + 1) * TILE]

    def flat(value, number, keep=keep):
        return jnp.sum(tile(value, number) * keep, axis=0, keepdims=True)

    def even(value):
        return jnp.sum(tile(value, 1) * keep_low + tile(value, 2) * keep_high, axis=0, keepdims=True)

    info_scale = 1.0 / (OBS_VAR * math.sqrt(modes))
    turn_cos, turn_sin = own_cos * info_scale, own_sin * info_scale
    info_cos, info_sin = flat(real, 3), flat(imaginary, 3)
    near_cos = flat(real, 0)
    mass = (variance * level) * near_cos[:, 0:1]
    swing = (own_cos * own_cos - own_sin * own_sin) * level * even(even_real)
    swing = swing + (own_cos * own_sin) * (2.0 * level) * even(even_imaginary)
    rows = (
        near_cos, flat(imaginary, 0), flat(real, 1), flat(real, 2), flat(imaginary, 1), flat(imaginary, 2),
        turn_cos * info_cos + turn_sin * info_sin, turn_cos * info_sin - turn_sin * info_cos,
        mass + swing, mass - swing, flat(back_real, 0, keep_back), -flat(back_imaginary, 0, keep_back),
        jnp.zeros((4, modes), jnp.float32),
    )
    mine[...] = jnp.concatenate(rows, axis=0)

    pl.semaphore_wait(barrier, count - 1)
    copies = []
    for offset in range(1, count):
        copy = pltpu.make_async_remote_copy(
            src_ref=mine,
            dst_ref=held.at[offset],
            send_sem=send_sem.at[offset],
            recv_sem=recv_sem.at[offset],
            device_id={tm_axis: lax.rem(own + offset, count)},
            device_id_type=pl.DeviceIdType.MESH,
        )
        copy.start()
        copies.append(copy)
    for step in range(steps):
        for number in range(2):
            tile_ref[step, number] = jnp.broadcast_to(turn_ref[step, number : number + 1, :], (modes, modes)).T

    sub = group

    def build(at, message):
        bases = []
        for numbers in ((10, 0), (11, 1), (2, 3), (4, 5)):
            base = jnp.concatenate(
                [jnp.broadcast_to(message[number : number + 1, :], (TILE, modes)) for number in numbers], axis=1
            )
            if numbers[0] >= FINE // 2 + 2:
                base = pltpu.roll(base, 0, 1, stride=1, stride_axis=0)
                bases.append((base[:, :modes], base[:, modes:]))
            else:
                base = pltpu.roll(base, 2 * modes - TILE + 1, 1, stride=1, stride_axis=0)
                bases.append([
                    jnp.take_along_axis(base[:, k * modes : (k + 1) * modes], TILE - 1 - sub, axis=0) for k in range(2)
                ])
        cos_c, sin_c = [jnp.broadcast_to(turn_ref[at, k : k + 1, :], (TILE, modes)) for k in range(2)]
        for q in range(modes // TILE):
            shift = TILE * q
            spots = slice(shift, shift + TILE)

            def moved(low, high, edge, amount):
                value = jnp.where(lane >= edge, low, high) if edge else low
                return pltpu.roll(value, amount, 1) if amount % modes else value

            near_cos, near_sin = [
                moved(low, high, modes - shift, shift) if shift else high for low, high in bases[:2]
            ]
            far_cos, far_sin = [moved(low, high, shift, modes - shift) for low, high in bases[2:]]
            up_a, up_b = near_cos + far_cos, far_sin + near_sin
            low_a, low_b = far_sin - near_sin, near_cos - far_cos
            up_left, up_right = up_a * cos_c + up_b * sin_c, up_b * cos_c - up_a * sin_c
            low_left, low_right = low_a * cos_c + low_b * sin_c, low_b * cos_c - low_a * sin_c
            cos_t, sin_t = tile_ref[at, 0, spots, :], tile_ref[at, 1, spots, :]
            off = lane != sub + shift
            under = slice(modes + shift, modes + shift + TILE)
            fresh_ref[at, spots, :modes] = jnp.where(off, cos_t * up_left + sin_t * low_left, 0.0)
            fresh_ref[at, spots, modes:] = cos_t * up_right + sin_t * low_right
            fresh_ref[at, under, :modes] = cos_t * low_left - sin_t * up_left
            fresh_ref[at, under, modes:] = jnp.where(off, cos_t * low_right - sin_t * up_right, 0.0)

    def arrive(offset):
        pltpu.make_async_remote_copy(
            src_ref=mine,
            dst_ref=held.at[offset],
            send_sem=send_sem.at[offset],
            recv_sem=recv_sem.at[offset],
            device_id={tm_axis: lax.rem(own + offset, count)},
            device_id_type=pl.DeviceIdType.MESH,
        ).wait_recv()

    def take(offsets):
        for offset in offsets:
            arrive(offset)
        for offset in offsets:
            peer = lax.rem(own + count - offset, count)
            message = held[offset]
            sums_ref[peer] = message
            build(peer, message)

    def take_two(number, carry):
        take((count - 1 - 2 * number, count - 2 - 2 * number))
        return carry

    message = mine[...]
    sums_ref[own] = message
    build(own, message)
    lax.fori_loop(0, (count - 1) // 2, take_two, 0)
    if (count - 1) % 2:
        take((1,))
    for copy in copies:
        copy.wait_send()


def solve_kernel(
    tm_axis, rows_axis, sums_ref, turn_ref, fresh, mode_ref, mean_ref, cov_ref,
    tab, cols, line, kept, main, full, answer, spare, result,
):
    steps = sums_ref.shape[0]
    modes = sums_ref.shape[2]
    width = 2 * modes
    block = cov_ref.shape[1]
    own = lax.axis_index(tm_axis)
    block_row = lax.axis_index(rows_axis)
    links = steps - 1
    sides = (slice(0, modes), slice(modes, width))
    damp = mode_ref[0:1, :]
    damp_sq = damp * damp
    lane = lax.broadcasted_iota(jnp.int32, (TILE, modes), 1)
    sub = lax.broadcasted_iota(jnp.int32, (TILE, modes), 0)
    before = jnp.maximum(own - 1, 0)
    inverse_row, flow_row, right_row, info_row, left_row, other_row = range(6)

    def node(i):
        return own if i == links else jnp.where(own > i, i, links - (i - own))

    def load(ref, index, row):
        return tuple(ref[index, row : row + 1, side] for side in sides)

    def weights_of(at):
        return tuple(sums_ref[at, row : row + 1, :] for row in (8, 9))

    def info_of(at):
        return tuple(sums_ref[at, row : row + 1, :] for row in (6, 7))

    def note(i, row, values):
        for side, value in zip(sides, values):
            line[i, row : row + 1, side] = value

    past = None
    for i in range(links):
        at = node(i)
        inner = jnp.where(jnp.logical_or(at == 0, at == links), 0.0, 1.0)
        keep = jnp.where(own == i, 0.0, 1.0) if i else 0.0
        level = [1.0 + inner * damp_sq + mass for mass in weights_of(at)]
        if i:
            level = [value - (keep * damp_sq) * old for value, old in zip(level, past)]
        inverse = [1.0 / value for value in level]
        note(i, inverse_row, inverse)
        note(i, right_row, [(keep * damp) * value for value in inverse])
        note(i, info_row, info_of(at))
        note(i, other_row, [(keep * damp) * old for old in past] if i else [jnp.zeros_like(damp)] * 2)
        for half, value in enumerate(inverse):
            tab[2 * i + half : 2 * i + half + 1, :] = damp * value
        past = inverse
    has_left, has_right = jnp.where(own > 0, 1.0, 0.0), jnp.where(own < links, 1.0, 0.0)
    left, right = load(line, before, inverse_row), past
    level = [
        1.0 + (has_left * has_right) * damp_sq + mass - (has_left * damp_sq) * a - (has_right * damp_sq) * b
        for mass, a, b in zip(weights_of(own), left, right)
    ]
    inverse = [1.0 / value for value in level]
    note(links, inverse_row, inverse)
    note(links, right_row, [damp * value for value in inverse])
    note(links, info_row, info_of(own))
    left, right = [(has_left * damp) * value for value in left], [(has_right * damp) * value for value in right]
    note(links, left_row, left)
    note(links, other_row, right)
    for half in range(2):
        tab[2 * links + half : 2 * links + half + 1, :] = left[half]
        tab[2 * steps + half : 2 * steps + half + 1, :] = right[half]
    for chunk in range(tab.shape[0] // modes):
        cols[chunk] = tab[chunk * modes : (chunk + 1) * modes, :].T

    def col_of(at, rows):
        value = cols[at // modes, rows, at % modes : at % modes + 1]
        return jnp.broadcast_to(value, (rows.stop - rows.start, modes))

    pair = 2 * TILE
    strips = [
        (half, slice(start, start + pair), slice(half * modes + start, half * modes + start + pair))
        for half in range(2) for start in range(0, modes, pair)
    ]
    pair_lane = lax.broadcasted_iota(jnp.int32, (pair, modes), 1)
    pair_sub = lax.broadcasted_iota(jnp.int32, (pair, modes), 0)
    ones = jnp.ones((TILE, width), jnp.bfloat16)

    def flow(i, state, third):
        sums = [jnp.zeros((pair, modes), jnp.float32) for _ in sides]
        for half, part, rows in strips:
            parts = []
            for k, side in enumerate(sides):
                value = main[i, rows, side] + third[rows, side]
                full[i, rows, side] = value
                parts.append(value * state[k])
            column = jnp.sum(parts[0] + parts[1], axis=1, keepdims=True)
            sums[half] += jnp.where(pair_lane == pair_sub + part.start, column, 0.0)
        moved = [value - jnp.sum(total, axis=0, keepdims=True) for value, total in zip(state, sums)]
        note(i, flow_row, moved)
        return moved

    def packed(whole):
        return jnp.concatenate([jnp.concatenate(values, axis=1) for values in whole], axis=0).astype(jnp.bfloat16)

    third, state, most = None, None, jnp.zeros((TILE, width), jnp.float32)
    for i in range(links):
        scales, rights = load(line, i, inverse_row), load(line, i, right_row)
        downs = [col_of(2 * (i - 1) + half, part) for half, part, rows in strips] if i else [None] * len(strips)
        whole = []
        for (half, part, rows), down in zip(strips, downs):
            values = []
            for side, scale, right in zip(sides, scales, rights):
                value = fresh[node(i), rows, side] * scale
                if i:
                    value = value + down * (main[i - 1, rows, side] * right)
                kept[i % 2, rows, side] = value
                values.append(value)
            whole.append(values)
        narrow = packed(whole)
        square = dot(narrow, narrow)
        if i:
            moved = flow(i - 1, state, third)
            state = [a + b * c for a, b, c in zip(load(line, i, info_row), load(line, i, other_row), moved)]
        else:
            state = load(line, i, info_row)
        for (half, part, rows), down in zip(strips, downs):
            for side, right in zip(sides, rights):
                value = kept[i % 2, rows, side] - square[rows, side]
                if i:
                    value = value + down * (third[rows, side] * right)
                main[i, rows, side] = value
        squared = square.astype(jnp.bfloat16)
        third = dot(squared, narrow)
        most = jnp.maximum(most, dot(ones, jnp.abs(squared)))
    flow(links - 1, state, third)

    height = block + pair
    tall = lax.broadcasted_iota(jnp.int32, (block, modes), 0)
    wide = lax.broadcasted_iota(jnp.int32, (block, modes), 1)
    hit = wide == (tall + block_row * block) // 2
    even = tall % 2 == 0
    cosines, sines = turn_ref[own, 2:3, :], turn_ref[own, 3:4, :]

    def pose():
        state = [
            a + b * c + d * e
            for a, b, c, d, e in zip(
                load(line, links, info_row), load(line, links, left_row), load(line, before, flow_row),
                load(line, links, other_row), load(line, links - 1, flow_row),
            )
        ]
        scales = load(line, links, inverse_row)
        spare[:block, sides[0]] = jnp.where(hit, jnp.where(even, cosines, sines) * scales[0], 0.0)
        spare[:block, sides[1]] = jnp.where(hit, jnp.where(even, -sines, cosines) * scales[1], 0.0)
        for side, value, scale in zip(sides, state, scales):
            spare[block:, side] = jnp.where(pair_sub == 0, value * scale, 0.0)

    def product(left, right):
        return dot(left[0], right[0]) + (dot(left[0], right[1]) + dot(left[1], right[0]))

    whole = []
    scales, rights = load(line, links, inverse_row), load(line, links, right_row)
    for half, part, rows in strips:
        first, second = col_of(2 * links + half, part), col_of(2 * steps + half, part)
        whole.append([
            fresh[own, rows, side] * scale + (first * full[before, rows, side] + second * full[links - 1, rows, side]) * right
            for side, scale, right in zip(sides, scales, rights)
        ])
    whole = halves(jnp.concatenate([jnp.concatenate(values, axis=1) for values in whole], axis=0))
    square = dot(whole[0], whole[0]).astype(jnp.bfloat16)
    pose()
    asked = spare[...]
    first = product(halves(asked), whole)
    second = product(halves(first), whole)
    fourth = dot(square, square).astype(jnp.bfloat16)
    third = dot(second.astype(jnp.bfloat16), whole[0])
    last = dot(ones, jnp.abs(fourth))
    reached = (asked - first) + (second - third)
    answer[...] = reached + dot(reached.astype(jnp.bfloat16), fourth)
    good = jnp.logical_and(jnp.max(most) <= CHAIN_BOUND, jnp.max(last) <= LAST_BOUND)

    @pl.when(jnp.logical_not(good))
    def _():
        rows = lax.broadcasted_iota(jnp.int32, (width, width), 0)
        unit = rows == lax.broadcasted_iota(jnp.int32, (width, width), 1)
        source, target = result.at[0], result.at[1]

        def column(row):
            return jnp.sum(jnp.where(unit, row, 0.0), axis=1, keepdims=True)

        def invert(low):
            high = 1.001 * jnp.max(jnp.sum(jnp.abs(source[...]), axis=0, keepdims=True))
            low = jnp.minimum(low, 0.5 * high)
            center = (high + low) / (high - low)
            slope = 2.0 / (high - low)
            top = 2.0 * center * center - 1.0
            target[...] = jnp.where(unit, 4.0 * center * slope / top, 0.0) - (2.0 * slope * slope / top) * source[...]

            def improve(radius):
                factor = 2.0 / (2.0 - radius * radius)
                residue = jnp.where(unit, 1.0, 0.0) - exact(source[...], target[...])
                target[...] = factor * (target[...] + exact(target[...], residue))
                return radius * radius / (2.0 - radius * radius)

            lax.while_loop(lambda radius: radius > TOLERANCE, improve, 1.0 / top)

        def even_out(i, whole):
            root = jnp.sqrt(line[i, inverse_row : inverse_row + 1, :])
            source[...] = jnp.where(unit, 1.0, 0.0) + column(root) * whole * (1.0 / root)
            return root, column(root)

        full[0] = jnp.zeros((width, width), jnp.float32)
        note(0, flow_row, [jnp.zeros_like(damp)] * 2)

        def advance(i, carry):
            old = jnp.maximum(i - 1, 0)
            down = column(line[old, inverse_row : inverse_row + 1, :] * jnp.concatenate([damp, damp], axis=1))
            at = jnp.where(own > i, i, links - (i - own))
            plain = fresh[at] * line[i, inverse_row : inverse_row + 1, :]
            root, root_col = even_out(i, plain + down * full[old] * line[i, right_row : right_row + 1, :])
            invert(0.999 * jnp.min(root * root))
            state = line[i, info_row : info_row + 1, :]
            state = state + line[i, other_row : other_row + 1, :] * line[old, flow_row : flow_row + 1, :]
            scaled = jnp.broadcast_to(state * root, (TILE, width))
            line[i, flow_row : flow_row + 1, :] = exact(scaled, target[...])[0:1] * (1.0 / root)
            full[i] = (1.0 / root_col) * (jnp.where(unit, 1.0, 0.0) - target[...]) * root
            return carry

        lax.fori_loop(0, links, advance, 0)
        root, root_col = even_out(
            links,
            fresh[own] * line[links, inverse_row : inverse_row + 1, :] + (
                column(line[links, left_row : left_row + 1, :]) * full[before]
                + column(line[links, other_row : other_row + 1, :]) * full[links - 1]
            ) * line[links, right_row : right_row + 1, :],
        )
        invert(0.999 * jnp.min(1.0 - damp_sq) * jnp.min(root * root))
        pose()
        answer[...] = exact(spare[...] * (1.0 / root), target[...]) * root

    left, right = answer[:, sides[0]], answer[:, sides[1]]
    left, right = left * cosines - right * sines, left * sines + right * cosines
    wide = lax.broadcasted_iota(jnp.int32, (height, modes), 1)
    out = []
    for number in range(2):
        pick = wide // 2 + number * (modes // 2)
        out.append(
            jnp.where(wide % 2 == 0, jnp.take_along_axis(left, pick, axis=1), jnp.take_along_axis(right, pick, axis=1))
        )
    for side, value in zip(sides, out):
        cov_ref[0, :, side] = value[:block]
    means = jnp.concatenate([value[block : block + TILE] for value in out], axis=1)
    mean_ref[...] = pltpu.roll(means, width - block_row * block, 1)[0:1, :block]


def local(observations, site_ids, counts, frequencies, decay, proc_var):
    modes = frequencies.shape[0]
    width = 2 * modes
    count = lax.axis_size("tm")
    steps = count * observations.shape[0]
    block = width // lax.axis_size("rows")
    height = block + 2 * TILE
    dense = (site_ids.shape[1] // LANES, LANES)
    table = -(-(2 * steps + 2) // modes) * modes
    vmem = pl.BlockSpec(memory_space=pltpu.VMEM)
    smem = pl.BlockSpec(memory_space=pltpu.SMEM)
    hbm = pl.BlockSpec(memory_space=pltpu.HBM)
    shared = pl.pallas_call(
        functools.partial(share_kernel, "tm"),
        out_shape=(
            jax.ShapeDtypeStruct((steps, 2 * TILE, modes), jnp.float32),
            jax.ShapeDtypeStruct((steps, 8, modes), jnp.float32),
            jax.ShapeDtypeStruct((steps, width, width), jnp.float32),
            jax.ShapeDtypeStruct((8, modes), jnp.float32),
        ),
        in_specs=[smem] + [hbm] * 5,
        out_specs=(vmem,) * 4,
        scratch_shapes=[
            pltpu.VMEM(dense, jnp.int32),
            pltpu.VMEM(dense, jnp.float32),
            pltpu.VMEM((1, modes), jnp.float32),
            pltpu.VMEM((1, modes), jnp.float32),
            pltpu.VMEM((1, modes), jnp.float32),
            pltpu.VMEM((steps, 2, modes, modes), jnp.float32),
            pltpu.VMEM((9, *dense), jnp.float32),
            pltpu.VMEM((2 * TILE, modes), jnp.float32),
            pltpu.VMEM((count, 2 * TILE, modes), jnp.float32),
            pltpu.SemaphoreType.DMA((5,)),
            pltpu.SemaphoreType.DMA((count,)),
            pltpu.SemaphoreType.DMA((count,)),
        ],
        compiler_params=pltpu.CompilerParams(collective_id=0, has_side_effects=True, vmem_limit_bytes=16 << 20),
        name="share",
    )(
        counts,
        *(
            pltpu.with_memory_space_constraint(value, pltpu.HBM)
            for value in (site_ids.reshape(dense), observations.reshape(dense), frequencies[None], decay[None], proc_var[None])
        ),
    )
    return pl.pallas_call(
        functools.partial(solve_kernel, "tm", "rows"),
        out_shape=(
            jax.ShapeDtypeStruct((1, block), jnp.float32),
            jax.ShapeDtypeStruct((1, block, width), jnp.float32),
        ),
        in_specs=[vmem] * 4,
        out_specs=(vmem, vmem),
        scratch_shapes=[
            pltpu.VMEM((table, modes), jnp.float32),
            pltpu.VMEM((table // modes, modes, modes), jnp.float32),
            pltpu.VMEM((steps, 8, width), jnp.float32),
            pltpu.VMEM((2, width, width), jnp.float32),
            pltpu.VMEM((steps - 1, width, width), jnp.float32),
            pltpu.VMEM((steps - 1, width, width), jnp.float32),
            pltpu.VMEM((height, width), jnp.float32),
            pltpu.VMEM((height, width), jnp.float32),
            pltpu.VMEM((2, width, width), jnp.float32),
        ],
        compiler_params=pltpu.CompilerParams(vmem_limit_bytes=40 << 20),
        name="solve",
    )(*shared)


def solution(mesh):
    return jax.shard_map(
        local,
        mesh=mesh,
        in_specs=(P("tm", None), P("tm", None), P("tm"), P(), P(), P()),
        out_specs=(P("tm", "rows"), P("tm", "rows", None)),
        check_vma=False,
    )
```

```python
import functools
import math

import jax
import jax.numpy as jnp
from jax import lax
from jax.experimental import pallas as pl
from jax.experimental.pallas import tpu as pltpu
from jax.sharding import PartitionSpec as P

GRID = 4096
OBS_VAR = 64
FINE = 16
TILE = 8
LANES = 128
CHAIN_BOUND = 2.5e-3
LAST_BOUND = 5e-3
TOLERANCE = 1e-6
HALF_UNIT = math.pi / GRID
HALF_SINE = tuple(-2.0 * c * HALF_UNIT ** (2 * k + 1) for k, c in enumerate((
    0.9999999766, -0.1666664763, 0.008332899823, -0.0001980089775, 2.590488469e-06
)))
HALF_COSINE = tuple(c * HALF_UNIT ** (2 * k) for k, c in enumerate((
    0.9999999535, -0.4999990535, 0.04166358469, -0.001385370429, 2.315393125e-05
)))

exact_mode = lax.Precision.HIGHEST


def exact(left, right):
    return jnp.dot(left, right, precision=exact_mode, preferred_element_type=jnp.float32)


dot = functools.partial(jnp.dot, preferred_element_type=jnp.float32)


def halves(value):
    high = value.astype(jnp.bfloat16)
    return high, (value - high.astype(jnp.float32)).astype(jnp.bfloat16)


def spread_by(value, picks):
    high, low = halves(value)
    picks = picks.astype(jnp.bfloat16)
    return dot(high, picks) + dot(low, picks)


def circle(angle):
    square = angle * angle
    cosine = 1.0 / 40320.0 - square * (1.0 / 3628800.0)
    cosine = 1.0 - square * (0.5 - square * (1.0 / 24.0 - square * (1.0 / 720.0 - square * cosine)))
    sine = 1.0 / 5040.0 - square * (1.0 / 362880.0)
    sine = angle * (1.0 - square * (1.0 / 6.0 - square * (1.0 / 120.0 - square * sine)))
    return cosine, sine


def quarter_turn(quadrant, cosine, sine):
    odd = (quadrant & 1) == 1
    new_cosine = jnp.where(odd, sine, cosine)
    new_sine = jnp.where(odd, cosine, sine)
    new_cosine = jnp.where(((quadrant + 1) & 2) == 2, -new_cosine, new_cosine)
    new_sine = jnp.where((quadrant & 2) == 2, -new_sine, new_sine)
    return new_cosine, new_sine


def share_kernel(
    tm_axis, counts_ref, site_hbm, obs_hbm, freq_hbm, decay_hbm, var_hbm,
    sums_ref, turn_ref, fresh_ref, mode_ref, site_ref, obs_ref, freq_ref, decay_ref, var_ref,
    tile_ref, factor_ref, mine, held, load_sem, send_sem, recv_sem,
):
    count = lax.axis_size(tm_axis)
    own = lax.axis_index(tm_axis)
    modes = freq_ref.shape[1]
    steps = sums_ref.shape[0]
    loads = [
        pltpu.make_async_copy(source, target, load_sem.at[number])
        for number, (source, target) in enumerate((
            (site_hbm, site_ref), (obs_hbm, obs_ref), (freq_hbm, freq_ref), (var_hbm, var_ref), (decay_hbm, decay_ref),
        ))
    ]
    for load in loads:
        load.start()
    barrier = pltpu.get_barrier_semaphore()
    for offset in range(1, count):
        pl.semaphore_signal(
            barrier, inc=1, device_id={tm_axis: lax.rem(own + offset, count)},
            device_id_type=pl.DeviceIdType.MESH,
        )
    for load in loads:
        load.wait()

    frequency = freq_ref[...]
    turns = jnp.where(jnp.abs(frequency) > 0.25 * math.pi, 1, 0) + jnp.where(
        jnp.abs(frequency) > 0.75 * math.pi, 1, 0
    )
    turns = jnp.where(frequency < 0.0, -turns, turns)
    share = turns.astype(jnp.float32)
    reduced = (frequency - share * 1.5703125) - share * (0.5 * math.pi - 1.5703125)
    turn_cosine, turn_sine = quarter_turn(turns + 4, *circle(reduced))
    level = 0.5 / (OBS_VAR * modes)
    root = math.sqrt(level)
    variance = var_ref[...]
    mode_ref[0:1, :] = jnp.exp(-decay_ref[...])
    now_cos = jnp.sqrt(variance)
    now_sin = jnp.zeros_like(now_cos)
    own_cos, own_sin = now_cos, now_sin
    for step in range(steps):
        for number, value in enumerate((now_cos * root, now_sin * root, now_cos, now_sin)):
            turn_ref[step, number : number + 1, :] = value
        own_cos = jnp.where(own == step, now_cos, own_cos)
        own_sin = jnp.where(own == step, now_sin, own_sin)
        now_cos, now_sin = (
            now_cos * turn_cosine - now_sin * turn_sine, now_cos * turn_sine + now_sin * turn_cosine
        )

    rows, lanes = site_ref.shape
    half_turn = GRID // 2
    place = lax.broadcasted_iota(jnp.int32, (TILE, lanes), 0)

    def wave(sites, exponent):
        at = ((exponent * sites) & (GRID - 1)).astype(jnp.float32) - half_turn
        square = at * at
        sine, cosine = HALF_SINE[-1], HALF_COSINE[-1]
        for a in HALF_SINE[-2::-1]:
            sine = sine * square + a
        for a in HALF_COSINE[-2::-1]:
            cosine = cosine * square + a
        sine = sine * at
        return (sine * sine) * 0.5 - 1.0, sine * cosine

    def turned(wave, by):
        return wave[0] * by[0] - wave[1] * by[1], wave[0] * by[1] + wave[1] * by[0]

    sites = site_ref[...]
    one = wave(sites, 1)
    two = turned(one, one)
    far = turned(wave(sites, FINE * TILE), two)
    slots = lax.broadcasted_iota(jnp.int32, (rows, lanes), 0) * lanes + lax.broadcasted_iota(jnp.int32, (rows, lanes), 1)
    live = jnp.where(slots < counts_ref[0], 1.0, 0.0)
    seen = live * obs_ref[...]
    factors = (live, *[v * live for v in two], *[v * live for v in far], *[v * seen for v in one], *wave(sites, TILE))
    for number, value in enumerate(factors):
        factor_ref[number] = value
    left, right = [], []
    for row in range(rows):
        spot = jnp.broadcast_to(site_ref[row : row + 1, :], (TILE, lanes))
        fine, coarse = wave(spot, place), wave(spot, place * FINE)
        live, *by = [jnp.broadcast_to(factor_ref[k, row : row + 1, :], (TILE, lanes)) for k in range(len(factors))]
        tiles = [(coarse[0] * live, coarse[1] * live)] + [turned(coarse, by[k : k + 2]) for k in (0, 2, 4)]
        upper = turned(fine, by[6:8])
        left.append(jnp.concatenate([tile[0] for tile in tiles] + [tile[1] for tile in tiles], axis=0))
        right.append(jnp.concatenate([fine[0], upper[0], fine[1], upper[1]], axis=0))
    left, right = jnp.concatenate(left, axis=1), jnp.concatenate(right, axis=1)
    left_high, left_low = halves(left)
    right_high, right_low = halves(right)
    beside = functools.partial(
        lax.dot_general,
        dimension_numbers=(((1,), (1,)), ((), ())),
        preferred_element_type=jnp.float32,
    )
    sums = beside(left_high, right_high) + (beside(left_high, right_low) + beside(left_low, right_high))
    tall = lax.broadcasted_iota(jnp.int32, (2 * FINE, 6 * modes), 0)
    wide = lax.broadcasted_iota(jnp.int32, (2 * FINE, 6 * modes), 1)
    picks = jnp.where(wide < 2 * modes, wide, jnp.where(wide < 4 * modes, 2 * wide, 6 * modes - wide)) & (FINE - 1)
    spread = spread_by(sums, jnp.where(tall == picks + (FINE * (wide // modes)) % (2 * FINE), 1.0, 0.0))
    half = left.shape[0] // 2
    pieces = [spread[:, number * modes : (number + 1) * modes] for number in range(6)]
    real, even_real, back_real = [pieces[number][:half] - pieces[number + 1][half:] for number in (0, 2, 4)]
    imaginary, even_imaginary, back_imaginary = [
        pieces[number][half:] + pieces[number + 1][:half] for number in (0, 2, 4)
    ]
    lane = lax.broadcasted_iota(jnp.int32, (TILE, modes), 1)
    group = lax.broadcasted_iota(jnp.int32, (TILE, modes), 0)
    keep = jnp.where(lane // FINE == group, 1.0, 0.0)
    keep_low = jnp.where(2 * lane // FINE == group, 1.0, 0.0)
    keep_back = jnp.where((modes - lane) // FINE == group, 1.0, 0.0)
    keep_high = jnp.where(2 * lane // FINE == group + TILE, 1.0, 0.0)

    def tile(value, number):
        return value[number * TILE : (number + 1) * TILE]

    def flat(value, number, keep=keep):
        return jnp.sum(tile(value, number) * keep, axis=0, keepdims=True)

    def even(value):
        return jnp.sum(tile(value, 1) * keep_low + tile(value, 2) * keep_high, axis=0, keepdims=True)

    info_scale = 1.0 / (OBS_VAR * math.sqrt(modes))
    turn_cos, turn_sin = own_cos * info_scale, own_sin * info_scale
    info_cos, info_sin = flat(real, 3), flat(imaginary, 3)
    near_cos = flat(real, 0)
    mass = (variance * level) * near_cos[:, 0:1]
    swing = (own_cos * own_cos - own_sin * own_sin) * level * even(even_real)
    swing = swing + (own_cos * own_sin) * (2.0 * level) * even(even_imaginary)
    rows = (
        near_cos, flat(imaginary, 0), flat(real, 1), flat(real, 2), flat(imaginary, 1), flat(imaginary, 2),
        turn_cos * info_cos + turn_sin * info_sin, turn_cos * info_sin - turn_sin * info_cos,
        mass + swing, mass - swing, flat(back_real, 0, keep_back), -flat(back_imaginary, 0, keep_back),
        jnp.zeros((4, modes), jnp.float32),
    )
    mine[...] = jnp.concatenate(rows, axis=0)

    pl.semaphore_wait(barrier, count - 1)
    copies = []
    for offset in range(1, count):
        copy = pltpu.make_async_remote_copy(
            src_ref=mine,
            dst_ref=held.at[offset],
            send_sem=send_sem.at[offset],
            recv_sem=recv_sem.at[offset],
            device_id={tm_axis: lax.rem(own + offset, count)},
            device_id_type=pl.DeviceIdType.MESH,
        )
        copy.start()
        copies.append(copy)
    for step in range(steps):
        for number in range(2):
            tile_ref[step, number] = jnp.broadcast_to(turn_ref[step, number : number + 1, :], (modes, modes)).T

    sub = group

    def build(at, message):
        bases = []
        for numbers in ((10, 0), (11, 1), (2, 3), (4, 5)):
            base = jnp.concatenate(
                [jnp.broadcast_to(message[number : number + 1, :], (TILE, modes)) for number in numbers], axis=1
            )
            if numbers[0] >= FINE // 2 + 2:
                base = pltpu.roll(base, 0, 1, stride=1, stride_axis=0)
                bases.append((base[:, :modes], base[:, modes:]))
            else:
                base = pltpu.roll(base, 2 * modes - TILE + 1, 1, stride=1, stride_axis=0)
                bases.append([
                    jnp.take_along_axis(base[:, k * modes : (k + 1) * modes], TILE - 1 - sub, axis=0) for k in range(2)
                ])
        cos_c, sin_c = [jnp.broadcast_to(turn_ref[at, k : k + 1, :], (TILE, modes)) for k in range(2)]
        for q in range(modes // TILE):
            shift = TILE * q
            spots = slice(shift, shift + TILE)

            def moved(low, high, edge, amount):
                value = jnp.where(lane >= edge, low, high) if edge else low
                return pltpu.roll(value, amount, 1) if amount % modes else value

            near_cos, near_sin = [
                moved(low, high, modes - shift, shift) if shift else high for low, high in bases[:2]
            ]
            far_cos, far_sin = [moved(low, high, shift, modes - shift) for low, high in bases[2:]]
            up_a, up_b = near_cos + far_cos, far_sin + near_sin
            low_a, low_b = far_sin - near_sin, near_cos - far_cos
            up_left, up_right = up_a * cos_c + up_b * sin_c, up_b * cos_c - up_a * sin_c
            low_left, low_right = low_a * cos_c + low_b * sin_c, low_b * cos_c - low_a * sin_c
            cos_t, sin_t = tile_ref[at, 0, spots, :], tile_ref[at, 1, spots, :]
            off = lane != sub + shift
            under = slice(modes + shift, modes + shift + TILE)
            fresh_ref[at, spots, :modes] = jnp.where(off, cos_t * up_left + sin_t * low_left, 0.0)
            fresh_ref[at, spots, modes:] = cos_t * up_right + sin_t * low_right
            fresh_ref[at, under, :modes] = cos_t * low_left - sin_t * up_left
            fresh_ref[at, under, modes:] = jnp.where(off, cos_t * low_right - sin_t * up_right, 0.0)

    def arrive(offset):
        pltpu.make_async_remote_copy(
            src_ref=mine,
            dst_ref=held.at[offset],
            send_sem=send_sem.at[offset],
            recv_sem=recv_sem.at[offset],
            device_id={tm_axis: lax.rem(own + offset, count)},
            device_id_type=pl.DeviceIdType.MESH,
        ).wait_recv()

    def take(offsets):
        for offset in offsets:
            arrive(offset)
        for offset in offsets:
            peer = lax.rem(own + count - offset, count)
            message = held[offset]
            sums_ref[peer] = message
            build(peer, message)

    paired = count - 1 - (count - 1) % 2

    def take_two(number, carry):
        take((paired - 2 * number, paired - 1 - 2 * number))
        return carry

    message = mine[...]
    sums_ref[own] = message
    build(own, message)
    if (count - 1) % 2:
        take((count - 1,))
    lax.fori_loop(0, (count - 1) // 2, take_two, 0)
    for copy in copies:
        copy.wait_send()


def solve_kernel(
    tm_axis, rows_axis, sums_ref, turn_ref, fresh, mode_ref, mean_ref, cov_ref,
    tab, cols, line, kept, main, full, answer, spare, result,
):
    steps = sums_ref.shape[0]
    modes = sums_ref.shape[2]
    width = 2 * modes
    block = cov_ref.shape[1]
    own = lax.axis_index(tm_axis)
    block_row = lax.axis_index(rows_axis)
    links = steps - 1
    sides = (slice(0, modes), slice(modes, width))
    damp = mode_ref[0:1, :]
    damp_sq = damp * damp
    lane = lax.broadcasted_iota(jnp.int32, (TILE, modes), 1)
    sub = lax.broadcasted_iota(jnp.int32, (TILE, modes), 0)
    before = jnp.maximum(own - 1, 0)
    inverse_row, flow_row, right_row, info_row, left_row, other_row = range(6)

    def node(i):
        return own if i == links else jnp.where(own > i, i, links - (i - own))

    def load(ref, index, row):
        return tuple(ref[index, row : row + 1, side] for side in sides)

    def weights_of(at):
        return tuple(sums_ref[at, row : row + 1, :] for row in (8, 9))

    def info_of(at):
        return tuple(sums_ref[at, row : row + 1, :] for row in (6, 7))

    def note(i, row, values):
        for side, value in zip(sides, values):
            line[i, row : row + 1, side] = value

    past = None
    for i in range(links):
        at = node(i)
        inner = jnp.where(jnp.logical_or(at == 0, at == links), 0.0, 1.0)
        keep = jnp.where(own == i, 0.0, 1.0) if i else 0.0
        level = [1.0 + inner * damp_sq + mass for mass in weights_of(at)]
        if i:
            level = [value - (keep * damp_sq) * old for value, old in zip(level, past)]
        inverse = [1.0 / value for value in level]
        note(i, inverse_row, inverse)
        note(i, right_row, [(keep * damp) * value for value in inverse])
        note(i, info_row, info_of(at))
        note(i, other_row, [(keep * damp) * old for old in past] if i else [jnp.zeros_like(damp)] * 2)
        for half, value in enumerate(inverse):
            tab[2 * i + half : 2 * i + half + 1, :] = damp * value
        past = inverse
    has_left, has_right = jnp.where(own > 0, 1.0, 0.0), jnp.where(own < links, 1.0, 0.0)
    left, right = load(line, before, inverse_row), past
    level = [
        1.0 + (has_left * has_right) * damp_sq + mass - (has_left * damp_sq) * a - (has_right * damp_sq) * b
        for mass, a, b in zip(weights_of(own), left, right)
    ]
    inverse = [1.0 / value for value in level]
    note(links, inverse_row, inverse)
    note(links, right_row, [damp * value for value in inverse])
    note(links, info_row, info_of(own))
    left, right = [(has_left * damp) * value for value in left], [(has_right * damp) * value for value in right]
    note(links, left_row, left)
    note(links, other_row, right)
    for half in range(2):
        tab[2 * links + half : 2 * links + half + 1, :] = left[half]
        tab[2 * steps + half : 2 * steps + half + 1, :] = right[half]
    for chunk in range(tab.shape[0] // modes):
        cols[chunk] = tab[chunk * modes : (chunk + 1) * modes, :].T

    def col_of(at, rows):
        value = cols[at // modes, rows, at % modes : at % modes + 1]
        return jnp.broadcast_to(value, (rows.stop - rows.start, modes))

    pair = 2 * TILE
    strips = [
        (half, slice(start, start + pair), slice(half * modes + start, half * modes + start + pair))
        for half in range(2) for start in range(0, modes, pair)
    ]
    pair_lane = lax.broadcasted_iota(jnp.int32, (pair, modes), 1)
    pair_sub = lax.broadcasted_iota(jnp.int32, (pair, modes), 0)
    ones = jnp.ones((TILE, width), jnp.bfloat16)

    def flow(i, state, third):
        sums = [jnp.zeros((pair, modes), jnp.float32) for _ in sides]
        for half, part, rows in strips:
            parts = []
            for k, side in enumerate(sides):
                value = main[i, rows, side] + third[rows, side]
                full[i, rows, side] = value
                parts.append(value * state[k])
            column = jnp.sum(parts[0] + parts[1], axis=1, keepdims=True)
            sums[half] += jnp.where(pair_lane == pair_sub + part.start, column, 0.0)
        moved = [value - jnp.sum(total, axis=0, keepdims=True) for value, total in zip(state, sums)]
        note(i, flow_row, moved)
        return moved

    def packed(whole):
        return jnp.concatenate([jnp.concatenate(values, axis=1) for values in whole], axis=0).astype(jnp.bfloat16)

    third, state, most = None, None, jnp.zeros((TILE, width), jnp.float32)
    for i in range(links):
        scales, rights = load(line, i, inverse_row), load(line, i, right_row)
        downs = [col_of(2 * (i - 1) + half, part) for half, part, rows in strips] if i else [None] * len(strips)
        whole = []
        for (half, part, rows), down in zip(strips, downs):
            values = []
            for side, scale, right in zip(sides, scales, rights):
                value = fresh[node(i), rows, side] * scale
                if i:
                    value = value + down * (main[i - 1, rows, side] * right)
                kept[i % 2, rows, side] = value
                values.append(value)
            whole.append(values)
        narrow = packed(whole)
        square = dot(narrow, narrow)
        if i:
            moved = flow(i - 1, state, third)
            state = [a + b * c for a, b, c in zip(load(line, i, info_row), load(line, i, other_row), moved)]
        else:
            state = load(line, i, info_row)
        for (half, part, rows), down in zip(strips, downs):
            for side, right in zip(sides, rights):
                value = kept[i % 2, rows, side] - square[rows, side]
                if i:
                    value = value + down * (third[rows, side] * right)
                main[i, rows, side] = value
        squared = square.astype(jnp.bfloat16)
        third = dot(squared, narrow)
        most = jnp.maximum(most, dot(ones, jnp.abs(squared)))
    flow(links - 1, state, third)

    height = block + pair
    tall = lax.broadcasted_iota(jnp.int32, (block, modes), 0)
    wide = lax.broadcasted_iota(jnp.int32, (block, modes), 1)
    hit = wide == (tall + block_row * block) // 2
    even = tall % 2 == 0
    cosines, sines = turn_ref[own, 2:3, :], turn_ref[own, 3:4, :]

    def pose():
        state = [
            a + b * c + d * e
            for a, b, c, d, e in zip(
                load(line, links, info_row), load(line, links, left_row), load(line, before, flow_row),
                load(line, links, other_row), load(line, links - 1, flow_row),
            )
        ]
        scales = load(line, links, inverse_row)
        spare[:block, sides[0]] = jnp.where(hit, jnp.where(even, cosines, sines) * scales[0], 0.0)
        spare[:block, sides[1]] = jnp.where(hit, jnp.where(even, -sines, cosines) * scales[1], 0.0)
        for side, value, scale in zip(sides, state, scales):
            spare[block:, side] = jnp.where(pair_sub == 0, value * scale, 0.0)

    def product(left, right):
        return dot(left[0], right[0]) + (dot(left[0], right[1]) + dot(left[1], right[0]))

    whole = []
    scales, rights = load(line, links, inverse_row), load(line, links, right_row)
    for half, part, rows in strips:
        first, second = col_of(2 * links + half, part), col_of(2 * steps + half, part)
        whole.append([
            fresh[own, rows, side] * scale + (first * full[before, rows, side] + second * full[links - 1, rows, side]) * right
            for side, scale, right in zip(sides, scales, rights)
        ])
    whole = halves(jnp.concatenate([jnp.concatenate(values, axis=1) for values in whole], axis=0))
    pose()
    asked = spare[...]
    first = product(halves(asked), whole)
    square = dot(whole[0], whole[0]).astype(jnp.bfloat16)
    second = product(halves(first), whole)
    fourth = dot(square, square).astype(jnp.bfloat16)
    third = dot(second.astype(jnp.bfloat16), whole[0])
    last = dot(ones, jnp.abs(fourth))
    reached = (asked - first) + (second - third)
    answer[...] = reached + dot(reached.astype(jnp.bfloat16), fourth)
    good = jnp.logical_and(jnp.max(most) <= CHAIN_BOUND, jnp.max(last) <= LAST_BOUND)

    @pl.when(jnp.logical_not(good))
    def _():
        rows = lax.broadcasted_iota(jnp.int32, (width, width), 0)
        unit = rows == lax.broadcasted_iota(jnp.int32, (width, width), 1)
        source, target = result.at[0], result.at[1]

        def column(row):
            return jnp.sum(jnp.where(unit, row, 0.0), axis=1, keepdims=True)

        def invert(low):
            high = 1.001 * jnp.max(jnp.sum(jnp.abs(source[...]), axis=0, keepdims=True))
            low = jnp.minimum(low, 0.5 * high)
            center = (high + low) / (high - low)
            slope = 2.0 / (high - low)
            top = 2.0 * center * center - 1.0
            target[...] = jnp.where(unit, 4.0 * center * slope / top, 0.0) - (2.0 * slope * slope / top) * source[...]

            def improve(radius):
                factor = 2.0 / (2.0 - radius * radius)
                residue = jnp.where(unit, 1.0, 0.0) - exact(source[...], target[...])
                target[...] = factor * (target[...] + exact(target[...], residue))
                return radius * radius / (2.0 - radius * radius)

            lax.while_loop(lambda radius: radius > TOLERANCE, improve, 1.0 / top)

        def even_out(i, whole):
            root = jnp.sqrt(line[i, inverse_row : inverse_row + 1, :])
            source[...] = jnp.where(unit, 1.0, 0.0) + column(root) * whole * (1.0 / root)
            return root, column(root)

        full[0] = jnp.zeros((width, width), jnp.float32)
        note(0, flow_row, [jnp.zeros_like(damp)] * 2)

        def advance(i, carry):
            old = jnp.maximum(i - 1, 0)
            down = column(line[old, inverse_row : inverse_row + 1, :] * jnp.concatenate([damp, damp], axis=1))
            at = jnp.where(own > i, i, links - (i - own))
            plain = fresh[at] * line[i, inverse_row : inverse_row + 1, :]
            root, root_col = even_out(i, plain + down * full[old] * line[i, right_row : right_row + 1, :])
            invert(0.999 * jnp.min(root * root))
            state = line[i, info_row : info_row + 1, :]
            state = state + line[i, other_row : other_row + 1, :] * line[old, flow_row : flow_row + 1, :]
            scaled = jnp.broadcast_to(state * root, (TILE, width))
            line[i, flow_row : flow_row + 1, :] = exact(scaled, target[...])[0:1] * (1.0 / root)
            full[i] = (1.0 / root_col) * (jnp.where(unit, 1.0, 0.0) - target[...]) * root
            return carry

        lax.fori_loop(0, links, advance, 0)
        root, root_col = even_out(
            links,
            fresh[own] * line[links, inverse_row : inverse_row + 1, :] + (
                column(line[links, left_row : left_row + 1, :]) * full[before]
                + column(line[links, other_row : other_row + 1, :]) * full[links - 1]
            ) * line[links, right_row : right_row + 1, :],
        )
        invert(0.999 * jnp.min(1.0 - damp_sq) * jnp.min(root * root))
        pose()
        answer[...] = exact(spare[...] * (1.0 / root), target[...]) * root

    left, right = answer[:, sides[0]], answer[:, sides[1]]
    left, right = left * cosines - right * sines, left * sines + right * cosines
    wide = lax.broadcasted_iota(jnp.int32, (height, modes), 1)
    out = []
    for number in range(2):
        pick = wide // 2 + number * (modes // 2)
        out.append(
            jnp.where(wide % 2 == 0, jnp.take_along_axis(left, pick, axis=1), jnp.take_along_axis(right, pick, axis=1))
        )
    for side, value in zip(sides, out):
        cov_ref[0, :, side] = value[:block]
    means = jnp.concatenate([value[block : block + TILE] for value in out], axis=1)
    mean_ref[...] = pltpu.roll(means, width - block_row * block, 1)[0:1, :block]


def local(observations, site_ids, counts, frequencies, decay, proc_var):
    modes = frequencies.shape[0]
    width = 2 * modes
    count = lax.axis_size("tm")
    steps = count * observations.shape[0]
    block = width // lax.axis_size("rows")
    height = block + 2 * TILE
    dense = (site_ids.shape[1] // LANES, LANES)
    table = -(-(2 * steps + 2) // modes) * modes
    vmem = pl.BlockSpec(memory_space=pltpu.VMEM)
    smem = pl.BlockSpec(memory_space=pltpu.SMEM)
    hbm = pl.BlockSpec(memory_space=pltpu.HBM)
    shared = pl.pallas_call(
        functools.partial(share_kernel, "tm"),
        out_shape=(
            jax.ShapeDtypeStruct((steps, 2 * TILE, modes), jnp.float32),
            jax.ShapeDtypeStruct((steps, 8, modes), jnp.float32),
            jax.ShapeDtypeStruct((steps, width, width), jnp.float32),
            jax.ShapeDtypeStruct((8, modes), jnp.float32),
        ),
        in_specs=[smem] + [hbm] * 5,
        out_specs=(vmem,) * 4,
        scratch_shapes=[
            pltpu.VMEM(dense, jnp.int32),
            pltpu.VMEM(dense, jnp.float32),
            pltpu.VMEM((1, modes), jnp.float32),
            pltpu.VMEM((1, modes), jnp.float32),
            pltpu.VMEM((1, modes), jnp.float32),
            pltpu.VMEM((steps, 2, modes, modes), jnp.float32),
            pltpu.VMEM((9, *dense), jnp.float32),
            pltpu.VMEM((2 * TILE, modes), jnp.float32),
            pltpu.VMEM((count, 2 * TILE, modes), jnp.float32),
            pltpu.SemaphoreType.DMA((5,)),
            pltpu.SemaphoreType.DMA((count,)),
            pltpu.SemaphoreType.DMA((count,)),
        ],
        compiler_params=pltpu.CompilerParams(collective_id=0, has_side_effects=True, vmem_limit_bytes=16 << 20),
        name="share",
    )(
        counts,
        *(
            pltpu.with_memory_space_constraint(value, pltpu.HBM)
            for value in (site_ids.reshape(dense), observations.reshape(dense), frequencies[None], decay[None], proc_var[None])
        ),
    )
    return pl.pallas_call(
        functools.partial(solve_kernel, "tm", "rows"),
        out_shape=(
            jax.ShapeDtypeStruct((1, block), jnp.float32),
            jax.ShapeDtypeStruct((1, block, width), jnp.float32),
        ),
        in_specs=[vmem] * 4,
        out_specs=(vmem, vmem),
        scratch_shapes=[
            pltpu.VMEM((table, modes), jnp.float32),
            pltpu.VMEM((table // modes, modes, modes), jnp.float32),
            pltpu.VMEM((steps, 8, width), jnp.float32),
            pltpu.VMEM((2, width, width), jnp.float32),
            pltpu.VMEM((steps - 1, width, width), jnp.float32),
            pltpu.VMEM((steps - 1, width, width), jnp.float32),
            pltpu.VMEM((height, width), jnp.float32),
            pltpu.VMEM((height, width), jnp.float32),
            pltpu.VMEM((2, width, width), jnp.float32),
        ],
        compiler_params=pltpu.CompilerParams(vmem_limit_bytes=40 << 20),
        name="solve",
    )(*shared)


def solution(mesh):
    return jax.shard_map(
        local,
        mesh=mesh,
        in_specs=(P("tm", None), P("tm", None), P("tm"), P(), P(), P()),
        out_specs=(P("tm", "rows"), P("tm", "rows", None)),
        check_vma=False,
    )
```
